128 devices in a mesh: dp: 16 (over y, z), mp: 8 (over x, core).
Axes of the slice: x: 4, y: 4, z: 4, core: 2. Of those that a mesh axis runs over, the one named last changes fastest.
Arguments:
- hidden_in: bfloat16 [4096, 2304], P('dp'), may hold values from -6 to 6
- attn_gain: float32 [2304], replicated, may hold values from 0.25 to 1.75
- w_query: bfloat16 [2304, 2048], P(None, 'mp'), may hold values from -0.25 to 0.25
- w_key: bfloat16 [2304, 2048], P(None, 'mp'), may hold values from -0.125 to 0.125
- w_value: bfloat16 [2304, 2048], P(None, 'mp'), may hold values from -0.125 to 0.125
- w_out: bfloat16 [2048, 2304], P('mp'), may hold values from -0.5 to 0.5
- root_cache: bfloat16 [2, 4096, 2048], P(None, 'dp', 'mp'), may hold values from -400 to 400
- mid_cache: bfloat16 [2, 16, 1024, 2048], P(None, 'dp', None, 'mp'), may hold values from -400 to 400
- leaf_cache: bfloat16 [2, 32, 1024, 2048], P(None, 'dp', None, 'mp'), may hold values from -400 to 400
- mid_len: int32 [16], P('dp'), may hold values from 1 to 1024, 8192 in all
- leaf_len: int32 [32], P('dp'), may hold values from 1 to 1024, 16384 in all
- leaf_of: int32 [128], P('dp'), may hold values from 0 to 31, as said below
- parents: int32 [32], replicated, may hold values from 0 to 15, as said below
- suffix_len: int32 [128], P('dp'), may hold values from 1 to 32, 3072 in all
- ffn_gain: float32 [2304], replicated, may hold values from 0.25 to 1.75
- w_router: float32 [2304, 8], replicated, may hold values from -0.5 to 0.5
- routes: int32 [4096, 2], P('dp'), may hold values from 0 to 7, all different within a row; in each aligned block of 256 rows (0 to 255, 256 to 511, ...) at most 96 rows name the same one
- w_gate: bfloat16 [8, 2304, 5760], P('mp', None, 'dp'), may hold values from -0.125 to 0.125
- w_up: bfloat16 [8, 2304, 5760], P('mp', None, 'dp'), may hold values from -0.125 to 0.125
- w_down: bfloat16 [8, 5760, 2304], P('mp', 'dp'), may hold values from -0.078125 to 0.078125
Outputs:
- layer_out: bfloat16 [4096, 2304], P(('dp', 'mp'))
The draws below stay inside these ranges and needn't reach their ends.
Inputs may be any that keep to these rules, and one draw needn't show every extreme that they name: `leaf_of`: leaf n belongs to index n // 2 of dp, mid-level node n to index n. The 8 sequences of one index of dp have different mid-level nodes and leaves of one parity, so that no two of them share a mid-level node or a leaf's owner. `parents`: every mid-level node is the parent of exactly one even and one odd leaf. `routes`: in the rows of one index of dp no expert is named by more than 96 rows; some indices of dp reach 96.
All inputs are finite; a program needn't handle non-finite values. No bound on the sum of `mid_len` or of `leaf_len` or of `suffix_len` on one device may be relied on, other than what follows from the above.
Results may differ from the reference program's by a relative error of at most 0.015.
The reference program's roundings to bfloat16 on the way (of `normed`, `probs`, `attended`, `ffn_in` and `act`) count: a program that leaves them out, or rounds other values in their place, can miss the bound.
Values may be sent and summed in bfloat16 or wider, within the bound.
A program may use at most 128 MiB of HBM per device.

```python
import math
import jax
import jax.numpy as jnp
import numpy as np
from jax import lax

D = 2304
HEADS = 32
HD = 64
FF = 5760
TOP = 2
SEQ_ROW = 8
SUF = 32
PL = 1024
EXPERTS = 8
NODES = 16
LEAVES = 32
ROOT_LEN = 4096
TOK_ROW = 256
SEQS = 128
TOKENS = 4096
CAPR = 96
N_DP = 16


def tree_tables(key):
    base = jax.random.fold_in(key, 4242)
    first_key, second_key, pick_key, side_key = jax.random.split(base, 4)
    first_order = jax.random.permutation(first_key, NODES).astype(jnp.int32)
    second_order = jax.random.permutation(second_key, NODES).astype(jnp.int32)
    middle = jnp.arange(NODES, dtype=jnp.int32)
    parents = jnp.zeros((LEAVES,), jnp.int32)
    parents = parents.at[2 * first_order].set(middle)
    parents = parents.at[2 * second_order + 1].set(middle)
    owner_keys = jax.random.split(pick_key, NODES)
    chosen = jax.vmap(lambda single: jax.random.permutation(single, NODES)[:SEQ_ROW])(owner_keys).astype(jnp.int32)
    sides = jax.random.randint(side_key, (NODES, 1), 0, 2)
    leaves = jnp.where(sides == 1, 2 * second_order[chosen] + 1, 2 * first_order[chosen])
    return (parents, leaves.reshape(SEQS).astype(jnp.int32))


def cache_values(key, shape):
    normal_key = jax.random.fold_in(jax.random.fold_in(key, 17), 0)
    base = jnp.clip(jax.random.normal(normal_key, shape, jnp.float32), -6.0, 6.0)
    return base.astype(jnp.bfloat16)


def draw_root_cache(key, part):
    return cache_values(key, (2, ROOT_LEN, HEADS * HD))


def draw_mid_cache(key, part):
    return cache_values(key, (2, NODES, PL, HEADS * HD))


def draw_leaf_cache(key, part):
    return cache_values(key, (2, LEAVES, PL, HEADS * HD))


def draw_leaf_of(key, part):
    return tree_tables(key)[1]


def draw_parents(key, part):
    return tree_tables(key)[0]


def shard_levels(rng, extent, cuts, smallest, high):
    level = 1.0
    for position, parts in cuts:
        steps = jax.random.uniform(jax.random.fold_in(jax.random.fold_in(rng, 6), position), (parts,), jnp.float32, smallest / len(cuts), high / len(cuts))
        level = level * jnp.repeat(jnp.exp(steps), extent[position] // parts).reshape((-1,) + (1,) * (len(extent) - 1 - position))
    return level


def profile(count, total, bound, slope):
    weights = [(1 << 20) // math.isqrt(grade ** slope) + 1 for grade in range(2, count + 1)]
    surplus, holding = total - bound - (count - 1), [1] * (count - 1)
    while surplus > 0:
        candidates = [i for i in range(count - 1) if holding[i] < bound]
        whole, budget = sum([weights[i] for i in candidates]), surplus
        for i in candidates:
            more = min(bound - holding[i], max(1, budget * weights[i] // whole), surplus)
            holding[i] = holding[i] + more
            surplus = surplus - more
    return np.array([bound] + holding)


def uneven(rng, count, total, bound, lean):
    if count == 2:
        one = jax.random.randint(rng, (), max(1, total - bound), min(bound, total - 1) + 1)
        return jnp.stack([one, total - one])
    lengths = jnp.asarray(profile(count, total, bound, lean), jnp.int32)
    couples = (count - 1) // 2
    giver, receiver = lengths[1:1 + 2 * couples:2], lengths[2:2 + 2 * couples:2]
    room = jnp.minimum(giver - 1, bound - receiver)
    shifted = jax.random.randint(jax.random.fold_in(rng, 1), (couples,), 0, 1 << 20) % (room + 1)
    lengths = lengths.at[1:1 + 2 * couples:2].set(giver - shifted).at[2:2 + 2 * couples:2].set(receiver + shifted)
    return lengths[jax.random.permutation(jax.random.fold_in(rng, 2), count)]


def routed_block(own_key, own, number, rows, number_of, top, most, skew):
    sequence = jax.random.permutation(own_key, number_of)
    crowded, usual = shares(number_of, rows * top, most, skew, True), shares(number_of, rows * top, most, skew, False)
    places = jnp.arange(number_of)

    def named(lengths, offset_by):
        used = int((lengths > 0).sum())
        fixed = max(1, used // 4)
        passed = fixed + (places - fixed + offset_by * (used - fixed)) % max(1, number_of - fixed)
        return jnp.zeros((number_of,), jnp.int32).at[sequence[jnp.where(places < fixed, places, passed)]].set(jnp.asarray(lengths, jnp.int32))

    lengths = jnp.where(number % 4 == 0, named(crowded, number // 4), named(usual, number - number // 4 - 1))
    mixed = jax.random.permutation(jax.random.fold_in(own, 3), number_of)
    giver, taker = mixed[0:number_of // 2 * 2:2], mixed[1:number_of // 2 * 2:2]
    slack = jnp.minimum(lengths[giver] - 1, most - lengths[taker]) // 2
    slack = jnp.where((giver == sequence[0]) | (taker == sequence[0]) | (lengths[taker] == 0), 0, jnp.maximum(slack, 0))
    passed = jax.random.randint(jax.random.fold_in(own, 4), (number_of // 2,), 0, 1 << 20) % (slack + 1)
    lengths = lengths.at[giver].add(-passed).at[taker].add(passed)
    members = jnp.searchsorted(jnp.cumsum(lengths), jnp.arange(rows * top), side="right").astype(jnp.int32)
    table = members.reshape(top, rows).T
    table = table[jax.random.permutation(jax.random.fold_in(own, 1), rows)]
    offset_by = jax.random.randint(jax.random.fold_in(own, 2), (rows, 1), 0, top)
    return jnp.take_along_axis(table, (jnp.arange(top)[None, :] + offset_by) % top, axis=1)


def shares(count, total, most, lean, full):
    loads = [(1 << 20) // math.isqrt(standing ** lean) + 1 for standing in range(1, count + 1)]
    largest = most if full else min(most, max(-(-total // count), total * loads[0] // sum(loads)))
    least = 1 if total - largest >= count - 1 else 0
    counts, rest = [largest] + [least] * (count - 1), total - largest - least * (count - 1)
    while rest > 0:
        movable = [i for i in range(1, count) if counts[i] < largest] or [i for i in range(1, count) if counts[i] < most]
        whole, budget = sum([loads[i] for i in movable]), rest
        for i in movable:
            extra = min(most - counts[i], max(1, budget * loads[i] // whole), rest)
            counts[i] = counts[i] + extra
            rest = rest - extra
    return np.array(counts)


def gaussian(own_key, extent, width, reach, cuts=(), kind=jnp.bfloat16):
    drawn = width * jax.random.normal(own_key, extent, jnp.float32)
    if cuts:
        drawn = drawn * shard_levels(own_key, extent, cuts, -0.22, 0.18)
    return jnp.clip(drawn, -reach, reach).astype(kind)


def setup_inputs(seed: int = 0) -> dict:
    streams_of = jax.random.split(jax.random.key(seed), 21)
    hidden_in = gaussian(streams_of[0], (TOKENS, D), 1.0, 6.0, ((0, 16),))
    attn_gain = jnp.clip(1.0 + 0.15 * jax.random.normal(streams_of[1], (D,), jnp.float32), 0.25, 1.75)
    w_query = gaussian(streams_of[2], (D, HEADS * HD), (D // 4) ** -0.5, 0.25, ((1, 8),))
    w_key = gaussian(streams_of[3], (D, HEADS * HD), D ** -0.5, 0.125, ((1, 8),))
    w_value = gaussian(streams_of[4], (D, HEADS * HD), D ** -0.5, 0.125, ((1, 8),))
    w_out = gaussian(streams_of[5], (HEADS * HD, D), (HEADS * HD // 16) ** -0.5, 0.5, ((0, 8),))
    root_cache = draw_root_cache(jax.random.fold_in(streams_of[20], 71), 0)
    mid_cache = draw_mid_cache(jax.random.fold_in(streams_of[20], 71), 0)
    leaf_cache = draw_leaf_cache(jax.random.fold_in(streams_of[20], 71), 0)
    mid_len = uneven(streams_of[9], NODES, NODES * PL // 2, PL, 2).astype(jnp.int32)
    leaf_len = uneven(streams_of[10], LEAVES, LEAVES * PL // 2, PL, 2).astype(jnp.int32)
    leaf_of = draw_leaf_of(jax.random.fold_in(streams_of[20], 71), 0)
    parents = draw_parents(jax.random.fold_in(streams_of[20], 71), 0)
    suffix_len = uneven(streams_of[13], SEQS, SEQS * SUF * 3 // 4, SUF, 1).astype(jnp.int32)
    ffn_gain = jnp.clip(1.0 + 0.15 * jax.random.normal(streams_of[14], (D,), jnp.float32), 0.25, 1.75)
    w_router = gaussian(streams_of[15], (D, EXPERTS), 0.08, 0.5, (), jnp.float32)
    routes_keys = jax.random.split(jax.random.fold_in(streams_of[16], 1), TOKENS // TOK_ROW)
    routes_turns = jax.random.permutation(jax.random.fold_in(streams_of[16], 3), TOKENS // TOK_ROW)
    routes = jax.vmap(lambda own, number: routed_block(jax.random.fold_in(streams_of[16], 2), own, number, TOK_ROW, EXPERTS, TOP, CAPR, 2))(routes_keys, routes_turns).reshape((TOKENS, TOP))
    w_gate = gaussian(streams_of[17], (EXPERTS, D, FF), D ** -0.5, 0.125, ((0, 8), (2, 16)))
    w_up = gaussian(streams_of[18], (EXPERTS, D, FF), D ** -0.5, 0.125, ((0, 8), (2, 16)))
    w_down = gaussian(streams_of[19], (EXPERTS, FF, D), FF ** -0.5, 0.078125, ((0, 8), (1, 16)))
    return {"hidden_in": hidden_in, "attn_gain": attn_gain, "w_query": w_query, "w_key": w_key, "w_value": w_value, "w_out": w_out, "root_cache": root_cache, "mid_cache": mid_cache, "leaf_cache": leaf_cache, "mid_len": mid_len, "leaf_len": leaf_len, "leaf_of": leaf_of, "parents": parents, "suffix_len": suffix_len, "ffn_gain": ffn_gain, "w_router": w_router, "routes": routes, "w_gate": w_gate, "w_up": w_up, "w_down": w_down}


EPS = 1e-05
NEGATIVE = -1e+30

def rms_scale(rows, gain):
    rows_wide = rows.astype(jnp.float32)
    mean_square = lax.optimization_barrier(jnp.mean(rows_wide * rows_wide, axis=-1, keepdims=True))
    return rows_wide * lax.rsqrt(mean_square + EPS) * gain

def reference(hidden_in, attn_gain, w_query, w_key, w_value, w_out, root_cache, mid_cache, leaf_cache, mid_len, leaf_len, leaf_of, parents, suffix_len, ffn_gain, w_router, routes, w_gate, w_up, w_down):
    scale = 1.0 / HD ** 0.5
    normed = rms_scale(hidden_in, attn_gain).astype(jnp.bfloat16)
    query = jnp.dot(normed, w_query, preferred_element_type=jnp.float32).astype(jnp.bfloat16)
    key = jnp.dot(normed, w_key, preferred_element_type=jnp.float32).astype(jnp.bfloat16)
    value = jnp.dot(normed, w_value, preferred_element_type=jnp.float32).astype(jnp.bfloat16)
    query_seq = query.reshape(SEQS, SUF, HEADS, HD)
    key_seq = key.reshape(SEQS, SUF, HEADS, HD)
    value_seq = value.reshape(SEQS, SUF, HEADS, HD)
    mid_of = parents[leaf_of]
    root_keys = root_cache[0].reshape(ROOT_LEN, HEADS, HD)
    root_values = root_cache[1].reshape(ROOT_LEN, HEADS, HD)
    node_slots = jnp.arange(PL, dtype=jnp.int32)
    suffix_slots = jnp.arange(SUF, dtype=jnp.int32)

    def one_sequence(index):
        leaf = leaf_of[index]
        middle = mid_of[index]
        keys_all = jnp.concatenate([root_keys, mid_cache[0, middle].reshape(PL, HEADS, HD), leaf_cache[0, leaf].reshape(PL, HEADS, HD), key_seq[index]], axis=0)
        values_all = jnp.concatenate([root_values, mid_cache[1, middle].reshape(PL, HEADS, HD), leaf_cache[1, leaf].reshape(PL, HEADS, HD), value_seq[index]], axis=0)
        root_ok = jnp.ones((SUF, ROOT_LEN), dtype=bool)
        mid_ok = jnp.broadcast_to(node_slots[None, :] < mid_len[middle], (SUF, PL))
        leaf_ok = jnp.broadcast_to(node_slots[None, :] < leaf_len[leaf], (SUF, PL))
        self_ok = (suffix_slots[None, :] <= suffix_slots[:, None]) & (suffix_slots[None, :] < suffix_len[index])
        allowed = jnp.concatenate([root_ok, mid_ok, leaf_ok, self_ok], axis=1)
        scores = jnp.einsum('qhd,khd->qhk', query_seq[index].astype(jnp.float32), keys_all.astype(jnp.float32)) * scale
        scores = jnp.where(allowed[:, None, :], scores, NEGATIVE)
        peak = lax.optimization_barrier(jnp.max(scores, axis=-1, keepdims=True))
        weights = jnp.exp(scores - peak)
        total = lax.optimization_barrier(jnp.sum(weights, axis=-1))
        probs = weights.astype(jnp.bfloat16)
        summed = jnp.einsum('qhk,khd->qhd', probs.astype(jnp.float32), values_all.astype(jnp.float32))
        return (summed / total[..., None]).reshape(SUF, HEADS * HD)
    attended = lax.map(one_sequence, jnp.arange(SEQS, dtype=jnp.int32)).reshape(TOKENS, HEADS * HD).astype(jnp.bfloat16)
    attn_proj = jnp.dot(attended, w_out, preferred_element_type=jnp.float32)
    resid = hidden_in.astype(jnp.float32) + attn_proj
    ffn_in = rms_scale(resid, ffn_gain).astype(jnp.bfloat16)
    logits = jnp.dot(ffn_in.astype(jnp.float32), w_router, precision=lax.Precision.HIGHEST)
    chosen = jnp.take_along_axis(logits, routes, axis=1)
    squashed = jax.nn.sigmoid(chosen)
    gates = squashed / lax.optimization_barrier(jnp.sum(squashed, axis=1, keepdims=True))
    limit = CAPR * N_DP

    def per_expert(mixed, expert):
        hit_each = routes == expert
        hit = jnp.any(hit_each, axis=1)
        weight = lax.optimization_barrier(jnp.sum(jnp.where(hit_each, gates, 0.0), axis=1))
        order_key = jnp.where(hit, 0, 1).astype(jnp.int32)
        picked = jnp.argsort(order_key, stable=True)[:limit].astype(jnp.int32)
        rows = ffn_in[picked]
        gate_part = jnp.dot(rows, w_gate[expert], preferred_element_type=jnp.float32)
        up_part = jnp.dot(rows, w_up[expert], preferred_element_type=jnp.float32)
        act = (jax.nn.silu(gate_part) * up_part).astype(jnp.bfloat16)
        expert_out = jnp.dot(act, w_down[expert], preferred_element_type=jnp.float32)
        return (mixed.at[picked].add(expert_out * weight[picked][:, None]), None)
    mixed, _ = lax.scan(per_expert, jnp.zeros((TOKENS, D), jnp.float32), jnp.arange(EXPERTS, dtype=jnp.int32))
    rows_all = jnp.arange(TOKENS, dtype=jnp.int32)
    valid = rows_all % SUF < suffix_len[rows_all // SUF]
    return jnp.where(valid[:, None], resid + mixed, 0.0).astype(jnp.bfloat16)
```

```python
import math

import jax
import jax.numpy as jnp
from jax import lax
from jax.sharding import PartitionSpec as P

HD = 64
TOP = 2


EPS = 1e-05
NEGATIVE = -1e30


def rms_scale(rows, gain):
    rows_wide = rows.astype(jnp.float32)
    mean_square = jnp.mean(rows_wide * rows_wide, axis=-1, keepdims=True)
    return rows_wide * lax.rsqrt(mean_square + EPS) * gain


def level_partial(queries, node_keys, node_values, limits, heads_here, batched):
    senders, row_count, width = queries.shape
    head_dim = width // heads_here
    scale = 1.0 / math.sqrt(head_dim)
    query_heads = queries.reshape(senders, row_count, heads_here, head_dim)
    if batched:
        key_heads = node_keys.reshape(senders, -1, heads_here, head_dim)
        value_heads = node_values.reshape(senders, -1, heads_here, head_dim)
        scores = jnp.einsum(
            "sqhd,skhd->sqhk", query_heads, key_heads, preferred_element_type=jnp.float32
        )
    else:
        key_heads = node_keys.reshape(-1, heads_here, head_dim)
        value_heads = node_values.reshape(-1, heads_here, head_dim)
        scores = jnp.einsum(
            "sqhd,khd->sqhk", query_heads, key_heads, preferred_element_type=jnp.float32
        )
    scores = scores * scale
    slots = jnp.arange(scores.shape[-1], dtype=jnp.int32)
    allowed = slots[None, :] < limits[:, None]
    scores = jnp.where(allowed[:, None, None, :], scores, NEGATIVE)
    peak = jnp.max(scores, axis=-1)
    weights = jnp.exp(scores - peak[..., None])
    total = jnp.sum(weights, axis=-1)
    probs = weights.astype(jnp.bfloat16)
    if batched:
        summed = jnp.einsum(
            "sqhk,skhd->sqhd", probs, value_heads, preferred_element_type=jnp.float32
        )
    else:
        summed = jnp.einsum(
            "sqhk,khd->sqhd", probs, value_heads, preferred_element_type=jnp.float32
        )
    result = (summed / total[..., None]).reshape(senders, row_count, width)
    return (result, peak + jnp.log(total))


def on_device(
    hidden_in,
    attn_gain,
    w_query,
    w_key,
    w_value,
    w_out,
    root_cache,
    mid_cache,
    leaf_cache,
    mid_len,
    leaf_len,
    leaf_of,
    parents,
    suffix_len,
    ffn_gain,
    w_router,
    routes,
    w_gate,
    w_up,
    w_down,
):
    tok_rows, width = hidden_in.shape
    seq_rows = suffix_len.shape[0]
    suffix = tok_rows // seq_rows
    head_dim = HD
    local_width = w_query.shape[1]
    heads_here = local_width // head_dim
    scale = 1.0 / math.sqrt(head_dim)
    owners = lax.axis_size("dp")
    normed = rms_scale(hidden_in, attn_gain).astype(jnp.bfloat16)
    query = jnp.dot(normed, w_query, preferred_element_type=jnp.float32).astype(jnp.bfloat16)
    key = jnp.dot(normed, w_key, preferred_element_type=jnp.float32).astype(jnp.bfloat16)
    value = jnp.dot(normed, w_value, preferred_element_type=jnp.float32).astype(jnp.bfloat16)
    query_heads = query.reshape(tok_rows, heads_here, head_dim)
    piece = lax.all_gather(root_cache, "dp", axis=1, tiled=True)
    running_peak = jnp.full((tok_rows, heads_here), NEGATIVE, jnp.float32)
    piece_keys = piece[0].reshape(-1, heads_here, head_dim)
    piece_values = piece[1].reshape(-1, heads_here, head_dim)
    scores = (
        jnp.einsum("qhd,khd->qhk", query_heads, piece_keys, preferred_element_type=jnp.float32)
        * scale
    )
    new_peak = jnp.maximum(running_peak, jnp.max(scores, axis=-1))
    weights = jnp.exp(scores - new_peak[..., None])
    new_total = jnp.sum(weights, axis=-1)
    added = jnp.einsum(
        "qhk,khd->qhd",
        weights.astype(jnp.bfloat16),
        piece_values,
        preferred_element_type=jnp.float32,
    )
    root_out = added / new_total[..., None]
    root_lse = new_peak + jnp.log(new_total)
    query_seq = query.reshape(seq_rows, suffix, heads_here, head_dim)
    key_seq = key.reshape(seq_rows, suffix, heads_here, head_dim)
    value_seq = value.reshape(seq_rows, suffix, heads_here, head_dim)
    slots = jnp.arange(suffix, dtype=jnp.int32)
    self_ok = (slots[None, None, :] <= slots[None, :, None]) & (
        slots[None, None, :] < suffix_len[:, None, None]
    )
    self_scores = (
        jnp.einsum("sqhd,skhd->sqhk", query_seq, key_seq, preferred_element_type=jnp.float32)
        * scale
    )
    self_scores = jnp.where(self_ok[:, :, None, :], self_scores, NEGATIVE)
    self_peak = jnp.max(self_scores, axis=-1)
    self_weights = jnp.exp(self_scores - self_peak[..., None])
    self_total = jnp.sum(self_weights, axis=-1)
    self_sum = jnp.einsum(
        "sqhk,skhd->sqhd",
        self_weights.astype(jnp.bfloat16),
        value_seq,
        preferred_element_type=jnp.float32,
    )
    self_out = (self_sum / self_total[..., None]).reshape(tok_rows, heads_here, head_dim)
    self_lse = (self_peak + jnp.log(self_total)).reshape(tok_rows, heads_here)
    mid_of = parents[leaf_of]
    leaf_owner = leaf_of // 2
    targets = jnp.arange(owners, dtype=jnp.int32)
    pick_mid = (mid_of[None, :] == targets[:, None]).astype(jnp.bfloat16)
    pick_leaf = (leaf_owner[None, :] == targets[:, None]).astype(jnp.bfloat16)
    flat_query = query.reshape(seq_rows, suffix * local_width)
    sent_mid = jnp.dot(pick_mid, flat_query, preferred_element_type=jnp.float32).astype(
        jnp.bfloat16
    )
    sent_leaf = jnp.dot(pick_leaf, flat_query, preferred_element_type=jnp.float32).astype(
        jnp.bfloat16
    )
    sent = jnp.stack([sent_mid, sent_leaf], axis=1).reshape(owners, 2, suffix, local_width)
    sent_queries = lax.all_to_all(sent, "dp", split_axis=0, concat_axis=0, tiled=True)
    leaf_every = lax.all_gather(leaf_of, "dp", axis=0, tiled=True).reshape(owners, seq_rows)
    me_dp = lax.axis_index("dp")
    second = jnp.any((leaf_every // 2 == me_dp) & (leaf_every % 2 == 1), axis=1)
    senders = sent_queries.shape[0]
    mid_limit = jnp.broadcast_to(mid_len[0], (senders,))
    mid_result, mid_logsum = level_partial(
        sent_queries[:, 0], mid_cache[0, 0], mid_cache[1, 0], mid_limit, heads_here, False
    )
    leaf_keys = jnp.where(second[:, None, None], leaf_cache[0, 1][None], leaf_cache[0, 0][None])
    leaf_values = jnp.where(second[:, None, None], leaf_cache[1, 1][None], leaf_cache[1, 0][None])
    leaf_limit = jnp.where(second, leaf_len[1], leaf_len[0])
    leaf_result, leaf_logsum = level_partial(
        sent_queries[:, 1], leaf_keys, leaf_values, leaf_limit, heads_here, True
    )
    owner_out = jnp.stack([mid_result, leaf_result], axis=1)
    owner_lse = jnp.stack([mid_logsum, leaf_logsum], axis=1)
    owner_all = jnp.concatenate([owner_out, owner_lse], axis=-1)
    back_all = lax.all_to_all(owner_all, "dp", split_axis=0, concat_axis=0, tiled=True)
    back_out = back_all[..., :local_width]
    back_lse = back_all[..., local_width:]
    mid_out = back_out[mid_of, 0].reshape(tok_rows, heads_here, head_dim)
    mid_lse = back_lse[mid_of, 0].reshape(tok_rows, heads_here)
    leaf_out = back_out[leaf_owner, 1].reshape(tok_rows, heads_here, head_dim)
    leaf_lse = back_lse[leaf_owner, 1].reshape(tok_rows, heads_here)
    stacked_lse = jnp.stack([root_lse, mid_lse, leaf_lse, self_lse])
    stacked_out = jnp.stack([root_out, mid_out, leaf_out, self_out])
    overall = jnp.max(stacked_lse, axis=0)
    shares = jnp.exp(stacked_lse - overall)
    combined = jnp.sum(shares[..., None] * stacked_out, axis=0) / jnp.sum(shares, axis=0)[..., None]
    attended = combined.reshape(tok_rows, local_width).astype(jnp.bfloat16)
    projected = jnp.dot(attended, w_out, preferred_element_type=jnp.float32)
    rows_here = tok_rows // lax.axis_size("mp")
    first = lax.axis_index("mp") * rows_here
    attn_rows = lax.psum_scatter(projected, "mp", scatter_dimension=0, tiled=True)
    resid = lax.dynamic_slice_in_dim(hidden_in, first, rows_here, 0).astype(jnp.float32) + attn_rows
    ffn_rows = rms_scale(resid, ffn_gain).astype(jnp.bfloat16)
    ffn_in = lax.all_gather(ffn_rows, "mp", axis=0, tiled=True)
    logits = jnp.dot(ffn_in.astype(jnp.float32), w_router, precision=lax.Precision.HIGHEST)
    chosen = jnp.take_along_axis(logits, routes, axis=1)
    squashed = jax.nn.sigmoid(chosen)
    gates = squashed / jnp.sum(squashed, axis=1, keepdims=True)
    expert = lax.axis_index("mp")
    hit_each = routes == expert
    hit = jnp.any(hit_each, axis=1)
    gate_here = jnp.sum(jnp.where(hit_each, gates, 0.0), axis=1)
    order = jnp.cumsum(hit.astype(jnp.int32)) - 1
    capacity = 3 * TOP * tok_rows // (2 * lax.axis_size("mp"))
    slot_ids = jnp.arange(capacity, dtype=jnp.int32)
    pick_slot = (order[None, :] == slot_ids[:, None]) & hit[None, :]
    dispatch = jnp.dot(
        pick_slot.astype(jnp.bfloat16), ffn_in, preferred_element_type=jnp.float32
    ).astype(jnp.bfloat16)
    slot_gate = jnp.dot(pick_slot.astype(jnp.float32), gate_here, precision=lax.Precision.HIGHEST)
    gate_weight = w_gate[0]
    up_weight = w_up[0]
    down_weight = w_down[0]
    piece = lax.all_gather(dispatch, "dp", axis=0, tiled=True)
    gate_part = jnp.dot(piece, gate_weight, preferred_element_type=jnp.float32)
    up_part = jnp.dot(piece, up_weight, preferred_element_type=jnp.float32)
    partial_out = jnp.dot(
        (jax.nn.silu(gate_part) * up_part).astype(jnp.bfloat16),
        down_weight,
        preferred_element_type=jnp.float32,
    )
    expert_out = lax.psum_scatter(
        partial_out.astype(jnp.bfloat16), "dp", scatter_dimension=0, tiled=True
    )
    weighted = expert_out.astype(jnp.float32) * slot_gate[:, None]
    spread = jnp.dot(pick_slot.astype(jnp.float32).T, weighted, precision=lax.Precision.HIGHEST)
    mixed = lax.psum_scatter(
        spread.astype(jnp.bfloat16), "mp", scatter_dimension=0, tiled=True
    ).astype(jnp.float32)
    row_ids = first + jnp.arange(rows_here, dtype=jnp.int32)
    valid = row_ids % suffix < suffix_len[row_ids // suffix]
    return jnp.where(valid[:, None], resid + mixed, 0.0).astype(jnp.bfloat16)


def solution(mesh):
    return jax.shard_map(
        on_device,
        mesh=mesh,
        in_specs=(
            P("dp", None),
            P(),
            P(None, "mp"),
            P(None, "mp"),
            P(None, "mp"),
            P("mp", None),
            P(None, "dp", "mp"),
            P(None, "dp", None, "mp"),
            P(None, "dp", None, "mp"),
            P("dp"),
            P("dp"),
            P("dp"),
            P(),
            P("dp"),
            P(),
            P(),
            P("dp", None),
            P("mp", None, "dp"),
            P("mp", None, "dp"),
            P("mp", "dp", None),
        ),
        out_specs=P(("dp", "mp"), None),
        check_vma=False,
    )
```

```python
import math

import jax
import jax.numpy as jnp
from jax import lax
from jax.sharding import PartitionSpec as P

HD = 64
TOP = 2


EPS = 1e-05
NEGATIVE = -1e30


def rms_scale(rows, gain):
    rows_wide = rows.astype(jnp.float32)
    mean_square = jnp.mean(rows_wide * rows_wide, axis=-1, keepdims=True)
    return rows_wide * lax.rsqrt(mean_square + EPS) * gain


def level_partial(queries, node_keys, node_values, limits, heads_here, batched):
    senders, row_count, width = queries.shape
    head_dim = width // heads_here
    scale = 1.0 / math.sqrt(head_dim)
    query_heads = queries.reshape(senders, row_count, heads_here, head_dim)
    if batched:
        key_heads = node_keys.reshape(senders, -1, heads_here, head_dim)
        value_heads = node_values.reshape(senders, -1, heads_here, head_dim)
        scores = jnp.einsum(
            "sqhd,skhd->sqhk", query_heads, key_heads, preferred_element_type=jnp.float32
        )
    else:
        key_heads = node_keys.reshape(-1, heads_here, head_dim)
        value_heads = node_values.reshape(-1, heads_here, head_dim)
        scores = jnp.einsum(
            "sqhd,khd->sqhk", query_heads, key_heads, preferred_element_type=jnp.float32
        )
    scores = scores * scale
    slots = jnp.arange(scores.shape[-1], dtype=jnp.int32)
    allowed = slots[None, :] < limits[:, None]
    scores = jnp.where(allowed[:, None, None, :], scores, NEGATIVE)
    peak = jnp.max(scores, axis=-1)
    weights = jnp.exp(scores - peak[..., None])
    total = jnp.sum(weights, axis=-1)
    probs = weights.astype(jnp.bfloat16)
    if batched:
        summed = jnp.einsum(
            "sqhk,skhd->sqhd", probs, value_heads, preferred_element_type=jnp.float32
        )
    else:
        summed = jnp.einsum(
            "sqhk,khd->sqhd", probs, value_heads, preferred_element_type=jnp.float32
        )
    result = (summed / total[..., None]).reshape(senders, row_count, width)
    return (result, peak + jnp.log(total))


def on_device(
    hidden_in,
    attn_gain,
    w_query,
    w_key,
    w_value,
    w_out,
    root_cache,
    mid_cache,
    leaf_cache,
    mid_len,
    leaf_len,
    leaf_of,
    parents,
    suffix_len,
    ffn_gain,
    w_router,
    routes,
    w_gate,
    w_up,
    w_down,
):
    tok_rows, width = hidden_in.shape
    seq_rows = suffix_len.shape[0]
    suffix = tok_rows // seq_rows
    head_dim = HD
    local_width = w_query.shape[1]
    heads_here = local_width // head_dim
    scale = 1.0 / math.sqrt(head_dim)
    owners = lax.axis_size("dp")
    normed = rms_scale(hidden_in, attn_gain).astype(jnp.bfloat16)
    query = jnp.dot(normed, w_query, preferred_element_type=jnp.float32).astype(jnp.bfloat16)
    key = jnp.dot(normed, w_key, preferred_element_type=jnp.float32).astype(jnp.bfloat16)
    value = jnp.dot(normed, w_value, preferred_element_type=jnp.float32).astype(jnp.bfloat16)
    query_heads = query.reshape(tok_rows, heads_here, head_dim)
    piece = lax.all_gather(root_cache, "dp", axis=1, tiled=True)
    running_peak = jnp.full((tok_rows, heads_here), NEGATIVE, jnp.float32)
    piece_keys = piece[0].reshape(-1, heads_here, head_dim)
    piece_values = piece[1].reshape(-1, heads_here, head_dim)
    scores = (
        jnp.einsum("qhd,khd->qhk", query_heads, piece_keys, preferred_element_type=jnp.float32)
        * scale
    )
    new_peak = jnp.maximum(running_peak, jnp.max(scores, axis=-1))
    weights = jnp.exp(scores - new_peak[..., None])
    new_total = jnp.sum(weights, axis=-1)
    added = jnp.einsum(
        "qhk,khd->qhd",
        weights.astype(jnp.bfloat16),
        piece_values,
        preferred_element_type=jnp.float32,
    )
    root_out = added / new_total[..., None]
    root_lse = new_peak + jnp.log(new_total)
    query_seq = query.reshape(seq_rows, suffix, heads_here, head_dim)
    key_seq = key.reshape(seq_rows, suffix, heads_here, head_dim)
    value_seq = value.reshape(seq_rows, suffix, heads_here, head_dim)
    slots = jnp.arange(suffix, dtype=jnp.int32)
    self_ok = (slots[None, None, :] <= slots[None, :, None]) & (
        slots[None, None, :] < suffix_len[:, None, None]
    )
    self_scores = (
        jnp.einsum("sqhd,skhd->sqhk", query_seq, key_seq, preferred_element_type=jnp.float32)
        * scale
    )
    self_scores = jnp.where(self_ok[:, :, None, :], self_scores, NEGATIVE)
    self_peak = jnp.max(self_scores, axis=-1)
    self_weights = jnp.exp(self_scores - self_peak[..., None])
    self_total = jnp.sum(self_weights, axis=-1)
    self_sum = jnp.einsum(
        "sqhk,skhd->sqhd",
        self_weights.astype(jnp.bfloat16),
        value_seq,
        preferred_element_type=jnp.float32,
    )
    self_out = (self_sum / self_total[..., None]).reshape(tok_rows, heads_here, head_dim)
    self_lse = (self_peak + jnp.log(self_total)).reshape(tok_rows, heads_here)
    mid_of = parents[leaf_of]
    leaf_owner = leaf_of // 2
    targets = jnp.arange(owners, dtype=jnp.int32)
    pick_mid = (mid_of[None, :] == targets[:, None]).astype(jnp.bfloat16)
    pick_leaf = (leaf_owner[None, :] == targets[:, None]).astype(jnp.bfloat16)
    flat_query = query.reshape(seq_rows, suffix * local_width)
    sent_mid = jnp.dot(pick_mid, flat_query, preferred_element_type=jnp.float32).astype(
        jnp.bfloat16
    )
    sent_leaf = jnp.dot(pick_leaf, flat_query, preferred_element_type=jnp.float32).astype(
        jnp.bfloat16
    )
    sent = jnp.stack([sent_mid, sent_leaf], axis=1).reshape(owners, 2, suffix, local_width)
    leaf_side = (leaf_of % 2).astype(jnp.float32)
    side_of_target = jnp.dot(
        pick_leaf.astype(jnp.float32), leaf_side, precision=lax.Precision.HIGHEST
    )
    side_rows = jnp.broadcast_to(side_of_target[:, None, None], (owners, 8, local_width))
    sent_all = jnp.concatenate(
        [sent.reshape(owners, 2 * suffix, local_width), side_rows.astype(jnp.bfloat16)], axis=1
    )
    got_all = lax.all_to_all(sent_all, "dp", split_axis=0, concat_axis=0, tiled=True)
    sent_queries = got_all[:, : 2 * suffix].reshape(owners, 2, suffix, local_width)
    second = got_all[:, 2 * suffix, 0] > 0.5
    senders = sent_queries.shape[0]
    mid_limit = jnp.broadcast_to(mid_len[0], (senders,))
    mid_result, mid_logsum = level_partial(
        sent_queries[:, 0], mid_cache[0, 0], mid_cache[1, 0], mid_limit, heads_here, False
    )
    leaf_keys = jnp.where(second[:, None, None], leaf_cache[0, 1][None], leaf_cache[0, 0][None])
    leaf_values = jnp.where(second[:, None, None], leaf_cache[1, 1][None], leaf_cache[1, 0][None])
    leaf_limit = jnp.where(second, leaf_len[1], leaf_len[0])
    leaf_result, leaf_logsum = level_partial(
        sent_queries[:, 1], leaf_keys, leaf_values, leaf_limit, heads_here, True
    )
    owner_out = jnp.stack([mid_result, leaf_result], axis=1)
    owner_lse = jnp.stack([mid_logsum, leaf_logsum], axis=1)
    owner_all = jnp.concatenate([owner_out, owner_lse], axis=-1)
    back_all = lax.all_to_all(owner_all, "dp", split_axis=0, concat_axis=0, tiled=True)
    back_out = back_all[..., :local_width]
    back_lse = back_all[..., local_width:]
    mid_out = back_out[mid_of, 0].reshape(tok_rows, heads_here, head_dim)
    mid_lse = back_lse[mid_of, 0].reshape(tok_rows, heads_here)
    leaf_out = back_out[leaf_owner, 1].reshape(tok_rows, heads_here, head_dim)
    leaf_lse = back_lse[leaf_owner, 1].reshape(tok_rows, heads_here)
    stacked_lse = jnp.stack([root_lse, mid_lse, leaf_lse, self_lse])
    stacked_out = jnp.stack([root_out, mid_out, leaf_out, self_out])
    overall = jnp.max(stacked_lse, axis=0)
    shares = jnp.exp(stacked_lse - overall)
    combined = jnp.sum(shares[..., None] * stacked_out, axis=0) / jnp.sum(shares, axis=0)[..., None]
    attended = combined.reshape(tok_rows, local_width).astype(jnp.bfloat16)
    projected = jnp.dot(attended, w_out, preferred_element_type=jnp.float32)
    rows_here = tok_rows // lax.axis_size("mp")
    first = lax.axis_index("mp") * rows_here
    attn_rows = lax.psum_scatter(projected, "mp", scatter_dimension=0, tiled=True)
    resid = lax.dynamic_slice_in_dim(hidden_in, first, rows_here, 0).astype(jnp.float32) + attn_rows
    ffn_rows = rms_scale(resid, ffn_gain).astype(jnp.bfloat16)
    ffn_in = lax.all_gather(ffn_rows, "mp", axis=0, tiled=True)
    logits = jnp.dot(ffn_in.astype(jnp.float32), w_router, precision=lax.Precision.HIGHEST)
    chosen = jnp.take_along_axis(logits, routes, axis=1)
    squashed = jax.nn.sigmoid(chosen)
    gates = squashed / jnp.sum(squashed, axis=1, keepdims=True)
    expert = lax.axis_index("mp")
    hit_each = routes == expert
    hit = jnp.any(hit_each, axis=1)
    gate_here = jnp.sum(jnp.where(hit_each, gates, 0.0), axis=1)
    order = jnp.cumsum(hit.astype(jnp.int32)) - 1
    capacity = 3 * TOP * tok_rows // (2 * lax.axis_size("mp"))
    slot_ids = jnp.arange(capacity, dtype=jnp.int32)
    pick_slot = (order[None, :] == slot_ids[:, None]) & hit[None, :]
    dispatch = jnp.dot(
        pick_slot.astype(jnp.bfloat16), ffn_in, preferred_element_type=jnp.float32
    ).astype(jnp.bfloat16)
    slot_gate = jnp.dot(pick_slot.astype(jnp.float32), gate_here, precision=lax.Precision.HIGHEST)
    gate_weight = w_gate[0]
    up_weight = w_up[0]
    down_weight = w_down[0]
    piece = lax.all_gather(dispatch, "dp", axis=0, tiled=True)
    gate_part = jnp.dot(piece, gate_weight, preferred_element_type=jnp.float32)
    up_part = jnp.dot(piece, up_weight, preferred_element_type=jnp.float32)
    partial_out = jnp.dot(
        (jax.nn.silu(gate_part) * up_part).astype(jnp.bfloat16),
        down_weight,
        preferred_element_type=jnp.float32,
    )
    expert_out = lax.psum_scatter(
        partial_out.astype(jnp.bfloat16), "dp", scatter_dimension=0, tiled=True
    )
    weighted = expert_out.astype(jnp.float32) * slot_gate[:, None]
    spread = jnp.dot(pick_slot.astype(jnp.float32).T, weighted, precision=lax.Precision.HIGHEST)
    mixed = lax.psum_scatter(
        spread.astype(jnp.bfloat16), "mp", scatter_dimension=0, tiled=True
    ).astype(jnp.float32)
    row_ids = first + jnp.arange(rows_here, dtype=jnp.int32)
    valid = row_ids % suffix < suffix_len[row_ids // suffix]
    return jnp.where(valid[:, None], resid + mixed, 0.0).astype(jnp.bfloat16)


def solution(mesh):
    return jax.shard_map(
        on_device,
        mesh=mesh,
        in_specs=(
            P("dp", None),
            P(),
            P(None, "mp"),
            P(None, "mp"),
            P(None, "mp"),
            P("mp", None),
            P(None, "dp", "mp"),
            P(None, "dp", None, "mp"),
            P(None, "dp", None, "mp"),
            P("dp"),
            P("dp"),
            P("dp"),
            P(),
            P("dp"),
            P(),
            P(),
            P("dp", None),
            P("mp", None, "dp"),
            P("mp", None, "dp"),
            P("mp", "dp", None),
        ),
        out_specs=P(("dp", "mp"), None),
        check_vma=False,
    )
```

```python
import math

import jax
import jax.numpy as jnp
from jax import lax
import functools

from jax.experimental import pallas as pl
from jax.experimental.pallas import tpu as pltpu
from jax.sharding import PartitionSpec as P

MESH = pl.DeviceIdType.MESH


def _greet(n, me, dp):
    barrier = pltpu.get_barrier_semaphore()
    for k in range(1, n):
        pl.semaphore_signal(barrier, 1, device_id=(dp, (me + k) % n), device_id_type=MESH)
    pl.semaphore_wait(barrier, n - 1)


def _mp_sum_kernel(n, x_ref, o_ref, recv, send_sem, recv_sem):
    me = lax.axis_index("mp")
    dp = lax.axis_index("dp")
    rows = o_ref.shape[0]
    _greet(n, me, dp)
    copies = []
    for k in range(1, n):
        peer = (me + k) % n
        copy = pltpu.make_async_remote_copy(
            src_ref=x_ref.at[pl.ds(pl.multiple_of(peer * rows, rows), rows)],
            dst_ref=recv.at[k],
            send_sem=send_sem.at[k],
            recv_sem=recv_sem.at[k],
            device_id=(dp, peer),
            device_id_type=MESH,
        )
        copy.start()
        copies.append(copy)
    for copy in copies:
        copy.wait()
    total = x_ref[pl.ds(pl.multiple_of(me * rows, rows), rows), :].astype(jnp.float32)
    for k in range(1, n):
        total = total + recv[k].astype(jnp.float32)
    o_ref[...] = total


def mp_sum_scatter(x, collective_id):
    n = lax.axis_size("mp")
    rows = x.shape[0] // n
    cols = x.shape[1]
    return pl.pallas_call(
        functools.partial(_mp_sum_kernel, n),
        out_shape=jax.ShapeDtypeStruct((rows, cols), jnp.float32),
        in_specs=[pl.BlockSpec(memory_space=pltpu.VMEM)],
        out_specs=pl.BlockSpec(memory_space=pltpu.VMEM),
        scratch_shapes=[
            pltpu.VMEM((n, rows, cols), x.dtype),
            pltpu.SemaphoreType.DMA((n,)),
            pltpu.SemaphoreType.DMA((n,)),
        ],
        compiler_params=pltpu.CompilerParams(collective_id=collective_id, has_side_effects=True),
    )(x)


def _mp_gather_kernel(n, x_ref, o_ref, recv, send_sem, recv_sem):
    me = lax.axis_index("mp")
    dp = lax.axis_index("dp")
    rows = x_ref.shape[0]
    _greet(n, me, dp)
    copies = []
    for k in range(1, n):
        peer = (me + k) % n
        copy = pltpu.make_async_remote_copy(
            src_ref=x_ref,
            dst_ref=recv.at[k],
            send_sem=send_sem.at[k],
            recv_sem=recv_sem.at[k],
            device_id=(dp, peer),
            device_id_type=MESH,
        )
        copy.start()
        copies.append(copy)
    for copy in copies:
        copy.wait()
    o_ref[pl.ds(pl.multiple_of(me * rows, rows), rows), :] = x_ref[...]
    for k in range(1, n):
        source = (me + n - k) % n
        o_ref[pl.ds(pl.multiple_of(source * rows, rows), rows), :] = recv[k]


def mp_gather(x, collective_id):
    n = lax.axis_size("mp")
    rows, cols = x.shape
    return pl.pallas_call(
        functools.partial(_mp_gather_kernel, n),
        out_shape=jax.ShapeDtypeStruct((n * rows, cols), x.dtype),
        in_specs=[pl.BlockSpec(memory_space=pltpu.VMEM)],
        out_specs=pl.BlockSpec(memory_space=pltpu.VMEM),
        scratch_shapes=[
            pltpu.VMEM((n, rows, cols), x.dtype),
            pltpu.SemaphoreType.DMA((n,)),
            pltpu.SemaphoreType.DMA((n,)),
        ],
        compiler_params=pltpu.CompilerParams(collective_id=collective_id, has_side_effects=True),
    )(x)


HD = 64
TOP = 2


EPS = 1e-05
NEGATIVE = -1e30


def rms_scale(rows, gain):
    rows_wide = rows.astype(jnp.float32)
    mean_square = jnp.mean(rows_wide * rows_wide, axis=-1, keepdims=True)
    return rows_wide * lax.rsqrt(mean_square + EPS) * gain


def level_partial(queries, node_keys, node_values, limits, heads_here, batched):
    senders, row_count, width = queries.shape
    head_dim = width // heads_here
    scale = 1.0 / math.sqrt(head_dim)
    query_heads = queries.reshape(senders, row_count, heads_here, head_dim)
    if batched:
        key_heads = node_keys.reshape(senders, -1, heads_here, head_dim)
        value_heads = node_values.reshape(senders, -1, heads_here, head_dim)
        scores = jnp.einsum(
            "sqhd,skhd->sqhk", query_heads, key_heads, preferred_element_type=jnp.float32
        )
    else:
        key_heads = node_keys.reshape(-1, heads_here, head_dim)
        value_heads = node_values.reshape(-1, heads_here, head_dim)
        scores = jnp.einsum(
            "sqhd,khd->sqhk", query_heads, key_heads, preferred_element_type=jnp.float32
        )
    scores = scores * scale
    slots = jnp.arange(scores.shape[-1], dtype=jnp.int32)
    allowed = slots[None, :] < limits[:, None]
    scores = jnp.where(allowed[:, None, None, :], scores, NEGATIVE)
    peak = jnp.max(scores, axis=-1)
    weights = jnp.exp(scores - peak[..., None])
    total = jnp.sum(weights, axis=-1)
    probs = weights.astype(jnp.bfloat16)
    if batched:
        summed = jnp.einsum(
            "sqhk,skhd->sqhd", probs, value_heads, preferred_element_type=jnp.float32
        )
    else:
        summed = jnp.einsum(
            "sqhk,khd->sqhd", probs, value_heads, preferred_element_type=jnp.float32
        )
    result = (summed / total[..., None]).reshape(senders, row_count, width)
    return (result, peak + jnp.log(total))


def on_device(
    hidden_in,
    attn_gain,
    w_query,
    w_key,
    w_value,
    w_out,
    root_cache,
    mid_cache,
    leaf_cache,
    mid_len,
    leaf_len,
    leaf_of,
    parents,
    suffix_len,
    ffn_gain,
    w_router,
    routes,
    w_gate,
    w_up,
    w_down,
):
    tok_rows, width = hidden_in.shape
    seq_rows = suffix_len.shape[0]
    suffix = tok_rows // seq_rows
    head_dim = HD
    local_width = w_query.shape[1]
    heads_here = local_width // head_dim
    scale = 1.0 / math.sqrt(head_dim)
    owners = lax.axis_size("dp")
    normed = rms_scale(hidden_in, attn_gain).astype(jnp.bfloat16)
    query = jnp.dot(normed, w_query, preferred_element_type=jnp.float32).astype(jnp.bfloat16)
    key = jnp.dot(normed, w_key, preferred_element_type=jnp.float32).astype(jnp.bfloat16)
    value = jnp.dot(normed, w_value, preferred_element_type=jnp.float32).astype(jnp.bfloat16)
    query_heads = query.reshape(tok_rows, heads_here, head_dim)
    piece = lax.all_gather(root_cache, "dp", axis=1, tiled=True)
    running_peak = jnp.full((tok_rows, heads_here), NEGATIVE, jnp.float32)
    piece_keys = piece[0].reshape(-1, heads_here, head_dim)
    piece_values = piece[1].reshape(-1, heads_here, head_dim)
    scores = (
        jnp.einsum("qhd,khd->qhk", query_heads, piece_keys, preferred_element_type=jnp.float32)
        * scale
    )
    new_peak = jnp.maximum(running_peak, jnp.max(scores, axis=-1))
    weights = jnp.exp(scores - new_peak[..., None])
    new_total = jnp.sum(weights, axis=-1)
    added = jnp.einsum(
        "qhk,khd->qhd",
        weights.astype(jnp.bfloat16),
        piece_values,
        preferred_element_type=jnp.float32,
    )
    root_out = added / new_total[..., None]
    root_lse = new_peak + jnp.log(new_total)
    query_seq = query.reshape(seq_rows, suffix, heads_here, head_dim)
    key_seq = key.reshape(seq_rows, suffix, heads_here, head_dim)
    value_seq = value.reshape(seq_rows, suffix, heads_here, head_dim)
    slots = jnp.arange(suffix, dtype=jnp.int32)
    self_ok = (slots[None, None, :] <= slots[None, :, None]) & (
        slots[None, None, :] < suffix_len[:, None, None]
    )
    self_scores = (
        jnp.einsum("sqhd,skhd->sqhk", query_seq, key_seq, preferred_element_type=jnp.float32)
        * scale
    )
    self_scores = jnp.where(self_ok[:, :, None, :], self_scores, NEGATIVE)
    self_peak = jnp.max(self_scores, axis=-1)
    self_weights = jnp.exp(self_scores - self_peak[..., None])
    self_total = jnp.sum(self_weights, axis=-1)
    self_sum = jnp.einsum(
        "sqhk,skhd->sqhd",
        self_weights.astype(jnp.bfloat16),
        value_seq,
        preferred_element_type=jnp.float32,
    )
    self_out = (self_sum / self_total[..., None]).reshape(tok_rows, heads_here, head_dim)
    self_lse = (self_peak + jnp.log(self_total)).reshape(tok_rows, heads_here)
    mid_of = parents[leaf_of]
    leaf_owner = leaf_of // 2
    targets = jnp.arange(owners, dtype=jnp.int32)
    pick_mid = (mid_of[None, :] == targets[:, None]).astype(jnp.bfloat16)
    pick_leaf = (leaf_owner[None, :] == targets[:, None]).astype(jnp.bfloat16)
    flat_query = query.reshape(seq_rows, suffix * local_width)
    sent_mid = jnp.dot(pick_mid, flat_query, preferred_element_type=jnp.float32).astype(
        jnp.bfloat16
    )
    sent_leaf = jnp.dot(pick_leaf, flat_query, preferred_element_type=jnp.float32).astype(
        jnp.bfloat16
    )
    sent = jnp.stack([sent_mid, sent_leaf], axis=1).reshape(owners, 2, suffix, local_width)
    leaf_side = (leaf_of % 2).astype(jnp.float32)
    side_of_target = jnp.dot(
        pick_leaf.astype(jnp.float32), leaf_side, precision=lax.Precision.HIGHEST
    )
    side_rows = jnp.broadcast_to(side_of_target[:, None, None], (owners, 8, local_width))
    sent_all = jnp.concatenate(
        [sent.reshape(owners, 2 * suffix, local_width), side_rows.astype(jnp.bfloat16)], axis=1
    )
    got_all = lax.all_to_all(sent_all, "dp", split_axis=0, concat_axis=0, tiled=True)
    sent_queries = got_all[:, : 2 * suffix].reshape(owners, 2, suffix, local_width)
    second = got_all[:, 2 * suffix, 0] > 0.5
    senders = sent_queries.shape[0]
    mid_limit = jnp.broadcast_to(mid_len[0], (senders,))
    mid_result, mid_logsum = level_partial(
        sent_queries[:, 0], mid_cache[0, 0], mid_cache[1, 0], mid_limit, heads_here, False
    )
    leaf_keys = jnp.where(second[:, None, None], leaf_cache[0, 1][None], leaf_cache[0, 0][None])
    leaf_values = jnp.where(second[:, None, None], leaf_cache[1, 1][None], leaf_cache[1, 0][None])
    leaf_limit = jnp.where(second, leaf_len[1], leaf_len[0])
    leaf_result, leaf_logsum = level_partial(
        sent_queries[:, 1], leaf_keys, leaf_values, leaf_limit, heads_here, True
    )
    owner_out = jnp.stack([mid_result, leaf_result], axis=1)
    owner_lse = jnp.stack([mid_logsum, leaf_logsum], axis=1)
    owner_all = jnp.concatenate([owner_out, owner_lse], axis=-1)
    back_all = lax.all_to_all(owner_all, "dp", split_axis=0, concat_axis=0, tiled=True)
    back_out = back_all[..., :local_width]
    back_lse = back_all[..., local_width:]
    mid_out = back_out[mid_of, 0].reshape(tok_rows, heads_here, head_dim)
    mid_lse = back_lse[mid_of, 0].reshape(tok_rows, heads_here)
    leaf_out = back_out[leaf_owner, 1].reshape(tok_rows, heads_here, head_dim)
    leaf_lse = back_lse[leaf_owner, 1].reshape(tok_rows, heads_here)
    stacked_lse = jnp.stack([root_lse, mid_lse, leaf_lse, self_lse])
    stacked_out = jnp.stack([root_out, mid_out, leaf_out, self_out])
    overall = jnp.max(stacked_lse, axis=0)
    shares = jnp.exp(stacked_lse - overall)
    combined = jnp.sum(shares[..., None] * stacked_out, axis=0) / jnp.sum(shares, axis=0)[..., None]
    attended = combined.reshape(tok_rows, local_width).astype(jnp.bfloat16)
    projected = jnp.dot(attended, w_out, preferred_element_type=jnp.float32)
    rows_here = tok_rows // lax.axis_size("mp")
    first = lax.axis_index("mp") * rows_here
    attn_rows = mp_sum_scatter(projected.astype(jnp.bfloat16), 0)
    resid = lax.dynamic_slice_in_dim(hidden_in, first, rows_here, 0).astype(jnp.float32) + attn_rows
    ffn_rows = rms_scale(resid, ffn_gain).astype(jnp.bfloat16)
    ffn_in = mp_gather(ffn_rows, 1)
    logits = jnp.dot(ffn_in.astype(jnp.float32), w_router, precision=lax.Precision.HIGHEST)
    chosen = jnp.take_along_axis(logits, routes, axis=1)
    squashed = jax.nn.sigmoid(chosen)
    gates = squashed / jnp.sum(squashed, axis=1, keepdims=True)
    expert = lax.axis_index("mp")
    hit_each = routes == expert
    hit = jnp.any(hit_each, axis=1)
    gate_here = jnp.sum(jnp.where(hit_each, gates, 0.0), axis=1)
    order = jnp.cumsum(hit.astype(jnp.int32)) - 1
    capacity = 3 * TOP * tok_rows // (2 * lax.axis_size("mp"))
    slot_ids = jnp.arange(capacity, dtype=jnp.int32)
    pick_slot = (order[None, :] == slot_ids[:, None]) & hit[None, :]
    dispatch = jnp.dot(
        pick_slot.astype(jnp.bfloat16), ffn_in, preferred_element_type=jnp.float32
    ).astype(jnp.bfloat16)
    slot_gate = jnp.dot(pick_slot.astype(jnp.float32), gate_here, precision=lax.Precision.HIGHEST)
    gate_weight = w_gate[0]
    up_weight = w_up[0]
    down_weight = w_down[0]
    piece = lax.all_gather(dispatch, "dp", axis=0, tiled=True)
    gate_part = jnp.dot(piece, gate_weight, preferred_element_type=jnp.float32)
    up_part = jnp.dot(piece, up_weight, preferred_element_type=jnp.float32)
    partial_out = jnp.dot(
        (jax.nn.silu(gate_part) * up_part).astype(jnp.bfloat16),
        down_weight,
        preferred_element_type=jnp.float32,
    )
    expert_out = lax.psum_scatter(
        partial_out.astype(jnp.bfloat16), "dp", scatter_dimension=0, tiled=True
    )
    weighted = expert_out.astype(jnp.float32) * slot_gate[:, None]
    spread = jnp.dot(pick_slot.astype(jnp.float32).T, weighted, precision=lax.Precision.HIGHEST)
    mixed = mp_sum_scatter(spread.astype(jnp.bfloat16), 2)
    row_ids = first + jnp.arange(rows_here, dtype=jnp.int32)
    valid = row_ids % suffix < suffix_len[row_ids // suffix]
    return jnp.where(valid[:, None], resid + mixed, 0.0).astype(jnp.bfloat16)


def solution(mesh):
    return jax.shard_map(
        on_device,
        mesh=mesh,
        in_specs=(
            P("dp", None),
            P(),
            P(None, "mp"),
            P(None, "mp"),
            P(None, "mp"),
            P("mp", None),
            P(None, "dp", "mp"),
            P(None, "dp", None, "mp"),
            P(None, "dp", None, "mp"),
            P("dp"),
            P("dp"),
            P("dp"),
            P(),
            P("dp"),
            P(),
            P(),
            P("dp", None),
            P("mp", None, "dp"),
            P("mp", None, "dp"),
            P("mp", "dp", None),
        ),
        out_specs=P(("dp", "mp"), None),
        check_vma=False,
    )
```

```python
import math

import jax
import jax.numpy as jnp
from jax import lax
import functools

from jax.experimental import pallas as pl
from jax.experimental.pallas import tpu as pltpu
from jax.sharding import PartitionSpec as P

MESH = pl.DeviceIdType.MESH


def _greet(n, me, dp):
    barrier = pltpu.get_barrier_semaphore()
    for k in range(1, n):
        pl.semaphore_signal(barrier, 1, device_id=(dp, (me + k) % n), device_id_type=MESH)
    pl.semaphore_wait(barrier, n - 1)


def _mp_sum_kernel(n, x_ref, o_ref, recv, send_sem, recv_sem):
    me = lax.axis_index("mp")
    dp = lax.axis_index("dp")
    rows = o_ref.shape[0]
    _greet(n, me, dp)
    copies = []
    for k in range(1, n):
        peer = (me + k) % n
        copy = pltpu.make_async_remote_copy(
            src_ref=x_ref.at[pl.ds(pl.multiple_of(peer * rows, rows), rows)],
            dst_ref=recv.at[k],
            send_sem=send_sem.at[k],
            recv_sem=recv_sem.at[k],
            device_id=(dp, peer),
            device_id_type=MESH,
        )
        copy.start()
        copies.append(copy)
    for copy in copies:
        copy.wait()
    total = x_ref[pl.ds(pl.multiple_of(me * rows, rows), rows), :].astype(jnp.float32)
    for k in range(1, n):
        total = total + recv[k].astype(jnp.float32)
    o_ref[...] = total


def mp_sum_scatter(x, collective_id):
    n = lax.axis_size("mp")
    rows = x.shape[0] // n
    cols = x.shape[1]
    return pl.pallas_call(
        functools.partial(_mp_sum_kernel, n),
        out_shape=jax.ShapeDtypeStruct((rows, cols), jnp.float32),
        in_specs=[pl.BlockSpec(memory_space=pltpu.VMEM)],
        out_specs=pl.BlockSpec(memory_space=pltpu.VMEM),
        scratch_shapes=[
            pltpu.VMEM((n, rows, cols), x.dtype),
            pltpu.SemaphoreType.DMA((n,)),
            pltpu.SemaphoreType.DMA((n,)),
        ],
        compiler_params=pltpu.CompilerParams(collective_id=collective_id, has_side_effects=True),
    )(x)


def _mp_gather_kernel(n, x_ref, o_ref, recv, send_sem, recv_sem):
    me = lax.axis_index("mp")
    dp = lax.axis_index("dp")
    rows = x_ref.shape[0]
    _greet(n, me, dp)
    copies = []
    for k in range(1, n):
        peer = (me + k) % n
        copy = pltpu.make_async_remote_copy(
            src_ref=x_ref,
            dst_ref=recv.at[k],
            send_sem=send_sem.at[k],
            recv_sem=recv_sem.at[k],
            device_id=(dp, peer),
            device_id_type=MESH,
        )
        copy.start()
        copies.append(copy)
    for copy in copies:
        copy.wait()
    o_ref[pl.ds(pl.multiple_of(me * rows, rows), rows), :] = x_ref[...]
    for k in range(1, n):
        source = (me + n - k) % n
        o_ref[pl.ds(pl.multiple_of(source * rows, rows), rows), :] = recv[k]


def mp_gather(x, collective_id):
    n = lax.axis_size("mp")
    rows, cols = x.shape
    return pl.pallas_call(
        functools.partial(_mp_gather_kernel, n),
        out_shape=jax.ShapeDtypeStruct((n * rows, cols), x.dtype),
        in_specs=[pl.BlockSpec(memory_space=pltpu.VMEM)],
        out_specs=pl.BlockSpec(memory_space=pltpu.VMEM),
        scratch_shapes=[
            pltpu.VMEM((n, rows, cols), x.dtype),
            pltpu.SemaphoreType.DMA((n,)),
            pltpu.SemaphoreType.DMA((n,)),
        ],
        compiler_params=pltpu.CompilerParams(collective_id=collective_id, has_side_effects=True),
    )(x)


HD = 64
TOP = 2


EPS = 1e-05
NEGATIVE = -1e30


def _attn_kernel(chunk, q_ref, k_ref, v_ref, lo_ref, hi_ref, o_ref, lse_ref):
    q = q_ref[0]
    rows, head_dim = q.shape
    scale = 1.0 / math.sqrt(head_dim)
    lo = lo_ref[...]
    hi = hi_ref[...]
    steps = k_ref.shape[1] // chunk

    def body(c, carry):
        peak, total, acc = carry
        start = pl.multiple_of(c * chunk, chunk)
        keys = k_ref[0, pl.ds(start, chunk), :]
        values = v_ref[0, pl.ds(start, chunk), :]
        scores = lax.dot_general(
            q, keys, (((1,), (1,)), ((), ())), preferred_element_type=jnp.float32
        ) * scale
        slots = start + lax.broadcasted_iota(jnp.int32, scores.shape, 1)
        scores = jnp.where((slots >= lo) & (slots < hi), scores, NEGATIVE)
        new_peak = jnp.maximum(peak, jnp.max(scores, axis=1, keepdims=True))
        alpha = jnp.exp(peak - new_peak)
        weights = jnp.exp(scores - new_peak)
        total = alpha * total + jnp.sum(weights, axis=1, keepdims=True)
        acc = alpha * acc + jnp.dot(
            weights.astype(jnp.bfloat16), values, preferred_element_type=jnp.float32
        )
        return new_peak, total, acc

    init = (
        jnp.full((rows, 1), NEGATIVE, jnp.float32),
        jnp.zeros((rows, 1), jnp.float32),
        jnp.zeros((rows, head_dim), jnp.float32),
    )
    peak, total, acc = lax.fori_loop(0, steps, body, init)
    o_ref[0] = acc / total
    lse_ref[0] = peak + jnp.log(total)


def masked_attention(q, k, v, lo, hi, row_tile=128, chunk=512):
    heads, rows, head_dim = q.shape
    keys = k.shape[1]
    chunk = min(chunk, keys)
    row_tile = min(row_tile, rows)
    grid = (heads, rows // row_tile)
    return pl.pallas_call(
        functools.partial(_attn_kernel, chunk),
        out_shape=(
            jax.ShapeDtypeStruct((heads, rows, head_dim), jnp.float32),
            jax.ShapeDtypeStruct((heads, rows, 1), jnp.float32),
        ),
        grid=grid,
        in_specs=[
            pl.BlockSpec((1, row_tile, head_dim), lambda h, r: (h, r, 0)),
            pl.BlockSpec((1, keys, head_dim), lambda h, r: (h, 0, 0)),
            pl.BlockSpec((1, keys, head_dim), lambda h, r: (h, 0, 0)),
            pl.BlockSpec((row_tile, 1), lambda h, r: (r, 0)),
            pl.BlockSpec((row_tile, 1), lambda h, r: (r, 0)),
        ],
        out_specs=(
            pl.BlockSpec((1, row_tile, head_dim), lambda h, r: (h, r, 0)),
            pl.BlockSpec((1, row_tile, 1), lambda h, r: (h, r, 0)),
        ),
        cost_estimate=pl.CostEstimate(
            flops=4 * heads * rows * keys * head_dim,
            transcendentals=heads * rows * keys,
            bytes_accessed=2 * (q.size + k.size + v.size) + 4 * heads * rows * (head_dim + 1),
        ),
    )(q, k, v, lo, hi)


def heads_first(x, heads_here):
    return x.reshape(x.shape[0], heads_here, -1).transpose(1, 0, 2)


def rms_scale(rows, gain):
    rows_wide = rows.astype(jnp.float32)
    mean_square = jnp.mean(rows_wide * rows_wide, axis=-1, keepdims=True)
    return rows_wide * lax.rsqrt(mean_square + EPS) * gain


def level_partial(queries, node_keys, node_values, limits, heads_here, batched):
    senders, row_count, width = queries.shape
    head_dim = width // heads_here
    scale = 1.0 / math.sqrt(head_dim)
    query_heads = queries.reshape(senders, row_count, heads_here, head_dim)
    if batched:
        key_heads = node_keys.reshape(senders, -1, heads_here, head_dim)
        value_heads = node_values.reshape(senders, -1, heads_here, head_dim)
        scores = jnp.einsum(
            "sqhd,skhd->sqhk", query_heads, key_heads, preferred_element_type=jnp.float32
        )
    else:
        key_heads = node_keys.reshape(-1, heads_here, head_dim)
        value_heads = node_values.reshape(-1, heads_here, head_dim)
        scores = jnp.einsum(
            "sqhd,khd->sqhk", query_heads, key_heads, preferred_element_type=jnp.float32
        )
    scores = scores * scale
    slots = jnp.arange(scores.shape[-1], dtype=jnp.int32)
    allowed = slots[None, :] < limits[:, None]
    scores = jnp.where(allowed[:, None, None, :], scores, NEGATIVE)
    peak = jnp.max(scores, axis=-1)
    weights = jnp.exp(scores - peak[..., None])
    total = jnp.sum(weights, axis=-1)
    probs = weights.astype(jnp.bfloat16)
    if batched:
        summed = jnp.einsum(
            "sqhk,skhd->sqhd", probs, value_heads, preferred_element_type=jnp.float32
        )
    else:
        summed = jnp.einsum(
            "sqhk,khd->sqhd", probs, value_heads, preferred_element_type=jnp.float32
        )
    result = (summed / total[..., None]).reshape(senders, row_count, width)
    return (result, peak + jnp.log(total))


def on_device(
    hidden_in,
    attn_gain,
    w_query,
    w_key,
    w_value,
    w_out,
    root_cache,
    mid_cache,
    leaf_cache,
    mid_len,
    leaf_len,
    leaf_of,
    parents,
    suffix_len,
    ffn_gain,
    w_router,
    routes,
    w_gate,
    w_up,
    w_down,
):
    tok_rows, width = hidden_in.shape
    seq_rows = suffix_len.shape[0]
    suffix = tok_rows // seq_rows
    head_dim = HD
    local_width = w_query.shape[1]
    heads_here = local_width // head_dim
    scale = 1.0 / math.sqrt(head_dim)
    owners = lax.axis_size("dp")
    normed = rms_scale(hidden_in, attn_gain).astype(jnp.bfloat16)
    query = jnp.dot(normed, w_query, preferred_element_type=jnp.float32).astype(jnp.bfloat16)
    key = jnp.dot(normed, w_key, preferred_element_type=jnp.float32).astype(jnp.bfloat16)
    value = jnp.dot(normed, w_value, preferred_element_type=jnp.float32).astype(jnp.bfloat16)
    query_heads = query.reshape(tok_rows, heads_here, head_dim)
    piece = lax.all_gather(root_cache, "dp", axis=1, tiled=True)
    root_keys_total = piece.shape[1]
    root_o, root_l = masked_attention(
        heads_first(query, heads_here),
        heads_first(piece[0], heads_here),
        heads_first(piece[1], heads_here),
        jnp.zeros((tok_rows, 1), jnp.int32),
        jnp.full((tok_rows, 1), root_keys_total, jnp.int32),
    )
    root_out = root_o.transpose(1, 0, 2)
    root_lse = root_l[..., 0].T
    query_seq = query.reshape(seq_rows, suffix, heads_here, head_dim)
    key_seq = key.reshape(seq_rows, suffix, heads_here, head_dim)
    value_seq = value.reshape(seq_rows, suffix, heads_here, head_dim)
    slots = jnp.arange(suffix, dtype=jnp.int32)
    self_ok = (slots[None, None, :] <= slots[None, :, None]) & (
        slots[None, None, :] < suffix_len[:, None, None]
    )
    self_scores = (
        jnp.einsum("sqhd,skhd->sqhk", query_seq, key_seq, preferred_element_type=jnp.float32)
        * scale
    )
    self_scores = jnp.where(self_ok[:, :, None, :], self_scores, NEGATIVE)
    self_peak = jnp.max(self_scores, axis=-1)
    self_weights = jnp.exp(self_scores - self_peak[..., None])
    self_total = jnp.sum(self_weights, axis=-1)
    self_sum = jnp.einsum(
        "sqhk,skhd->sqhd",
        self_weights.astype(jnp.bfloat16),
        value_seq,
        preferred_element_type=jnp.float32,
    )
    self_out = (self_sum / self_total[..., None]).reshape(tok_rows, heads_here, head_dim)
    self_lse = (self_peak + jnp.log(self_total)).reshape(tok_rows, heads_here)
    mid_of = parents[leaf_of]
    leaf_owner = leaf_of // 2
    targets = jnp.arange(owners, dtype=jnp.int32)
    pick_mid = (mid_of[None, :] == targets[:, None]).astype(jnp.bfloat16)
    pick_leaf = (leaf_owner[None, :] == targets[:, None]).astype(jnp.bfloat16)
    flat_query = query.reshape(seq_rows, suffix * local_width)
    sent_mid = jnp.dot(pick_mid, flat_query, preferred_element_type=jnp.float32).astype(
        jnp.bfloat16
    )
    sent_leaf = jnp.dot(pick_leaf, flat_query, preferred_element_type=jnp.float32).astype(
        jnp.bfloat16
    )
    sent = jnp.stack([sent_mid, sent_leaf], axis=1).reshape(owners, 2, suffix, local_width)
    leaf_side = (leaf_of % 2).astype(jnp.float32)
    side_of_target = jnp.dot(
        pick_leaf.astype(jnp.float32), leaf_side, precision=lax.Precision.HIGHEST
    )
    side_rows = jnp.broadcast_to(side_of_target[:, None, None], (owners, 8, local_width))
    sent_all = jnp.concatenate(
        [sent.reshape(owners, 2 * suffix, local_width), side_rows.astype(jnp.bfloat16)], axis=1
    )
    got_all = lax.all_to_all(sent_all, "dp", split_axis=0, concat_axis=0, tiled=True)
    sent_queries = got_all[:, : 2 * suffix].reshape(owners, 2, suffix, local_width)
    second = got_all[:, 2 * suffix, 0] > 0.5
    senders = sent_queries.shape[0]
    node_len = mid_cache.shape[2]
    level_rows = senders * suffix
    mid_o, mid_l = masked_attention(
        heads_first(sent_queries[:, 0].reshape(level_rows, local_width), heads_here),
        heads_first(mid_cache[0, 0], heads_here),
        heads_first(mid_cache[1, 0], heads_here),
        jnp.zeros((level_rows, 1), jnp.int32),
        jnp.broadcast_to(mid_len[0], (level_rows, 1)),
    )
    mid_result = mid_o.transpose(1, 0, 2).reshape(senders, suffix, local_width)
    mid_logsum = mid_l[..., 0].T.reshape(senders, suffix, heads_here)
    leaf_low = jnp.where(second, node_len, 0).astype(jnp.int32)
    leaf_high = leaf_low + jnp.where(second, leaf_len[1], leaf_len[0])
    leaf_o, leaf_l = masked_attention(
        heads_first(sent_queries[:, 1].reshape(level_rows, local_width), heads_here),
        heads_first(leaf_cache[0].reshape(-1, local_width), heads_here),
        heads_first(leaf_cache[1].reshape(-1, local_width), heads_here),
        jnp.repeat(leaf_low, suffix)[:, None],
        jnp.repeat(leaf_high, suffix)[:, None],
    )
    leaf_result = leaf_o.transpose(1, 0, 2).reshape(senders, suffix, local_width)
    leaf_logsum = leaf_l[..., 0].T.reshape(senders, suffix, heads_here)
    owner_out = jnp.stack([mid_result, leaf_result], axis=1)
    owner_lse = jnp.stack([mid_logsum, leaf_logsum], axis=1)
    owner_all = jnp.concatenate([owner_out, owner_lse], axis=-1)
    back_all = lax.all_to_all(owner_all, "dp", split_axis=0, concat_axis=0, tiled=True)
    back_out = back_all[..., :local_width]
    back_lse = back_all[..., local_width:]
    mid_out = back_out[mid_of, 0].reshape(tok_rows, heads_here, head_dim)
    mid_lse = back_lse[mid_of, 0].reshape(tok_rows, heads_here)
    leaf_out = back_out[leaf_owner, 1].reshape(tok_rows, heads_here, head_dim)
    leaf_lse = back_lse[leaf_owner, 1].reshape(tok_rows, heads_here)
    stacked_lse = jnp.stack([root_lse, mid_lse, leaf_lse, self_lse])
    stacked_out = jnp.stack([root_out, mid_out, leaf_out, self_out])
    overall = jnp.max(stacked_lse, axis=0)
    shares = jnp.exp(stacked_lse - overall)
    combined = jnp.sum(shares[..., None] * stacked_out, axis=0) / jnp.sum(shares, axis=0)[..., None]
    attended = combined.reshape(tok_rows, local_width).astype(jnp.bfloat16)
    projected = jnp.dot(attended, w_out, preferred_element_type=jnp.float32)
    rows_here = tok_rows // lax.axis_size("mp")
    first = lax.axis_index("mp") * rows_here
    attn_rows = mp_sum_scatter(projected.astype(jnp.bfloat16), 0)
    resid = lax.dynamic_slice_in_dim(hidden_in, first, rows_here, 0).astype(jnp.float32) + attn_rows
    ffn_rows = rms_scale(resid, ffn_gain).astype(jnp.bfloat16)
    ffn_in = mp_gather(ffn_rows, 1)
    logits = jnp.dot(ffn_in.astype(jnp.float32), w_router, precision=lax.Precision.HIGHEST)
    chosen = jnp.take_along_axis(logits, routes, axis=1)
    squashed = jax.nn.sigmoid(chosen)
    gates = squashed / jnp.sum(squashed, axis=1, keepdims=True)
    expert = lax.axis_index("mp")
    hit_each = routes == expert
    hit = jnp.any(hit_each, axis=1)
    gate_here = jnp.sum(jnp.where(hit_each, gates, 0.0), axis=1)
    order = jnp.cumsum(hit.astype(jnp.int32)) - 1
    capacity = 3 * TOP * tok_rows // (2 * lax.axis_size("mp"))
    slot_ids = jnp.arange(capacity, dtype=jnp.int32)
    pick_slot = (order[None, :] == slot_ids[:, None]) & hit[None, :]
    dispatch = jnp.dot(
        pick_slot.astype(jnp.bfloat16), ffn_in, preferred_element_type=jnp.float32
    ).astype(jnp.bfloat16)
    slot_gate = jnp.dot(pick_slot.astype(jnp.float32), gate_here, precision=lax.Precision.HIGHEST)
    gate_weight = w_gate[0]
    up_weight = w_up[0]
    down_weight = w_down[0]
    piece = lax.all_gather(dispatch, "dp", axis=0, tiled=True)
    gate_part = jnp.dot(piece, gate_weight, preferred_element_type=jnp.float32)
    up_part = jnp.dot(piece, up_weight, preferred_element_type=jnp.float32)
    partial_out = jnp.dot(
        (jax.nn.silu(gate_part) * up_part).astype(jnp.bfloat16),
        down_weight,
        preferred_element_type=jnp.float32,
    )
    expert_out = lax.psum_scatter(
        partial_out.astype(jnp.bfloat16), "dp", scatter_dimension=0, tiled=True
    )
    weighted = expert_out.astype(jnp.float32) * slot_gate[:, None]
    spread = jnp.dot(pick_slot.astype(jnp.float32).T, weighted, precision=lax.Precision.HIGHEST)
    mixed = mp_sum_scatter(spread.astype(jnp.bfloat16), 2)
    row_ids = first + jnp.arange(rows_here, dtype=jnp.int32)
    valid = row_ids % suffix < suffix_len[row_ids // suffix]
    return jnp.where(valid[:, None], resid + mixed, 0.0).astype(jnp.bfloat16)


def solution(mesh):
    return jax.shard_map(
        on_device,
        mesh=mesh,
        in_specs=(
            P("dp", None),
            P(),
            P(None, "mp"),
            P(None, "mp"),
            P(None, "mp"),
            P("mp", None),
            P(None, "dp", "mp"),
            P(None, "dp", None, "mp"),
            P(None, "dp", None, "mp"),
            P("dp"),
            P("dp"),
            P("dp"),
            P(),
            P("dp"),
            P(),
            P(),
            P("dp", None),
            P("mp", None, "dp"),
            P("mp", None, "dp"),
            P("mp", "dp", None),
        ),
        out_specs=P(("dp", "mp"), None),
        check_vma=False,
    )
```

```python
import math

import jax
import jax.numpy as jnp
from jax import lax
import functools

from jax.experimental import pallas as pl
from jax.experimental.pallas import tpu as pltpu
from jax.sharding import PartitionSpec as P

MESH = pl.DeviceIdType.MESH


def _greet(n, me, dp):
    barrier = pltpu.get_barrier_semaphore()
    for k in range(1, n):
        pl.semaphore_signal(barrier, 1, device_id=(dp, (me + k) % n), device_id_type=MESH)
    pl.semaphore_wait(barrier, n - 1)


def _mp_sum_kernel(n, x_ref, o_ref, recv, send_sem, recv_sem):
    me = lax.axis_index("mp")
    dp = lax.axis_index("dp")
    rows = o_ref.shape[0]
    _greet(n, me, dp)
    copies = []
    for k in range(1, n):
        peer = (me + k) % n
        copy = pltpu.make_async_remote_copy(
            src_ref=x_ref.at[pl.ds(pl.multiple_of(peer * rows, rows), rows)],
            dst_ref=recv.at[k],
            send_sem=send_sem.at[k],
            recv_sem=recv_sem.at[k],
            device_id=(dp, peer),
            device_id_type=MESH,
        )
        copy.start()
        copies.append(copy)
    for copy in copies:
        copy.wait()
    total = x_ref[pl.ds(pl.multiple_of(me * rows, rows), rows), :].astype(jnp.float32)
    for k in range(1, n):
        total = total + recv[k].astype(jnp.float32)
    o_ref[...] = total


def mp_sum_scatter(x, collective_id):
    n = lax.axis_size("mp")
    rows = x.shape[0] // n
    cols = x.shape[1]
    return pl.pallas_call(
        functools.partial(_mp_sum_kernel, n),
        out_shape=jax.ShapeDtypeStruct((rows, cols), jnp.float32),
        in_specs=[pl.BlockSpec(memory_space=pltpu.VMEM)],
        out_specs=pl.BlockSpec(memory_space=pltpu.VMEM),
        scratch_shapes=[
            pltpu.VMEM((n, rows, cols), x.dtype),
            pltpu.SemaphoreType.DMA((n,)),
            pltpu.SemaphoreType.DMA((n,)),
        ],
        compiler_params=pltpu.CompilerParams(collective_id=collective_id, has_side_effects=True),
    )(x)


def _mp_gather_kernel(n, x_ref, o_ref, recv, send_sem, recv_sem):
    me = lax.axis_index("mp")
    dp = lax.axis_index("dp")
    rows = x_ref.shape[0]
    _greet(n, me, dp)
    copies = []
    for k in range(1, n):
        peer = (me + k) % n
        copy = pltpu.make_async_remote_copy(
            src_ref=x_ref,
            dst_ref=recv.at[k],
            send_sem=send_sem.at[k],
            recv_sem=recv_sem.at[k],
            device_id=(dp, peer),
            device_id_type=MESH,
        )
        copy.start()
        copies.append(copy)
    for copy in copies:
        copy.wait()
    o_ref[pl.ds(pl.multiple_of(me * rows, rows), rows), :] = x_ref[...]
    for k in range(1, n):
        source = (me + n - k) % n
        o_ref[pl.ds(pl.multiple_of(source * rows, rows), rows), :] = recv[k]


def mp_gather(x, collective_id):
    n = lax.axis_size("mp")
    rows, cols = x.shape
    return pl.pallas_call(
        functools.partial(_mp_gather_kernel, n),
        out_shape=jax.ShapeDtypeStruct((n * rows, cols), x.dtype),
        in_specs=[pl.BlockSpec(memory_space=pltpu.VMEM)],
        out_specs=pl.BlockSpec(memory_space=pltpu.VMEM),
        scratch_shapes=[
            pltpu.VMEM((n, rows, cols), x.dtype),
            pltpu.SemaphoreType.DMA((n,)),
            pltpu.SemaphoreType.DMA((n,)),
        ],
        compiler_params=pltpu.CompilerParams(collective_id=collective_id, has_side_effects=True),
    )(x)


HD = 64
TOP = 2


EPS = 1e-05
NEGATIVE = -1e30


def _attn_kernel(chunk, masked, head_dim, q_ref, k_ref, v_ref, lo_ref, hi_ref, o_ref, lse_ref):
    rows, width = q_ref.shape
    scale = 1.0 / math.sqrt(head_dim)
    pair = (q_ref[...].astype(jnp.float32) * scale).astype(jnp.bfloat16)
    first_half = lax.broadcasted_iota(jnp.int32, (rows, width), 1) < head_dim
    zero = jnp.zeros_like(pair)
    queries = (jnp.where(first_half, pair, zero), jnp.where(first_half, zero, pair))
    lo = lo_ref[...]
    hi = hi_ref[...]
    steps = k_ref.shape[0] // chunk

    def body(c, carry):
        start = pl.multiple_of(c * chunk, chunk)
        keys = k_ref[pl.ds(start, chunk), :]
        values = v_ref[pl.ds(start, chunk), :]
        if masked:
            slots = start + lax.broadcasted_iota(jnp.int32, (rows, chunk), 1)
            allowed = (slots >= lo) & (slots < hi)
        out = []
        for h in range(2):
            peak, total, acc = carry[3 * h: 3 * h + 3]
            scores = lax.dot_general(
                queries[h], keys, (((1,), (1,)), ((), ())), preferred_element_type=jnp.float32
            )
            if masked:
                scores = jnp.where(allowed, scores, NEGATIVE)
            new_peak = jnp.maximum(peak, jnp.max(scores, axis=1, keepdims=True))
            alpha = jnp.exp(peak - new_peak)
            weights = jnp.exp(scores - new_peak)
            total = alpha * total + jnp.sum(weights, axis=1, keepdims=True)
            acc = alpha * acc + jnp.dot(
                weights.astype(jnp.bfloat16), values, preferred_element_type=jnp.float32
            )
            out += [new_peak, total, acc]
        return tuple(out)

    start_peak = jnp.full((rows, 1), NEGATIVE, jnp.float32)
    start_total = jnp.zeros((rows, 1), jnp.float32)
    start_acc = jnp.zeros((rows, width), jnp.float32)
    init = (start_peak, start_total, start_acc) * 2
    pe, te, ae, po, to, ao = lax.fori_loop(0, steps, body, init)
    o_ref[...] = jnp.where(first_half, ae / te, ao / to)
    lse_ref[...] = jnp.where(first_half, pe + jnp.log(te), po + jnp.log(to))


def pair_attention(q, k, v, lo, hi, head_dim, masked, row_tile=128, chunk=256):
    rows, width = q.shape
    keys = k.shape[0]
    chunk = min(chunk, keys)
    row_tile = min(row_tile, rows)
    lanes = 2 * head_dim
    grid = (width // lanes, rows // row_tile)
    return pl.pallas_call(
        functools.partial(_attn_kernel, chunk, masked, head_dim),
        out_shape=(
            jax.ShapeDtypeStruct((rows, width), jnp.float32),
            jax.ShapeDtypeStruct((rows, width), jnp.float32),
        ),
        grid=grid,
        in_specs=[
            pl.BlockSpec((row_tile, lanes), lambda j, r: (r, j)),
            pl.BlockSpec((keys, lanes), lambda j, r: (0, j)),
            pl.BlockSpec((keys, lanes), lambda j, r: (0, j)),
            pl.BlockSpec((row_tile, 1), lambda j, r: (r, 0)),
            pl.BlockSpec((row_tile, 1), lambda j, r: (r, 0)),
        ],
        out_specs=(
            pl.BlockSpec((row_tile, lanes), lambda j, r: (r, j)),
            pl.BlockSpec((row_tile, lanes), lambda j, r: (r, j)),
        ),
        cost_estimate=pl.CostEstimate(
            flops=8 * rows * keys * width,
            transcendentals=rows * keys * (width // head_dim),
            bytes_accessed=2 * (q.size + k.size + v.size) + 8 * rows * width,
        ),
    )(q, k, v, lo, hi)


def heads_first(x, heads_here):
    return x.reshape(x.shape[0], heads_here, -1).transpose(1, 0, 2)


def rms_scale(rows, gain):
    rows_wide = rows.astype(jnp.float32)
    mean_square = jnp.mean(rows_wide * rows_wide, axis=-1, keepdims=True)
    return rows_wide * lax.rsqrt(mean_square + EPS) * gain


def level_partial(queries, node_keys, node_values, limits, heads_here, batched):
    senders, row_count, width = queries.shape
    head_dim = width // heads_here
    scale = 1.0 / math.sqrt(head_dim)
    query_heads = queries.reshape(senders, row_count, heads_here, head_dim)
    if batched:
        key_heads = node_keys.reshape(senders, -1, heads_here, head_dim)
        value_heads = node_values.reshape(senders, -1, heads_here, head_dim)
        scores = jnp.einsum(
            "sqhd,skhd->sqhk", query_heads, key_heads, preferred_element_type=jnp.float32
        )
    else:
        key_heads = node_keys.reshape(-1, heads_here, head_dim)
        value_heads = node_values.reshape(-1, heads_here, head_dim)
        scores = jnp.einsum(
            "sqhd,khd->sqhk", query_heads, key_heads, preferred_element_type=jnp.float32
        )
    scores = scores * scale
    slots = jnp.arange(scores.shape[-1], dtype=jnp.int32)
    allowed = slots[None, :] < limits[:, None]
    scores = jnp.where(allowed[:, None, None, :], scores, NEGATIVE)
    peak = jnp.max(scores, axis=-1)
    weights = jnp.exp(scores - peak[..., None])
    total = jnp.sum(weights, axis=-1)
    probs = weights.astype(jnp.bfloat16)
    if batched:
        summed = jnp.einsum(
            "sqhk,skhd->sqhd", probs, value_heads, preferred_element_type=jnp.float32
        )
    else:
        summed = jnp.einsum(
            "sqhk,khd->sqhd", probs, value_heads, preferred_element_type=jnp.float32
        )
    result = (summed / total[..., None]).reshape(senders, row_count, width)
    return (result, peak + jnp.log(total))


def on_device(
    hidden_in,
    attn_gain,
    w_query,
    w_key,
    w_value,
    w_out,
    root_cache,
    mid_cache,
    leaf_cache,
    mid_len,
    leaf_len,
    leaf_of,
    parents,
    suffix_len,
    ffn_gain,
    w_router,
    routes,
    w_gate,
    w_up,
    w_down,
):
    tok_rows, width = hidden_in.shape
    seq_rows = suffix_len.shape[0]
    suffix = tok_rows // seq_rows
    head_dim = HD
    local_width = w_query.shape[1]
    heads_here = local_width // head_dim
    scale = 1.0 / math.sqrt(head_dim)
    owners = lax.axis_size("dp")
    normed = rms_scale(hidden_in, attn_gain).astype(jnp.bfloat16)
    query = jnp.dot(normed, w_query, preferred_element_type=jnp.float32).astype(jnp.bfloat16)
    key = jnp.dot(normed, w_key, preferred_element_type=jnp.float32).astype(jnp.bfloat16)
    value = jnp.dot(normed, w_value, preferred_element_type=jnp.float32).astype(jnp.bfloat16)
    query_heads = query.reshape(tok_rows, heads_here, head_dim)
    piece = lax.all_gather(root_cache, "dp", axis=1, tiled=True)
    root_keys_total = piece.shape[1]
    root_o, root_l = pair_attention(
        query,
        piece[0],
        piece[1],
        jnp.zeros((tok_rows, 1), jnp.int32),
        jnp.full((tok_rows, 1), root_keys_total, jnp.int32),
        head_dim,
        False,
    )
    root_out = root_o.reshape(tok_rows, heads_here, head_dim)
    root_lse = root_l[:, ::head_dim]
    query_seq = query.reshape(seq_rows, suffix, heads_here, head_dim)
    key_seq = key.reshape(seq_rows, suffix, heads_here, head_dim)
    value_seq = value.reshape(seq_rows, suffix, heads_here, head_dim)
    slots = jnp.arange(suffix, dtype=jnp.int32)
    self_ok = (slots[None, None, :] <= slots[None, :, None]) & (
        slots[None, None, :] < suffix_len[:, None, None]
    )
    self_scores = (
        jnp.einsum("sqhd,skhd->sqhk", query_seq, key_seq, preferred_element_type=jnp.float32)
        * scale
    )
    self_scores = jnp.where(self_ok[:, :, None, :], self_scores, NEGATIVE)
    self_peak = jnp.max(self_scores, axis=-1)
    self_weights = jnp.exp(self_scores - self_peak[..., None])
    self_total = jnp.sum(self_weights, axis=-1)
    self_sum = jnp.einsum(
        "sqhk,skhd->sqhd",
        self_weights.astype(jnp.bfloat16),
        value_seq,
        preferred_element_type=jnp.float32,
    )
    self_out = (self_sum / self_total[..., None]).reshape(tok_rows, heads_here, head_dim)
    self_lse = (self_peak + jnp.log(self_total)).reshape(tok_rows, heads_here)
    mid_of = parents[leaf_of]
    leaf_owner = leaf_of // 2
    targets = jnp.arange(owners, dtype=jnp.int32)
    pick_mid = (mid_of[None, :] == targets[:, None]).astype(jnp.bfloat16)
    pick_leaf = (leaf_owner[None, :] == targets[:, None]).astype(jnp.bfloat16)
    flat_query = query.reshape(seq_rows, suffix * local_width)
    sent_mid = jnp.dot(pick_mid, flat_query, preferred_element_type=jnp.float32).astype(
        jnp.bfloat16
    )
    sent_leaf = jnp.dot(pick_leaf, flat_query, preferred_element_type=jnp.float32).astype(
        jnp.bfloat16
    )
    sent = jnp.stack([sent_mid, sent_leaf], axis=1).reshape(owners, 2, suffix, local_width)
    leaf_side = (leaf_of % 2).astype(jnp.float32)
    side_of_target = jnp.dot(
        pick_leaf.astype(jnp.float32), leaf_side, precision=lax.Precision.HIGHEST
    )
    side_rows = jnp.broadcast_to(side_of_target[:, None, None], (owners, 8, local_width))
    sent_all = jnp.concatenate(
        [sent.reshape(owners, 2 * suffix, local_width), side_rows.astype(jnp.bfloat16)], axis=1
    )
    got_all = lax.all_to_all(sent_all, "dp", split_axis=0, concat_axis=0, tiled=True)
    sent_queries = got_all[:, : 2 * suffix].reshape(owners, 2, suffix, local_width)
    second = got_all[:, 2 * suffix, 0] > 0.5
    senders = sent_queries.shape[0]
    node_len = mid_cache.shape[2]
    level_rows = senders * suffix
    mid_o, mid_l = pair_attention(
        sent_queries[:, 0].reshape(level_rows, local_width),
        mid_cache[0, 0],
        mid_cache[1, 0],
        jnp.zeros((level_rows, 1), jnp.int32),
        jnp.broadcast_to(mid_len[0], (level_rows, 1)),
        head_dim,
        True,
    )
    mid_result = mid_o.reshape(senders, suffix, local_width)
    mid_logsum = mid_l[:, ::head_dim].reshape(senders, suffix, heads_here)
    leaf_low = jnp.where(second, node_len, 0).astype(jnp.int32)
    leaf_high = leaf_low + jnp.where(second, leaf_len[1], leaf_len[0])
    leaf_o, leaf_l = pair_attention(
        sent_queries[:, 1].reshape(level_rows, local_width),
        leaf_cache[0].reshape(-1, local_width),
        leaf_cache[1].reshape(-1, local_width),
        jnp.repeat(leaf_low, suffix)[:, None],
        jnp.repeat(leaf_high, suffix)[:, None],
        head_dim,
        True,
    )
    leaf_result = leaf_o.reshape(senders, suffix, local_width)
    leaf_logsum = leaf_l[:, ::head_dim].reshape(senders, suffix, heads_here)
    owner_out = jnp.stack([mid_result, leaf_result], axis=1)
    owner_lse = jnp.stack([mid_logsum, leaf_logsum], axis=1)
    owner_all = jnp.concatenate([owner_out, owner_lse], axis=-1)
    back_all = lax.all_to_all(owner_all, "dp", split_axis=0, concat_axis=0, tiled=True)
    back_out = back_all[..., :local_width]
    back_lse = back_all[..., local_width:]
    mid_out = back_out[mid_of, 0].reshape(tok_rows, heads_here, head_dim)
    mid_lse = back_lse[mid_of, 0].reshape(tok_rows, heads_here)
    leaf_out = back_out[leaf_owner, 1].reshape(tok_rows, heads_here, head_dim)
    leaf_lse = back_lse[leaf_owner, 1].reshape(tok_rows, heads_here)
    stacked_lse = jnp.stack([root_lse, mid_lse, leaf_lse, self_lse])
    stacked_out = jnp.stack([root_out, mid_out, leaf_out, self_out])
    overall = jnp.max(stacked_lse, axis=0)
    shares = jnp.exp(stacked_lse - overall)
    combined = jnp.sum(shares[..., None] * stacked_out, axis=0) / jnp.sum(shares, axis=0)[..., None]
    attended = combined.reshape(tok_rows, local_width).astype(jnp.bfloat16)
    projected = jnp.dot(attended, w_out, preferred_element_type=jnp.float32)
    rows_here = tok_rows // lax.axis_size("mp")
    first = lax.axis_index("mp") * rows_here
    attn_rows = mp_sum_scatter(projected.astype(jnp.bfloat16), 0)
    resid = lax.dynamic_slice_in_dim(hidden_in, first, rows_here, 0).astype(jnp.float32) + attn_rows
    ffn_rows = rms_scale(resid, ffn_gain).astype(jnp.bfloat16)
    ffn_in = mp_gather(ffn_rows, 1)
    logits = jnp.dot(ffn_in.astype(jnp.float32), w_router, precision=lax.Precision.HIGHEST)
    chosen = jnp.take_along_axis(logits, routes, axis=1)
    squashed = jax.nn.sigmoid(chosen)
    gates = squashed / jnp.sum(squashed, axis=1, keepdims=True)
    expert = lax.axis_index("mp")
    hit_each = routes == expert
    hit = jnp.any(hit_each, axis=1)
    gate_here = jnp.sum(jnp.where(hit_each, gates, 0.0), axis=1)
    order = jnp.cumsum(hit.astype(jnp.int32)) - 1
    capacity = 3 * TOP * tok_rows // (2 * lax.axis_size("mp"))
    slot_ids = jnp.arange(capacity, dtype=jnp.int32)
    pick_slot = (order[None, :] == slot_ids[:, None]) & hit[None, :]
    dispatch = jnp.dot(
        pick_slot.astype(jnp.bfloat16), ffn_in, preferred_element_type=jnp.float32
    ).astype(jnp.bfloat16)
    slot_gate = jnp.dot(pick_slot.astype(jnp.float32), gate_here, precision=lax.Precision.HIGHEST)
    gate_weight = w_gate[0]
    up_weight = w_up[0]
    down_weight = w_down[0]
    piece = lax.all_gather(dispatch, "dp", axis=0, tiled=True)
    gate_part = jnp.dot(piece, gate_weight, preferred_element_type=jnp.float32)
    up_part = jnp.dot(piece, up_weight, preferred_element_type=jnp.float32)
    partial_out = jnp.dot(
        (jax.nn.silu(gate_part) * up_part).astype(jnp.bfloat16),
        down_weight,
        preferred_element_type=jnp.float32,
    )
    expert_out = lax.psum_scatter(
        partial_out.astype(jnp.bfloat16), "dp", scatter_dimension=0, tiled=True
    )
    weighted = expert_out.astype(jnp.float32) * slot_gate[:, None]
    spread = jnp.dot(pick_slot.astype(jnp.float32).T, weighted, precision=lax.Precision.HIGHEST)
    mixed = mp_sum_scatter(spread.astype(jnp.bfloat16), 2)
    row_ids = first + jnp.arange(rows_here, dtype=jnp.int32)
    valid = row_ids % suffix < suffix_len[row_ids // suffix]
    return jnp.where(valid[:, None], resid + mixed, 0.0).astype(jnp.bfloat16)


def solution(mesh):
    return jax.shard_map(
        on_device,
        mesh=mesh,
        in_specs=(
            P("dp", None),
            P(),
            P(None, "mp"),
            P(None, "mp"),
            P(None, "mp"),
            P("mp", None),
            P(None, "dp", "mp"),
            P(None, "dp", None, "mp"),
            P(None, "dp", None, "mp"),
            P("dp"),
            P("dp"),
            P("dp"),
            P(),
            P("dp"),
            P(),
            P(),
            P("dp", None),
            P("mp", None, "dp"),
            P("mp", None, "dp"),
            P("mp", "dp", None),
        ),
        out_specs=P(("dp", "mp"), None),
        check_vma=False,
    )
```

```python
import math

import jax
import jax.numpy as jnp
from jax import lax
import functools

from jax.experimental import pallas as pl
from jax.experimental.pallas import tpu as pltpu
from jax.sharding import PartitionSpec as P

MESH = pl.DeviceIdType.MESH


def _greet(n, me, dp):
    barrier = pltpu.get_barrier_semaphore()
    for k in range(1, n):
        pl.semaphore_signal(barrier, 1, device_id=(dp, (me + k) % n), device_id_type=MESH)
    pl.semaphore_wait(barrier, n - 1)


def _mp_sum_kernel(n, x_ref, o_ref, recv, send_sem, recv_sem):
    me = lax.axis_index("mp")
    dp = lax.axis_index("dp")
    rows = o_ref.shape[0]
    _greet(n, me, dp)
    copies = []
    for k in range(1, n):
        peer = (me + k) % n
        copy = pltpu.make_async_remote_copy(
            src_ref=x_ref.at[pl.ds(pl.multiple_of(peer * rows, rows), rows)],
            dst_ref=recv.at[k],
            send_sem=send_sem.at[k],
            recv_sem=recv_sem.at[k],
            device_id=(dp, peer),
            device_id_type=MESH,
        )
        copy.start()
        copies.append(copy)
    for copy in copies:
        copy.wait()
    total = x_ref[pl.ds(pl.multiple_of(me * rows, rows), rows), :].astype(jnp.float32)
    for k in range(1, n):
        total = total + recv[k].astype(jnp.float32)
    o_ref[...] = total


def mp_sum_scatter(x, collective_id):
    n = lax.axis_size("mp")
    rows = x.shape[0] // n
    cols = x.shape[1]
    return pl.pallas_call(
        functools.partial(_mp_sum_kernel, n),
        out_shape=jax.ShapeDtypeStruct((rows, cols), jnp.float32),
        in_specs=[pl.BlockSpec(memory_space=pltpu.VMEM)],
        out_specs=pl.BlockSpec(memory_space=pltpu.VMEM),
        scratch_shapes=[
            pltpu.VMEM((n, rows, cols), x.dtype),
            pltpu.SemaphoreType.DMA((n,)),
            pltpu.SemaphoreType.DMA((n,)),
        ],
        compiler_params=pltpu.CompilerParams(collective_id=collective_id, has_side_effects=True),
    )(x)


def _mp_gather_kernel(n, x_ref, o_ref, recv, send_sem, recv_sem):
    me = lax.axis_index("mp")
    dp = lax.axis_index("dp")
    rows = x_ref.shape[0]
    _greet(n, me, dp)
    copies = []
    for k in range(1, n):
        peer = (me + k) % n
        copy = pltpu.make_async_remote_copy(
            src_ref=x_ref,
            dst_ref=recv.at[k],
            send_sem=send_sem.at[k],
            recv_sem=recv_sem.at[k],
            device_id=(dp, peer),
            device_id_type=MESH,
        )
        copy.start()
        copies.append(copy)
    for copy in copies:
        copy.wait()
    o_ref[pl.ds(pl.multiple_of(me * rows, rows), rows), :] = x_ref[...]
    for k in range(1, n):
        source = (me + n - k) % n
        o_ref[pl.ds(pl.multiple_of(source * rows, rows), rows), :] = recv[k]


def mp_gather(x, collective_id):
    n = lax.axis_size("mp")
    rows, cols = x.shape
    return pl.pallas_call(
        functools.partial(_mp_gather_kernel, n),
        out_shape=jax.ShapeDtypeStruct((n * rows, cols), x.dtype),
        in_specs=[pl.BlockSpec(memory_space=pltpu.VMEM)],
        out_specs=pl.BlockSpec(memory_space=pltpu.VMEM),
        scratch_shapes=[
            pltpu.VMEM((n, rows, cols), x.dtype),
            pltpu.SemaphoreType.DMA((n,)),
            pltpu.SemaphoreType.DMA((n,)),
        ],
        compiler_params=pltpu.CompilerParams(collective_id=collective_id, has_side_effects=True),
    )(x)


HD = 64
TOP = 2


EPS = 1e-05
NEGATIVE = -1e30


def rms_scale(rows, gain):
    rows_wide = rows.astype(jnp.float32)
    mean_square = jnp.mean(rows_wide * rows_wide, axis=-1, keepdims=True)
    return rows_wide * lax.rsqrt(mean_square + EPS) * gain


def level_partial(queries, node_keys, node_values, limits, heads_here, batched):
    senders, row_count, width = queries.shape
    head_dim = width // heads_here
    scale = 1.0 / math.sqrt(head_dim)
    query_heads = queries.reshape(senders, row_count, heads_here, head_dim)
    if batched:
        key_heads = node_keys.reshape(senders, -1, heads_here, head_dim)
        value_heads = node_values.reshape(senders, -1, heads_here, head_dim)
        scores = jnp.einsum(
            "sqhd,skhd->sqhk", query_heads, key_heads, preferred_element_type=jnp.float32
        )
    else:
        key_heads = node_keys.reshape(-1, heads_here, head_dim)
        value_heads = node_values.reshape(-1, heads_here, head_dim)
        scores = jnp.einsum(
            "sqhd,khd->sqhk", query_heads, key_heads, preferred_element_type=jnp.float32
        )
    scores = scores * scale
    slots = jnp.arange(scores.shape[-1], dtype=jnp.int32)
    allowed = slots[None, :] < limits[:, None]
    scores = jnp.where(allowed[:, None, None, :], scores, NEGATIVE)
    peak = jnp.max(scores, axis=-1)
    weights = jnp.exp(scores - peak[..., None])
    total = jnp.sum(weights, axis=-1)
    probs = weights.astype(jnp.bfloat16)
    if batched:
        summed = jnp.einsum(
            "sqhk,skhd->sqhd", probs, value_heads, preferred_element_type=jnp.float32
        )
    else:
        summed = jnp.einsum(
            "sqhk,khd->sqhd", probs, value_heads, preferred_element_type=jnp.float32
        )
    result = (summed / total[..., None]).reshape(senders, row_count, width)
    return (result, peak + jnp.log(total))


def on_device(
    hidden_in,
    attn_gain,
    w_query,
    w_key,
    w_value,
    w_out,
    root_cache,
    mid_cache,
    leaf_cache,
    mid_len,
    leaf_len,
    leaf_of,
    parents,
    suffix_len,
    ffn_gain,
    w_router,
    routes,
    w_gate,
    w_up,
    w_down,
):
    tok_rows, width = hidden_in.shape
    seq_rows = suffix_len.shape[0]
    suffix = tok_rows // seq_rows
    head_dim = HD
    local_width = w_query.shape[1]
    heads_here = local_width // head_dim
    scale = 1.0 / math.sqrt(head_dim)
    owners = lax.axis_size("dp")
    normed = rms_scale(hidden_in, attn_gain).astype(jnp.bfloat16)
    query = jnp.dot(normed, w_query, preferred_element_type=jnp.float32).astype(jnp.bfloat16)
    key = jnp.dot(normed, w_key, preferred_element_type=jnp.float32).astype(jnp.bfloat16)
    value = jnp.dot(normed, w_value, preferred_element_type=jnp.float32).astype(jnp.bfloat16)
    query_heads = query.reshape(tok_rows, heads_here, head_dim)
    piece = lax.all_gather(root_cache, "dp", axis=1, tiled=True)
    running_peak = jnp.full((tok_rows, heads_here), NEGATIVE, jnp.float32)
    piece_keys = piece[0].reshape(-1, heads_here, head_dim)
    piece_values = piece[1].reshape(-1, heads_here, head_dim)
    scores = (
        jnp.einsum("qhd,khd->qhk", query_heads, piece_keys, preferred_element_type=jnp.float32)
        * scale
    )
    new_peak = jnp.maximum(running_peak, jnp.max(scores, axis=-1))
    weights = jnp.exp(scores - new_peak[..., None])
    new_total = jnp.sum(weights, axis=-1)
    added = jnp.einsum(
        "qhk,khd->qhd",
        weights.astype(jnp.bfloat16),
        piece_values,
        preferred_element_type=jnp.float32,
    )
    root_out = added / new_total[..., None]
    root_lse = new_peak + jnp.log(new_total)
    query_seq = query.reshape(seq_rows, suffix, heads_here, head_dim)
    key_seq = key.reshape(seq_rows, suffix, heads_here, head_dim)
    value_seq = value.reshape(seq_rows, suffix, heads_here, head_dim)
    slots = jnp.arange(suffix, dtype=jnp.int32)
    self_ok = (slots[None, None, :] <= slots[None, :, None]) & (
        slots[None, None, :] < suffix_len[:, None, None]
    )
    self_scores = (
        jnp.einsum("sqhd,skhd->sqhk", query_seq, key_seq, preferred_element_type=jnp.float32)
        * scale
    )
    self_scores = jnp.where(self_ok[:, :, None, :], self_scores, NEGATIVE)
    self_peak = jnp.max(self_scores, axis=-1)
    self_weights = jnp.exp(self_scores - self_peak[..., None])
    self_total = jnp.sum(self_weights, axis=-1)
    self_sum = jnp.einsum(
        "sqhk,skhd->sqhd",
        self_weights.astype(jnp.bfloat16),
        value_seq,
        preferred_element_type=jnp.float32,
    )
    self_out = (self_sum / self_total[..., None]).reshape(tok_rows, heads_here, head_dim)
    self_lse = (self_peak + jnp.log(self_total)).reshape(tok_rows, heads_here)
    mid_of = parents[leaf_of]
    leaf_owner = leaf_of // 2
    targets = jnp.arange(owners, dtype=jnp.int32)
    pick_mid = (mid_of[None, :] == targets[:, None]).astype(jnp.bfloat16)
    pick_leaf = (leaf_owner[None, :] == targets[:, None]).astype(jnp.bfloat16)
    flat_query = query.reshape(seq_rows, suffix * local_width)
    sent_mid = jnp.dot(pick_mid, flat_query, preferred_element_type=jnp.float32).astype(
        jnp.bfloat16
    )
    sent_leaf = jnp.dot(pick_leaf, flat_query, preferred_element_type=jnp.float32).astype(
        jnp.bfloat16
    )
    sent = jnp.stack([sent_mid, sent_leaf], axis=1).reshape(owners, 2, suffix, local_width)
    leaf_side = (leaf_of % 2).astype(jnp.float32)
    side_of_target = jnp.dot(
        pick_leaf.astype(jnp.float32), leaf_side, precision=lax.Precision.HIGHEST
    )
    side_rows = jnp.broadcast_to(side_of_target[:, None, None], (owners, 8, local_width))
    sent_all = jnp.concatenate(
        [sent.reshape(owners, 2 * suffix, local_width), side_rows.astype(jnp.bfloat16)], axis=1
    )
    got_all = lax.all_to_all(sent_all, "dp", split_axis=0, concat_axis=0, tiled=True)
    sent_queries = got_all[:, : 2 * suffix].reshape(owners, 2, suffix, local_width)
    second = got_all[:, 2 * suffix, 0] > 0.5
    senders = sent_queries.shape[0]
    mid_limit = jnp.broadcast_to(mid_len[0], (senders,))
    mid_result, mid_logsum = level_partial(
        sent_queries[:, 0], mid_cache[0, 0], mid_cache[1, 0], mid_limit, heads_here, False
    )
    leaf_keys = jnp.where(second[:, None, None], leaf_cache[0, 1][None], leaf_cache[0, 0][None])
    leaf_values = jnp.where(second[:, None, None], leaf_cache[1, 1][None], leaf_cache[1, 0][None])
    leaf_limit = jnp.where(second, leaf_len[1], leaf_len[0])
    leaf_result, leaf_logsum = level_partial(
        sent_queries[:, 1], leaf_keys, leaf_values, leaf_limit, heads_here, True
    )
    owner_out = jnp.stack([mid_result, leaf_result], axis=1)
    owner_lse = jnp.stack([mid_logsum, leaf_logsum], axis=1)
    owner_all = jnp.concatenate([owner_out, owner_lse], axis=-1)
    back_all = lax.all_to_all(owner_all, "dp", split_axis=0, concat_axis=0, tiled=True)
    back_out = back_all[..., :local_width]
    back_lse = back_all[..., local_width:]
    mid_out = back_out[mid_of, 0].reshape(tok_rows, heads_here, head_dim)
    mid_lse = back_lse[mid_of, 0].reshape(tok_rows, heads_here)
    leaf_out = back_out[leaf_owner, 1].reshape(tok_rows, heads_here, head_dim)
    leaf_lse = back_lse[leaf_owner, 1].reshape(tok_rows, heads_here)
    stacked_lse = jnp.stack([root_lse, mid_lse, leaf_lse, self_lse])
    stacked_out = jnp.stack([root_out, mid_out, leaf_out, self_out])
    overall = jnp.max(stacked_lse, axis=0)
    shares = jnp.exp(stacked_lse - overall)
    combined = jnp.sum(shares[..., None] * stacked_out, axis=0) / jnp.sum(shares, axis=0)[..., None]
    attended = combined.reshape(tok_rows, local_width).astype(jnp.bfloat16)
    projected = jnp.dot(attended, w_out, preferred_element_type=jnp.float32)
    rows_here = tok_rows // lax.axis_size("mp")
    first = lax.axis_index("mp") * rows_here
    attn_rows = mp_sum_scatter(projected.astype(jnp.bfloat16), 0)
    resid = lax.dynamic_slice_in_dim(hidden_in, first, rows_here, 0).astype(jnp.float32) + attn_rows
    ffn_rows = rms_scale(resid, ffn_gain).astype(jnp.bfloat16)
    ffn_in = mp_gather(ffn_rows, 1)
    logits = jnp.dot(ffn_in.astype(jnp.float32), w_router, precision=lax.Precision.HIGHEST)
    chosen = jnp.take_along_axis(logits, routes, axis=1)
    squashed = jax.nn.sigmoid(chosen)
    gates = squashed / jnp.sum(squashed, axis=1, keepdims=True)
    expert = lax.axis_index("mp")
    hit_each = routes == expert
    hit = jnp.any(hit_each, axis=1)
    gate_here = jnp.sum(jnp.where(hit_each, gates, 0.0), axis=1)
    order = jnp.cumsum(hit.astype(jnp.int32)) - 1
    capacity = 3 * TOP * tok_rows // (2 * lax.axis_size("mp"))
    slot_ids = jnp.arange(capacity, dtype=jnp.int32)
    pick_slot = (order[None, :] == slot_ids[:, None]) & hit[None, :]
    dispatch = jnp.dot(
        pick_slot.astype(jnp.bfloat16), ffn_in, preferred_element_type=jnp.float32
    ).astype(jnp.bfloat16)
    slot_gate = jnp.dot(pick_slot.astype(jnp.float32), gate_here, precision=lax.Precision.HIGHEST)
    gate_weight = w_gate[0]
    up_weight = w_up[0]
    down_weight = w_down[0]
    half = capacity // 2
    pieces = [
        lax.all_gather(dispatch[:half], "dp", axis=0, tiled=True),
        lax.all_gather(dispatch[half:], "dp", axis=0, tiled=True),
    ]
    outs = []
    for piece in pieces:
        gate_part = jnp.dot(piece, gate_weight, preferred_element_type=jnp.float32)
        up_part = jnp.dot(piece, up_weight, preferred_element_type=jnp.float32)
        partial_out = jnp.dot(
            (jax.nn.silu(gate_part) * up_part).astype(jnp.bfloat16),
            down_weight,
            preferred_element_type=jnp.float32,
        )
        outs.append(
            lax.psum_scatter(
                partial_out.astype(jnp.bfloat16), "dp", scatter_dimension=0, tiled=True
            )
        )
    expert_out = jnp.concatenate(outs, axis=0)
    weighted = expert_out.astype(jnp.float32) * slot_gate[:, None]
    spread = jnp.dot(pick_slot.astype(jnp.float32).T, weighted, precision=lax.Precision.HIGHEST)
    mixed = mp_sum_scatter(spread.astype(jnp.bfloat16), 2)
    row_ids = first + jnp.arange(rows_here, dtype=jnp.int32)
    valid = row_ids % suffix < suffix_len[row_ids // suffix]
    return jnp.where(valid[:, None], resid + mixed, 0.0).astype(jnp.bfloat16)


def solution(mesh):
    return jax.shard_map(
        on_device,
        mesh=mesh,
        in_specs=(
            P("dp", None),
            P(),
            P(None, "mp"),
            P(None, "mp"),
            P(None, "mp"),
            P("mp", None),
            P(None, "dp", "mp"),
            P(None, "dp", None, "mp"),
            P(None, "dp", None, "mp"),
            P("dp"),
            P("dp"),
            P("dp"),
            P(),
            P("dp"),
            P(),
            P(),
            P("dp", None),
            P("mp", None, "dp"),
            P("mp", None, "dp"),
            P("mp", "dp", None),
        ),
        out_specs=P(("dp", "mp"), None),
        check_vma=False,
    )
```

```python
import math

import jax
import jax.numpy as jnp
from jax import lax
import functools

from jax.experimental import pallas as pl
from jax.experimental.pallas import tpu as pltpu
from jax.sharding import Mesh, PartitionSpec as P

DP = ("y", "z")

MESH = pl.DeviceIdType.MESH


def _greet(n, me, dp):
    barrier = pltpu.get_barrier_semaphore()
    for k in range(1, n):
        pl.semaphore_signal(barrier, 1, device_id=(*dp, (me + k) % n), device_id_type=MESH)
    pl.semaphore_wait(barrier, n - 1)


def _mp_sum_kernel(n, x_ref, o_ref, recv, send_sem, recv_sem):
    me = lax.axis_index("mp")
    dp = (lax.axis_index("y"), lax.axis_index("z"))
    rows = o_ref.shape[0]
    _greet(n, me, dp)
    copies = []
    for k in range(1, n):
        peer = (me + k) % n
        copy = pltpu.make_async_remote_copy(
            src_ref=x_ref.at[pl.ds(pl.multiple_of(peer * rows, rows), rows)],
            dst_ref=recv.at[k],
            send_sem=send_sem.at[k],
            recv_sem=recv_sem.at[k],
            device_id=(*dp, peer),
            device_id_type=MESH,
        )
        copy.start()
        copies.append(copy)
    for copy in copies:
        copy.wait()
    total = x_ref[pl.ds(pl.multiple_of(me * rows, rows), rows), :].astype(jnp.float32)
    for k in range(1, n):
        total = total + recv[k].astype(jnp.float32)
    o_ref[...] = total


def mp_sum_scatter(x, collective_id):
    n = lax.axis_size("mp")
    rows = x.shape[0] // n
    cols = x.shape[1]
    return pl.pallas_call(
        functools.partial(_mp_sum_kernel, n),
        out_shape=jax.ShapeDtypeStruct((rows, cols), jnp.float32),
        in_specs=[pl.BlockSpec(memory_space=pltpu.VMEM)],
        out_specs=pl.BlockSpec(memory_space=pltpu.VMEM),
        scratch_shapes=[
            pltpu.VMEM((n, rows, cols), x.dtype),
            pltpu.SemaphoreType.DMA((n,)),
            pltpu.SemaphoreType.DMA((n,)),
        ],
        compiler_params=pltpu.CompilerParams(collective_id=collective_id, has_side_effects=True),
    )(x)


def _mp_gather_kernel(n, x_ref, o_ref, recv, send_sem, recv_sem):
    me = lax.axis_index("mp")
    dp = (lax.axis_index("y"), lax.axis_index("z"))
    rows = x_ref.shape[0]
    _greet(n, me, dp)
    copies = []
    for k in range(1, n):
        peer = (me + k) % n
        copy = pltpu.make_async_remote_copy(
            src_ref=x_ref,
            dst_ref=recv.at[k],
            send_sem=send_sem.at[k],
            recv_sem=recv_sem.at[k],
            device_id=(*dp, peer),
            device_id_type=MESH,
        )
        copy.start()
        copies.append(copy)
    for copy in copies:
        copy.wait()
    o_ref[pl.ds(pl.multiple_of(me * rows, rows), rows), :] = x_ref[...]
    for k in range(1, n):
        source = (me + n - k) % n
        o_ref[pl.ds(pl.multiple_of(source * rows, rows), rows), :] = recv[k]


def mp_gather(x, collective_id):
    n = lax.axis_size("mp")
    rows, cols = x.shape
    return pl.pallas_call(
        functools.partial(_mp_gather_kernel, n),
        out_shape=jax.ShapeDtypeStruct((n * rows, cols), x.dtype),
        in_specs=[pl.BlockSpec(memory_space=pltpu.VMEM)],
        out_specs=pl.BlockSpec(memory_space=pltpu.VMEM),
        scratch_shapes=[
            pltpu.VMEM((n, rows, cols), x.dtype),
            pltpu.SemaphoreType.DMA((n,)),
            pltpu.SemaphoreType.DMA((n,)),
        ],
        compiler_params=pltpu.CompilerParams(collective_id=collective_id, has_side_effects=True),
    )(x)


HD = 64
TOP = 2


EPS = 1e-05
NEGATIVE = -1e30


def rms_scale(rows, gain):
    rows_wide = rows.astype(jnp.float32)
    mean_square = jnp.mean(rows_wide * rows_wide, axis=-1, keepdims=True)
    return rows_wide * lax.rsqrt(mean_square + EPS) * gain


def level_partial(queries, node_keys, node_values, limits, heads_here, batched):
    senders, row_count, width = queries.shape
    head_dim = width // heads_here
    scale = 1.0 / math.sqrt(head_dim)
    query_heads = queries.reshape(senders, row_count, heads_here, head_dim)
    if batched:
        key_heads = node_keys.reshape(senders, -1, heads_here, head_dim)
        value_heads = node_values.reshape(senders, -1, heads_here, head_dim)
        scores = jnp.einsum(
            "sqhd,skhd->sqhk", query_heads, key_heads, preferred_element_type=jnp.float32
        )
    else:
        key_heads = node_keys.reshape(-1, heads_here, head_dim)
        value_heads = node_values.reshape(-1, heads_here, head_dim)
        scores = jnp.einsum(
            "sqhd,khd->sqhk", query_heads, key_heads, preferred_element_type=jnp.float32
        )
    scores = scores * scale
    slots = jnp.arange(scores.shape[-1], dtype=jnp.int32)
    allowed = slots[None, :] < limits[:, None]
    scores = jnp.where(allowed[:, None, None, :], scores, NEGATIVE)
    peak = jnp.max(scores, axis=-1)
    weights = jnp.exp(scores - peak[..., None])
    total = jnp.sum(weights, axis=-1)
    probs = weights.astype(jnp.bfloat16)
    if batched:
        summed = jnp.einsum(
            "sqhk,skhd->sqhd", probs, value_heads, preferred_element_type=jnp.float32
        )
    else:
        summed = jnp.einsum(
            "sqhk,khd->sqhd", probs, value_heads, preferred_element_type=jnp.float32
        )
    result = (summed / total[..., None]).reshape(senders, row_count, width)
    return (result, peak + jnp.log(total))


def on_device(
    hidden_in,
    attn_gain,
    w_query,
    w_key,
    w_value,
    w_out,
    root_cache,
    mid_cache,
    leaf_cache,
    mid_len,
    leaf_len,
    leaf_of,
    parents,
    suffix_len,
    ffn_gain,
    w_router,
    routes,
    w_gate,
    w_up,
    w_down,
):
    tok_rows, width = hidden_in.shape
    seq_rows = suffix_len.shape[0]
    suffix = tok_rows // seq_rows
    head_dim = HD
    local_width = w_query.shape[1]
    heads_here = local_width // head_dim
    scale = 1.0 / math.sqrt(head_dim)
    owners = lax.axis_size(DP)
    normed = rms_scale(hidden_in, attn_gain).astype(jnp.bfloat16)
    query = jnp.dot(normed, w_query, preferred_element_type=jnp.float32).astype(jnp.bfloat16)
    key = jnp.dot(normed, w_key, preferred_element_type=jnp.float32).astype(jnp.bfloat16)
    value = jnp.dot(normed, w_value, preferred_element_type=jnp.float32).astype(jnp.bfloat16)
    query_heads = query.reshape(tok_rows, heads_here, head_dim)
    piece = lax.all_gather(root_cache, DP, axis=1, tiled=True)
    running_peak = jnp.full((tok_rows, heads_here), NEGATIVE, jnp.float32)
    piece_keys = piece[0].reshape(-1, heads_here, head_dim)
    piece_values = piece[1].reshape(-1, heads_here, head_dim)
    scores = (
        jnp.einsum("qhd,khd->qhk", query_heads, piece_keys, preferred_element_type=jnp.float32)
        * scale
    )
    new_peak = jnp.maximum(running_peak, jnp.max(scores, axis=-1))
    weights = jnp.exp(scores - new_peak[..., None])
    new_total = jnp.sum(weights, axis=-1)
    added = jnp.einsum(
        "qhk,khd->qhd",
        weights.astype(jnp.bfloat16),
        piece_values,
        preferred_element_type=jnp.float32,
    )
    root_out = added / new_total[..., None]
    root_lse = new_peak + jnp.log(new_total)
    query_seq = query.reshape(seq_rows, suffix, heads_here, head_dim)
    key_seq = key.reshape(seq_rows, suffix, heads_here, head_dim)
    value_seq = value.reshape(seq_rows, suffix, heads_here, head_dim)
    slots = jnp.arange(suffix, dtype=jnp.int32)
    self_ok = (slots[None, None, :] <= slots[None, :, None]) & (
        slots[None, None, :] < suffix_len[:, None, None]
    )
    self_scores = (
        jnp.einsum("sqhd,skhd->sqhk", query_seq, key_seq, preferred_element_type=jnp.float32)
        * scale
    )
    self_scores = jnp.where(self_ok[:, :, None, :], self_scores, NEGATIVE)
    self_peak = jnp.max(self_scores, axis=-1)
    self_weights = jnp.exp(self_scores - self_peak[..., None])
    self_total = jnp.sum(self_weights, axis=-1)
    self_sum = jnp.einsum(
        "sqhk,skhd->sqhd",
        self_weights.astype(jnp.bfloat16),
        value_seq,
        preferred_element_type=jnp.float32,
    )
    self_out = (self_sum / self_total[..., None]).reshape(tok_rows, heads_here, head_dim)
    self_lse = (self_peak + jnp.log(self_total)).reshape(tok_rows, heads_here)
    mid_of = parents[leaf_of]
    leaf_owner = leaf_of // 2
    targets = jnp.arange(owners, dtype=jnp.int32)
    pick_mid = (mid_of[None, :] == targets[:, None]).astype(jnp.bfloat16)
    pick_leaf = (leaf_owner[None, :] == targets[:, None]).astype(jnp.bfloat16)
    flat_query = query.reshape(seq_rows, suffix * local_width)
    sent_mid = jnp.dot(pick_mid, flat_query, preferred_element_type=jnp.float32).astype(
        jnp.bfloat16
    )
    sent_leaf = jnp.dot(pick_leaf, flat_query, preferred_element_type=jnp.float32).astype(
        jnp.bfloat16
    )
    sent = jnp.stack([sent_mid, sent_leaf], axis=1).reshape(owners, 2, suffix, local_width)
    leaf_side = (leaf_of % 2).astype(jnp.float32)
    side_of_target = jnp.dot(
        pick_leaf.astype(jnp.float32), leaf_side, precision=lax.Precision.HIGHEST
    )
    side_rows = jnp.broadcast_to(side_of_target[:, None, None], (owners, 8, local_width))
    sent_all = jnp.concatenate(
        [sent.reshape(owners, 2 * suffix, local_width), side_rows.astype(jnp.bfloat16)], axis=1
    )
    got_all = lax.all_to_all(sent_all, DP, split_axis=0, concat_axis=0, tiled=True)
    sent_queries = got_all[:, : 2 * suffix].reshape(owners, 2, suffix, local_width)
    second = got_all[:, 2 * suffix, 0] > 0.5
    senders = sent_queries.shape[0]
    mid_limit = jnp.broadcast_to(mid_len[0], (senders,))
    mid_result, mid_logsum = level_partial(
        sent_queries[:, 0], mid_cache[0, 0], mid_cache[1, 0], mid_limit, heads_here, False
    )
    leaf_keys = jnp.where(second[:, None, None], leaf_cache[0, 1][None], leaf_cache[0, 0][None])
    leaf_values = jnp.where(second[:, None, None], leaf_cache[1, 1][None], leaf_cache[1, 0][None])
    leaf_limit = jnp.where(second, leaf_len[1], leaf_len[0])
    leaf_result, leaf_logsum = level_partial(
        sent_queries[:, 1], leaf_keys, leaf_values, leaf_limit, heads_here, True
    )
    owner_out = jnp.stack([mid_result, leaf_result], axis=1)
    owner_lse = jnp.stack([mid_logsum, leaf_logsum], axis=1)
    owner_all = jnp.concatenate([owner_out, owner_lse], axis=-1)
    back_all = lax.all_to_all(owner_all, DP, split_axis=0, concat_axis=0, tiled=True)
    back_out = back_all[..., :local_width]
    back_lse = back_all[..., local_width:]
    mid_out = back_out[mid_of, 0].reshape(tok_rows, heads_here, head_dim)
    mid_lse = back_lse[mid_of, 0].reshape(tok_rows, heads_here)
    leaf_out = back_out[leaf_owner, 1].reshape(tok_rows, heads_here, head_dim)
    leaf_lse = back_lse[leaf_owner, 1].reshape(tok_rows, heads_here)
    stacked_lse = jnp.stack([root_lse, mid_lse, leaf_lse, self_lse])
    stacked_out = jnp.stack([root_out, mid_out, leaf_out, self_out])
    overall = jnp.max(stacked_lse, axis=0)
    shares = jnp.exp(stacked_lse - overall)
    combined = jnp.sum(shares[..., None] * stacked_out, axis=0) / jnp.sum(shares, axis=0)[..., None]
    attended = combined.reshape(tok_rows, local_width).astype(jnp.bfloat16)
    projected = jnp.dot(attended, w_out, preferred_element_type=jnp.float32)
    rows_here = tok_rows // lax.axis_size("mp")
    first = lax.axis_index("mp") * rows_here
    attn_rows = mp_sum_scatter(projected.astype(jnp.bfloat16), 0)
    resid = lax.dynamic_slice_in_dim(hidden_in, first, rows_here, 0).astype(jnp.float32) + attn_rows
    ffn_rows = rms_scale(resid, ffn_gain).astype(jnp.bfloat16)
    ffn_in = mp_gather(ffn_rows, 1)
    logits = jnp.dot(ffn_in.astype(jnp.float32), w_router, precision=lax.Precision.HIGHEST)
    chosen = jnp.take_along_axis(logits, routes, axis=1)
    squashed = jax.nn.sigmoid(chosen)
    gates = squashed / jnp.sum(squashed, axis=1, keepdims=True)
    expert = lax.axis_index("mp")
    hit_each = routes == expert
    hit = jnp.any(hit_each, axis=1)
    gate_here = jnp.sum(jnp.where(hit_each, gates, 0.0), axis=1)
    order = jnp.cumsum(hit.astype(jnp.int32)) - 1
    capacity = 3 * TOP * tok_rows // (2 * lax.axis_size("mp"))
    slot_ids = jnp.arange(capacity, dtype=jnp.int32)
    pick_slot = (order[None, :] == slot_ids[:, None]) & hit[None, :]
    dispatch = jnp.dot(
        pick_slot.astype(jnp.bfloat16), ffn_in, preferred_element_type=jnp.float32
    ).astype(jnp.bfloat16)
    slot_gate = jnp.dot(pick_slot.astype(jnp.float32), gate_here, precision=lax.Precision.HIGHEST)
    gate_weight = w_gate[0]
    up_weight = w_up[0]
    down_weight = w_down[0]
    piece = lax.all_gather(
        lax.all_gather(dispatch, "z", axis=0, tiled=True), "y", axis=0, tiled=True
    )
    gate_part = jnp.dot(piece, gate_weight, preferred_element_type=jnp.float32)
    up_part = jnp.dot(piece, up_weight, preferred_element_type=jnp.float32)
    partial_out = jnp.dot(
        (jax.nn.silu(gate_part) * up_part).astype(jnp.bfloat16),
        down_weight,
        preferred_element_type=jnp.float32,
    )
    expert_out = lax.psum_scatter(
        lax.psum_scatter(partial_out.astype(jnp.bfloat16), "y", scatter_dimension=0, tiled=True),
        "z",
        scatter_dimension=0,
        tiled=True,
    )
    weighted = expert_out.astype(jnp.float32) * slot_gate[:, None]
    spread = jnp.dot(pick_slot.astype(jnp.float32).T, weighted, precision=lax.Precision.HIGHEST)
    mixed = mp_sum_scatter(spread.astype(jnp.bfloat16), 2)
    row_ids = first + jnp.arange(rows_here, dtype=jnp.int32)
    valid = row_ids % suffix < suffix_len[row_ids // suffix]
    return jnp.where(valid[:, None], resid + mixed, 0.0).astype(jnp.bfloat16)


def solution(mesh):
    return jax.shard_map(
        on_device,
        mesh=Mesh(mesh.devices.reshape(4, 4, -1), ("y", "z", "mp")),
        in_specs=(
            P(DP, None),
            P(),
            P(None, "mp"),
            P(None, "mp"),
            P(None, "mp"),
            P("mp", None),
            P(None, DP, "mp"),
            P(None, DP, None, "mp"),
            P(None, DP, None, "mp"),
            P(DP),
            P(DP),
            P(DP),
            P(),
            P(DP),
            P(),
            P(),
            P(DP, None),
            P("mp", None, DP),
            P("mp", None, DP),
            P("mp", DP, None),
        ),
        out_specs=P(("y", "z", "mp"), None),
        check_vma=False,
    )
```

```python
import math

import jax
import jax.numpy as jnp
from jax import lax
import functools

from jax.experimental import pallas as pl
from jax.experimental.pallas import tpu as pltpu
from jax.sharding import Mesh, PartitionSpec as P

DP = ("y", "z")

MESH = pl.DeviceIdType.MESH


def _greet(n, me, dp):
    barrier = pltpu.get_barrier_semaphore()
    for k in range(1, n):
        pl.semaphore_signal(barrier, 1, device_id=(*dp, (me + k) % n), device_id_type=MESH)
    pl.semaphore_wait(barrier, n - 1)


def _mp_sum_kernel(n, x_ref, o_ref, recv, send_sem, recv_sem):
    me = lax.axis_index("mp")
    dp = (lax.axis_index("y"), lax.axis_index("z"))
    rows = o_ref.shape[0]
    _greet(n, me, dp)
    copies = []
    for k in range(1, n):
        peer = (me + k) % n
        copy = pltpu.make_async_remote_copy(
            src_ref=x_ref.at[pl.ds(pl.multiple_of(peer * rows, rows), rows)],
            dst_ref=recv.at[k],
            send_sem=send_sem.at[k],
            recv_sem=recv_sem.at[k],
            device_id=(*dp, peer),
            device_id_type=MESH,
        )
        copy.start()
        copies.append(copy)
    for copy in copies:
        copy.wait()
    total = x_ref[pl.ds(pl.multiple_of(me * rows, rows), rows), :].astype(jnp.float32)
    for k in range(1, n):
        total = total + recv[k].astype(jnp.float32)
    o_ref[...] = total


def mp_sum_scatter(x, collective_id):
    n = lax.axis_size("mp")
    rows = x.shape[0] // n
    cols = x.shape[1]
    return pl.pallas_call(
        functools.partial(_mp_sum_kernel, n),
        out_shape=jax.ShapeDtypeStruct((rows, cols), jnp.float32),
        in_specs=[pl.BlockSpec(memory_space=pltpu.VMEM)],
        out_specs=pl.BlockSpec(memory_space=pltpu.VMEM),
        scratch_shapes=[
            pltpu.VMEM((n, rows, cols), x.dtype),
            pltpu.SemaphoreType.DMA((n,)),
            pltpu.SemaphoreType.DMA((n,)),
        ],
        compiler_params=pltpu.CompilerParams(collective_id=collective_id, has_side_effects=True),
    )(x)


def _mp_gather_kernel(n, x_ref, o_ref, recv, send_sem, recv_sem):
    me = lax.axis_index("mp")
    dp = (lax.axis_index("y"), lax.axis_index("z"))
    rows = x_ref.shape[0]
    _greet(n, me, dp)
    copies = []
    for k in range(1, n):
        peer = (me + k) % n
        copy = pltpu.make_async_remote_copy(
            src_ref=x_ref,
            dst_ref=recv.at[k],
            send_sem=send_sem.at[k],
            recv_sem=recv_sem.at[k],
            device_id=(*dp, peer),
            device_id_type=MESH,
        )
        copy.start()
        copies.append(copy)
    for copy in copies:
        copy.wait()
    o_ref[pl.ds(pl.multiple_of(me * rows, rows), rows), :] = x_ref[...]
    for k in range(1, n):
        source = (me + n - k) % n
        o_ref[pl.ds(pl.multiple_of(source * rows, rows), rows), :] = recv[k]


def mp_gather(x, collective_id):
    n = lax.axis_size("mp")
    rows, cols = x.shape
    return pl.pallas_call(
        functools.partial(_mp_gather_kernel, n),
        out_shape=jax.ShapeDtypeStruct((n * rows, cols), x.dtype),
        in_specs=[pl.BlockSpec(memory_space=pltpu.VMEM)],
        out_specs=pl.BlockSpec(memory_space=pltpu.VMEM),
        scratch_shapes=[
            pltpu.VMEM((n, rows, cols), x.dtype),
            pltpu.SemaphoreType.DMA((n,)),
            pltpu.SemaphoreType.DMA((n,)),
        ],
        compiler_params=pltpu.CompilerParams(collective_id=collective_id, has_side_effects=True),
    )(x)


HD = 64
TOP = 2


EPS = 1e-05
NEGATIVE = -1e30


def rms_scale(rows, gain):
    rows_wide = rows.astype(jnp.float32)
    mean_square = jnp.mean(rows_wide * rows_wide, axis=-1, keepdims=True)
    return rows_wide * lax.rsqrt(mean_square + EPS) * gain


def level_partial(queries, node_keys, node_values, limits, heads_here, batched):
    senders, row_count, width = queries.shape
    head_dim = width // heads_here
    scale = 1.0 / math.sqrt(head_dim)
    query_heads = queries.reshape(senders, row_count, heads_here, head_dim)
    if batched:
        key_heads = node_keys.reshape(senders, -1, heads_here, head_dim)
        value_heads = node_values.reshape(senders, -1, heads_here, head_dim)
        scores = jnp.einsum(
            "sqhd,skhd->sqhk", query_heads, key_heads, preferred_element_type=jnp.float32
        )
    else:
        key_heads = node_keys.reshape(-1, heads_here, head_dim)
        value_heads = node_values.reshape(-1, heads_here, head_dim)
        scores = jnp.einsum(
            "sqhd,khd->sqhk", query_heads, key_heads, preferred_element_type=jnp.float32
        )
    scores = scores * scale
    slots = jnp.arange(scores.shape[-1], dtype=jnp.int32)
    allowed = slots[None, :] < limits[:, None]
    scores = jnp.where(allowed[:, None, None, :], scores, NEGATIVE)
    peak = jnp.max(scores, axis=-1)
    weights = jnp.exp(scores - peak[..., None])
    total = jnp.sum(weights, axis=-1)
    probs = weights.astype(jnp.bfloat16)
    if batched:
        summed = jnp.einsum(
            "sqhk,skhd->sqhd", probs, value_heads, preferred_element_type=jnp.float32
        )
    else:
        summed = jnp.einsum(
            "sqhk,khd->sqhd", probs, value_heads, preferred_element_type=jnp.float32
        )
    result = (summed / total[..., None]).reshape(senders, row_count, width)
    return (result, peak + jnp.log(total))


def on_device(
    hidden_in,
    attn_gain,
    w_query,
    w_key,
    w_value,
    w_out,
    root_cache,
    mid_cache,
    leaf_cache,
    mid_len,
    leaf_len,
    leaf_of,
    parents,
    suffix_len,
    ffn_gain,
    w_router,
    routes,
    w_gate,
    w_up,
    w_down,
):
    tok_rows, width = hidden_in.shape
    seq_rows = suffix_len.shape[0]
    suffix = tok_rows // seq_rows
    head_dim = HD
    local_width = w_query.shape[1]
    heads_here = local_width // head_dim
    scale = 1.0 / math.sqrt(head_dim)
    owners = lax.axis_size(DP)
    normed = rms_scale(hidden_in, attn_gain).astype(jnp.bfloat16)
    query = jnp.dot(normed, w_query, preferred_element_type=jnp.float32).astype(jnp.bfloat16)
    key = jnp.dot(normed, w_key, preferred_element_type=jnp.float32).astype(jnp.bfloat16)
    value = jnp.dot(normed, w_value, preferred_element_type=jnp.float32).astype(jnp.bfloat16)
    query_heads = query.reshape(tok_rows, heads_here, head_dim)
    piece = lax.all_gather(root_cache, DP, axis=1, tiled=True)
    running_peak = jnp.full((tok_rows, heads_here), NEGATIVE, jnp.float32)
    piece_keys = piece[0].reshape(-1, heads_here, head_dim)
    piece_values = piece[1].reshape(-1, heads_here, head_dim)
    scores = (
        jnp.einsum("qhd,khd->qhk", query_heads, piece_keys, preferred_element_type=jnp.float32)
        * scale
    )
    new_peak = jnp.maximum(running_peak, jnp.max(scores, axis=-1))
    weights = jnp.exp(scores - new_peak[..., None])
    new_total = jnp.sum(weights, axis=-1)
    added = jnp.einsum(
        "qhk,khd->qhd",
        weights.astype(jnp.bfloat16),
        piece_values,
        preferred_element_type=jnp.float32,
    )
    root_out = added / new_total[..., None]
    root_lse = new_peak + jnp.log(new_total)
    query_seq = query.reshape(seq_rows, suffix, heads_here, head_dim)
    key_seq = key.reshape(seq_rows, suffix, heads_here, head_dim)
    value_seq = value.reshape(seq_rows, suffix, heads_here, head_dim)
    slots = jnp.arange(suffix, dtype=jnp.int32)
    self_ok = (slots[None, None, :] <= slots[None, :, None]) & (
        slots[None, None, :] < suffix_len[:, None, None]
    )
    self_scores = (
        jnp.einsum("sqhd,skhd->sqhk", query_seq, key_seq, preferred_element_type=jnp.float32)
        * scale
    )
    self_scores = jnp.where(self_ok[:, :, None, :], self_scores, NEGATIVE)
    self_peak = jnp.max(self_scores, axis=-1)
    self_weights = jnp.exp(self_scores - self_peak[..., None])
    self_total = jnp.sum(self_weights, axis=-1)
    self_sum = jnp.einsum(
        "sqhk,skhd->sqhd",
        self_weights.astype(jnp.bfloat16),
        value_seq,
        preferred_element_type=jnp.float32,
    )
    self_out = (self_sum / self_total[..., None]).reshape(tok_rows, heads_here, head_dim)
    self_lse = (self_peak + jnp.log(self_total)).reshape(tok_rows, heads_here)
    mid_of = parents[leaf_of]
    leaf_owner = leaf_of // 2
    targets = jnp.arange(owners, dtype=jnp.int32)
    pick_mid = (mid_of[None, :] == targets[:, None]).astype(jnp.bfloat16)
    pick_leaf = (leaf_owner[None, :] == targets[:, None]).astype(jnp.bfloat16)
    flat_query = query.reshape(seq_rows, suffix * local_width)
    sent_mid = jnp.dot(pick_mid, flat_query, preferred_element_type=jnp.float32).astype(
        jnp.bfloat16
    )
    sent_leaf = jnp.dot(pick_leaf, flat_query, preferred_element_type=jnp.float32).astype(
        jnp.bfloat16
    )
    sent = jnp.stack([sent_mid, sent_leaf], axis=1).reshape(owners, 2, suffix, local_width)
    leaf_side = (leaf_of % 2).astype(jnp.float32)
    side_of_target = jnp.dot(
        pick_leaf.astype(jnp.float32), leaf_side, precision=lax.Precision.HIGHEST
    )
    side_rows = jnp.broadcast_to(side_of_target[:, None, None], (owners, 8, local_width))
    sent_all = jnp.concatenate(
        [sent.reshape(owners, 2 * suffix, local_width), side_rows.astype(jnp.bfloat16)], axis=1
    )
    got_all = lax.all_to_all(sent_all, DP, split_axis=0, concat_axis=0, tiled=True)
    sent_queries = got_all[:, : 2 * suffix].reshape(owners, 2, suffix, local_width)
    second = got_all[:, 2 * suffix, 0] > 0.5
    senders = sent_queries.shape[0]
    mid_limit = jnp.broadcast_to(mid_len[0], (senders,))
    mid_result, mid_logsum = level_partial(
        sent_queries[:, 0], mid_cache[0, 0], mid_cache[1, 0], mid_limit, heads_here, False
    )
    leaf_keys = jnp.where(second[:, None, None], leaf_cache[0, 1][None], leaf_cache[0, 0][None])
    leaf_values = jnp.where(second[:, None, None], leaf_cache[1, 1][None], leaf_cache[1, 0][None])
    leaf_limit = jnp.where(second, leaf_len[1], leaf_len[0])
    leaf_result, leaf_logsum = level_partial(
        sent_queries[:, 1], leaf_keys, leaf_values, leaf_limit, heads_here, True
    )
    owner_out = jnp.stack([mid_result, leaf_result], axis=1)
    owner_lse = jnp.stack([mid_logsum, leaf_logsum], axis=1)
    owner_all = jnp.concatenate([owner_out, owner_lse], axis=-1)
    back_all = lax.all_to_all(owner_all, DP, split_axis=0, concat_axis=0, tiled=True)
    back_out = back_all[..., :local_width]
    back_lse = back_all[..., local_width:]
    mid_out = back_out[mid_of, 0].reshape(tok_rows, heads_here, head_dim)
    mid_lse = back_lse[mid_of, 0].reshape(tok_rows, heads_here)
    leaf_out = back_out[leaf_owner, 1].reshape(tok_rows, heads_here, head_dim)
    leaf_lse = back_lse[leaf_owner, 1].reshape(tok_rows, heads_here)
    stacked_lse = jnp.stack([root_lse, mid_lse, leaf_lse, self_lse])
    stacked_out = jnp.stack([root_out, mid_out, leaf_out, self_out])
    overall = jnp.max(stacked_lse, axis=0)
    shares = jnp.exp(stacked_lse - overall)
    combined = jnp.sum(shares[..., None] * stacked_out, axis=0) / jnp.sum(shares, axis=0)[..., None]
    attended = combined.reshape(tok_rows, local_width).astype(jnp.bfloat16)
    unit_weights = lax.all_gather(
        jnp.stack([w_gate[0], w_up[0], w_down[0].T]), "z", axis=0, tiled=False
    )
    projected = jnp.dot(attended, w_out, preferred_element_type=jnp.float32)
    unit_weights, projected = lax.optimization_barrier((unit_weights, projected))
    rows_here = tok_rows // lax.axis_size("mp")
    first = lax.axis_index("mp") * rows_here
    attn_rows = mp_sum_scatter(projected.astype(jnp.bfloat16), 0)
    resid = lax.dynamic_slice_in_dim(hidden_in, first, rows_here, 0).astype(jnp.float32) + attn_rows
    ffn_rows = rms_scale(resid, ffn_gain).astype(jnp.bfloat16)
    ffn_in = mp_gather(ffn_rows, 1)
    logits = jnp.dot(ffn_in.astype(jnp.float32), w_router, precision=lax.Precision.HIGHEST)
    chosen = jnp.take_along_axis(logits, routes, axis=1)
    squashed = jax.nn.sigmoid(chosen)
    gates = squashed / jnp.sum(squashed, axis=1, keepdims=True)
    expert = lax.axis_index("mp")
    hit_each = routes == expert
    hit = jnp.any(hit_each, axis=1)
    gate_here = jnp.sum(jnp.where(hit_each, gates, 0.0), axis=1)
    order = jnp.cumsum(hit.astype(jnp.int32)) - 1
    capacity = 3 * TOP * tok_rows // (2 * lax.axis_size("mp"))
    slot_ids = jnp.arange(capacity, dtype=jnp.int32)
    pick_slot = (order[None, :] == slot_ids[:, None]) & hit[None, :]
    dispatch = jnp.dot(
        pick_slot.astype(jnp.bfloat16), ffn_in, preferred_element_type=jnp.float32
    ).astype(jnp.bfloat16)
    slot_gate = jnp.dot(pick_slot.astype(jnp.float32), gate_here, precision=lax.Precision.HIGHEST)
    piece = lax.all_gather(dispatch, "y", axis=0, tiled=True)
    gate_part = jnp.einsum(
        "td,zdu->tzu", piece, unit_weights[:, 0], preferred_element_type=jnp.float32
    )
    up_part = jnp.einsum(
        "td,zdu->tzu", piece, unit_weights[:, 1], preferred_element_type=jnp.float32
    )
    partial_out = jnp.einsum(
        "tzu,zdu->td",
        (jax.nn.silu(gate_part) * up_part).astype(jnp.bfloat16),
        unit_weights[:, 2],
        preferred_element_type=jnp.float32,
    )
    expert_out = lax.psum_scatter(
        partial_out.astype(jnp.bfloat16), "y", scatter_dimension=0, tiled=True
    )
    weighted = expert_out.astype(jnp.float32) * slot_gate[:, None]
    spread = jnp.dot(pick_slot.astype(jnp.float32).T, weighted, precision=lax.Precision.HIGHEST)
    mixed = mp_sum_scatter(spread.astype(jnp.bfloat16), 2)
    row_ids = first + jnp.arange(rows_here, dtype=jnp.int32)
    valid = row_ids % suffix < suffix_len[row_ids // suffix]
    return jnp.where(valid[:, None], resid + mixed, 0.0).astype(jnp.bfloat16)


def solution(mesh):
    return jax.shard_map(
        on_device,
        mesh=Mesh(mesh.devices.reshape(4, 4, -1), ("y", "z", "mp")),
        in_specs=(
            P(DP, None),
            P(),
            P(None, "mp"),
            P(None, "mp"),
            P(None, "mp"),
            P("mp", None),
            P(None, DP, "mp"),
            P(None, DP, None, "mp"),
            P(None, DP, None, "mp"),
            P(DP),
            P(DP),
            P(DP),
            P(),
            P(DP),
            P(),
            P(),
            P(DP, None),
            P("mp", None, DP),
            P("mp", None, DP),
            P("mp", DP, None),
        ),
        out_specs=P(("y", "z", "mp"), None),
        check_vma=False,
    )
```

```python
import math

import jax
import jax.numpy as jnp
from jax import lax
import functools

from jax.experimental import pallas as pl
from jax.experimental.pallas import tpu as pltpu
from jax.sharding import Mesh, PartitionSpec as P

DP = ("y", "zh", "zl")
TOKEN_GROUP = ("y", "zh")

MESH = pl.DeviceIdType.MESH


def _greet(n, me, dp):
    barrier = pltpu.get_barrier_semaphore()
    for k in range(1, n):
        pl.semaphore_signal(barrier, 1, device_id=(*dp, (me + k) % n), device_id_type=MESH)
    pl.semaphore_wait(barrier, n - 1)


def _mp_sum_kernel(n, x_ref, o_ref, recv, send_sem, recv_sem):
    me = lax.axis_index("mp")
    dp = tuple(lax.axis_index(name) for name in DP)
    rows = o_ref.shape[0]
    _greet(n, me, dp)
    copies = []
    for k in range(1, n):
        peer = (me + k) % n
        copy = pltpu.make_async_remote_copy(
            src_ref=x_ref.at[pl.ds(pl.multiple_of(peer * rows, rows), rows)],
            dst_ref=recv.at[k],
            send_sem=send_sem.at[k],
            recv_sem=recv_sem.at[k],
            device_id=(*dp, peer),
            device_id_type=MESH,
        )
        copy.start()
        copies.append(copy)
    for copy in copies:
        copy.wait()
    total = x_ref[pl.ds(pl.multiple_of(me * rows, rows), rows), :].astype(jnp.float32)
    for k in range(1, n):
        total = total + recv[k].astype(jnp.float32)
    o_ref[...] = total


def mp_sum_scatter(x, collective_id):
    n = lax.axis_size("mp")
    rows = x.shape[0] // n
    cols = x.shape[1]
    return pl.pallas_call(
        functools.partial(_mp_sum_kernel, n),
        out_shape=jax.ShapeDtypeStruct((rows, cols), jnp.float32),
        in_specs=[pl.BlockSpec(memory_space=pltpu.VMEM)],
        out_specs=pl.BlockSpec(memory_space=pltpu.VMEM),
        scratch_shapes=[
            pltpu.VMEM((n, rows, cols), x.dtype),
            pltpu.SemaphoreType.DMA((n,)),
            pltpu.SemaphoreType.DMA((n,)),
        ],
        compiler_params=pltpu.CompilerParams(collective_id=collective_id, has_side_effects=True),
    )(x)


def _mp_gather_kernel(n, x_ref, o_ref, recv, send_sem, recv_sem):
    me = lax.axis_index("mp")
    dp = tuple(lax.axis_index(name) for name in DP)
    rows = x_ref.shape[0]
    _greet(n, me, dp)
    copies = []
    for k in range(1, n):
        peer = (me + k) % n
        copy = pltpu.make_async_remote_copy(
            src_ref=x_ref,
            dst_ref=recv.at[k],
            send_sem=send_sem.at[k],
            recv_sem=recv_sem.at[k],
            device_id=(*dp, peer),
            device_id_type=MESH,
        )
        copy.start()
        copies.append(copy)
    for copy in copies:
        copy.wait()
    o_ref[pl.ds(pl.multiple_of(me * rows, rows), rows), :] = x_ref[...]
    for k in range(1, n):
        source = (me + n - k) % n
        o_ref[pl.ds(pl.multiple_of(source * rows, rows), rows), :] = recv[k]


def mp_gather(x, collective_id):
    n = lax.axis_size("mp")
    rows, cols = x.shape
    return pl.pallas_call(
        functools.partial(_mp_gather_kernel, n),
        out_shape=jax.ShapeDtypeStruct((n * rows, cols), x.dtype),
        in_specs=[pl.BlockSpec(memory_space=pltpu.VMEM)],
        out_specs=pl.BlockSpec(memory_space=pltpu.VMEM),
        scratch_shapes=[
            pltpu.VMEM((n, rows, cols), x.dtype),
            pltpu.SemaphoreType.DMA((n,)),
            pltpu.SemaphoreType.DMA((n,)),
        ],
        compiler_params=pltpu.CompilerParams(collective_id=collective_id, has_side_effects=True),
    )(x)


HD = 64
TOP = 2


EPS = 1e-05
NEGATIVE = -1e30


def rms_scale(rows, gain):
    rows_wide = rows.astype(jnp.float32)
    mean_square = jnp.mean(rows_wide * rows_wide, axis=-1, keepdims=True)
    return rows_wide * lax.rsqrt(mean_square + EPS) * gain


def level_partial(queries, node_keys, node_values, limits, heads_here, batched):
    senders, row_count, width = queries.shape
    head_dim = width // heads_here
    scale = 1.0 / math.sqrt(head_dim)
    query_heads = queries.reshape(senders, row_count, heads_here, head_dim)
    if batched:
        key_heads = node_keys.reshape(senders, -1, heads_here, head_dim)
        value_heads = node_values.reshape(senders, -1, heads_here, head_dim)
        scores = jnp.einsum(
            "sqhd,skhd->sqhk", query_heads, key_heads, preferred_element_type=jnp.float32
        )
    else:
        key_heads = node_keys.reshape(-1, heads_here, head_dim)
        value_heads = node_values.reshape(-1, heads_here, head_dim)
        scores = jnp.einsum(
            "sqhd,khd->sqhk", query_heads, key_heads, preferred_element_type=jnp.float32
        )
    scores = scores * scale
    slots = jnp.arange(scores.shape[-1], dtype=jnp.int32)
    allowed = slots[None, :] < limits[:, None]
    scores = jnp.where(allowed[:, None, None, :], scores, NEGATIVE)
    peak = jnp.max(scores, axis=-1)
    weights = jnp.exp(scores - peak[..., None])
    total = jnp.sum(weights, axis=-1)
    probs = weights.astype(jnp.bfloat16)
    if batched:
        summed = jnp.einsum(
            "sqhk,skhd->sqhd", probs, value_heads, preferred_element_type=jnp.float32
        )
    else:
        summed = jnp.einsum(
            "sqhk,khd->sqhd", probs, value_heads, preferred_element_type=jnp.float32
        )
    result = (summed / total[..., None]).reshape(senders, row_count, width)
    return (result, peak + jnp.log(total))


def on_device(
    hidden_in,
    attn_gain,
    w_query,
    w_key,
    w_value,
    w_out,
    root_cache,
    mid_cache,
    leaf_cache,
    mid_len,
    leaf_len,
    leaf_of,
    parents,
    suffix_len,
    ffn_gain,
    w_router,
    routes,
    w_gate,
    w_up,
    w_down,
):
    tok_rows, width = hidden_in.shape
    seq_rows = suffix_len.shape[0]
    suffix = tok_rows // seq_rows
    head_dim = HD
    local_width = w_query.shape[1]
    heads_here = local_width // head_dim
    scale = 1.0 / math.sqrt(head_dim)
    owners = lax.axis_size(DP)
    normed = rms_scale(hidden_in, attn_gain).astype(jnp.bfloat16)
    query = jnp.dot(normed, w_query, preferred_element_type=jnp.float32).astype(jnp.bfloat16)
    key = jnp.dot(normed, w_key, preferred_element_type=jnp.float32).astype(jnp.bfloat16)
    value = jnp.dot(normed, w_value, preferred_element_type=jnp.float32).astype(jnp.bfloat16)
    query_heads = query.reshape(tok_rows, heads_here, head_dim)
    piece = lax.all_gather(root_cache, DP, axis=1, tiled=True)
    running_peak = jnp.full((tok_rows, heads_here), NEGATIVE, jnp.float32)
    piece_keys = piece[0].reshape(-1, heads_here, head_dim)
    piece_values = piece[1].reshape(-1, heads_here, head_dim)
    scores = (
        jnp.einsum("qhd,khd->qhk", query_heads, piece_keys, preferred_element_type=jnp.float32)
        * scale
    )
    new_peak = jnp.maximum(running_peak, jnp.max(scores, axis=-1))
    weights = jnp.exp(scores - new_peak[..., None])
    new_total = jnp.sum(weights, axis=-1)
    added = jnp.einsum(
        "qhk,khd->qhd",
        weights.astype(jnp.bfloat16),
        piece_values,
        preferred_element_type=jnp.float32,
    )
    root_out = added / new_total[..., None]
    root_lse = new_peak + jnp.log(new_total)
    query_seq = query.reshape(seq_rows, suffix, heads_here, head_dim)
    key_seq = key.reshape(seq_rows, suffix, heads_here, head_dim)
    value_seq = value.reshape(seq_rows, suffix, heads_here, head_dim)
    slots = jnp.arange(suffix, dtype=jnp.int32)
    self_ok = (slots[None, None, :] <= slots[None, :, None]) & (
        slots[None, None, :] < suffix_len[:, None, None]
    )
    self_scores = (
        jnp.einsum("sqhd,skhd->sqhk", query_seq, key_seq, preferred_element_type=jnp.float32)
        * scale
    )
    self_scores = jnp.where(self_ok[:, :, None, :], self_scores, NEGATIVE)
    self_peak = jnp.max(self_scores, axis=-1)
    self_weights = jnp.exp(self_scores - self_peak[..., None])
    self_total = jnp.sum(self_weights, axis=-1)
    self_sum = jnp.einsum(
        "sqhk,skhd->sqhd",
        self_weights.astype(jnp.bfloat16),
        value_seq,
        preferred_element_type=jnp.float32,
    )
    self_out = (self_sum / self_total[..., None]).reshape(tok_rows, heads_here, head_dim)
    self_lse = (self_peak + jnp.log(self_total)).reshape(tok_rows, heads_here)
    mid_of = parents[leaf_of]
    leaf_owner = leaf_of // 2
    targets = jnp.arange(owners, dtype=jnp.int32)
    pick_mid = (mid_of[None, :] == targets[:, None]).astype(jnp.bfloat16)
    pick_leaf = (leaf_owner[None, :] == targets[:, None]).astype(jnp.bfloat16)
    flat_query = query.reshape(seq_rows, suffix * local_width)
    sent_mid = jnp.dot(pick_mid, flat_query, preferred_element_type=jnp.float32).astype(
        jnp.bfloat16
    )
    sent_leaf = jnp.dot(pick_leaf, flat_query, preferred_element_type=jnp.float32).astype(
        jnp.bfloat16
    )
    sent = jnp.stack([sent_mid, sent_leaf], axis=1).reshape(owners, 2, suffix, local_width)
    leaf_side = (leaf_of % 2).astype(jnp.float32)
    side_of_target = jnp.dot(
        pick_leaf.astype(jnp.float32), leaf_side, precision=lax.Precision.HIGHEST
    )
    side_rows = jnp.broadcast_to(side_of_target[:, None, None], (owners, 8, local_width))
    sent_all = jnp.concatenate(
        [sent.reshape(owners, 2 * suffix, local_width), side_rows.astype(jnp.bfloat16)], axis=1
    )
    got_all = lax.all_to_all(sent_all, DP, split_axis=0, concat_axis=0, tiled=True)
    sent_queries = got_all[:, : 2 * suffix].reshape(owners, 2, suffix, local_width)
    second = got_all[:, 2 * suffix, 0] > 0.5
    senders = sent_queries.shape[0]
    mid_limit = jnp.broadcast_to(mid_len[0], (senders,))
    mid_result, mid_logsum = level_partial(
        sent_queries[:, 0], mid_cache[0, 0], mid_cache[1, 0], mid_limit, heads_here, False
    )
    leaf_keys = jnp.where(second[:, None, None], leaf_cache[0, 1][None], leaf_cache[0, 0][None])
    leaf_values = jnp.where(second[:, None, None], leaf_cache[1, 1][None], leaf_cache[1, 0][None])
    leaf_limit = jnp.where(second, leaf_len[1], leaf_len[0])
    leaf_result, leaf_logsum = level_partial(
        sent_queries[:, 1], leaf_keys, leaf_values, leaf_limit, heads_here, True
    )
    owner_out = jnp.stack([mid_result, leaf_result], axis=1)
    owner_lse = jnp.stack([mid_logsum, leaf_logsum], axis=1)
    owner_all = jnp.concatenate([owner_out, owner_lse], axis=-1)
    back_all = lax.all_to_all(owner_all, DP, split_axis=0, concat_axis=0, tiled=True)
    back_out = back_all[..., :local_width]
    back_lse = back_all[..., local_width:]
    mid_out = back_out[mid_of, 0].reshape(tok_rows, heads_here, head_dim)
    mid_lse = back_lse[mid_of, 0].reshape(tok_rows, heads_here)
    leaf_out = back_out[leaf_owner, 1].reshape(tok_rows, heads_here, head_dim)
    leaf_lse = back_lse[leaf_owner, 1].reshape(tok_rows, heads_here)
    stacked_lse = jnp.stack([root_lse, mid_lse, leaf_lse, self_lse])
    stacked_out = jnp.stack([root_out, mid_out, leaf_out, self_out])
    overall = jnp.max(stacked_lse, axis=0)
    shares = jnp.exp(stacked_lse - overall)
    combined = jnp.sum(shares[..., None] * stacked_out, axis=0) / jnp.sum(shares, axis=0)[..., None]
    attended = combined.reshape(tok_rows, local_width).astype(jnp.bfloat16)
    unit_weights = lax.all_gather(
        jnp.stack([w_gate[0], w_up[0], w_down[0].T]), "zl", axis=0, tiled=False
    )
    projected = jnp.dot(attended, w_out, preferred_element_type=jnp.float32)
    rows_here = tok_rows // lax.axis_size("mp")
    first = lax.axis_index("mp") * rows_here
    attn_rows = mp_sum_scatter(projected.astype(jnp.bfloat16), 0)
    resid = lax.dynamic_slice_in_dim(hidden_in, first, rows_here, 0).astype(jnp.float32) + attn_rows
    ffn_rows = rms_scale(resid, ffn_gain).astype(jnp.bfloat16)
    ffn_in = mp_gather(ffn_rows, 1)
    unit_weights, ffn_in = lax.optimization_barrier((unit_weights, ffn_in))
    logits = jnp.dot(ffn_in.astype(jnp.float32), w_router, precision=lax.Precision.HIGHEST)
    chosen = jnp.take_along_axis(logits, routes, axis=1)
    squashed = jax.nn.sigmoid(chosen)
    gates = squashed / jnp.sum(squashed, axis=1, keepdims=True)
    expert = lax.axis_index("mp")
    hit_each = routes == expert
    hit = jnp.any(hit_each, axis=1)
    gate_here = jnp.sum(jnp.where(hit_each, gates, 0.0), axis=1)
    order = jnp.cumsum(hit.astype(jnp.int32)) - 1
    capacity = 3 * TOP * tok_rows // (2 * lax.axis_size("mp"))
    slot_ids = jnp.arange(capacity, dtype=jnp.int32)
    pick_slot = (order[None, :] == slot_ids[:, None]) & hit[None, :]
    dispatch = jnp.dot(
        pick_slot.astype(jnp.bfloat16), ffn_in, preferred_element_type=jnp.float32
    ).astype(jnp.bfloat16)
    slot_gate = jnp.dot(pick_slot.astype(jnp.float32), gate_here, precision=lax.Precision.HIGHEST)
    piece = lax.all_gather(dispatch, TOKEN_GROUP, axis=0, tiled=True)
    gate_part = jnp.einsum(
        "td,zdu->tzu", piece, unit_weights[:, 0], preferred_element_type=jnp.float32
    )
    up_part = jnp.einsum(
        "td,zdu->tzu", piece, unit_weights[:, 1], preferred_element_type=jnp.float32
    )
    partial_out = jnp.einsum(
        "tzu,zdu->td",
        (jax.nn.silu(gate_part) * up_part).astype(jnp.bfloat16),
        unit_weights[:, 2],
        preferred_element_type=jnp.float32,
    )
    expert_out = lax.psum_scatter(
        partial_out.astype(jnp.bfloat16), TOKEN_GROUP, scatter_dimension=0, tiled=True
    )
    weighted = expert_out.astype(jnp.float32) * slot_gate[:, None]
    spread = jnp.dot(pick_slot.astype(jnp.float32).T, weighted, precision=lax.Precision.HIGHEST)
    mixed = mp_sum_scatter(spread.astype(jnp.bfloat16), 2)
    row_ids = first + jnp.arange(rows_here, dtype=jnp.int32)
    valid = row_ids % suffix < suffix_len[row_ids // suffix]
    return jnp.where(valid[:, None], resid + mixed, 0.0).astype(jnp.bfloat16)


def solution(mesh):
    return jax.shard_map(
        on_device,
        mesh=Mesh(mesh.devices.reshape(4, 2, 2, -1), (*DP, "mp")),
        in_specs=(
            P(DP, None),
            P(),
            P(None, "mp"),
            P(None, "mp"),
            P(None, "mp"),
            P("mp", None),
            P(None, DP, "mp"),
            P(None, DP, None, "mp"),
            P(None, DP, None, "mp"),
            P(DP),
            P(DP),
            P(DP),
            P(),
            P(DP),
            P(),
            P(),
            P(DP, None),
            P("mp", None, DP),
            P("mp", None, DP),
            P("mp", DP, None),
        ),
        out_specs=P((*DP, "mp"), None),
        check_vma=False,
    )
```

```python
import math

import jax
import jax.numpy as jnp
from jax import lax
import functools

from jax.experimental import pallas as pl
from jax.experimental.pallas import tpu as pltpu
from jax.sharding import Mesh, PartitionSpec as P

DP = ("y", "zh", "zl")
TOKEN_GROUP = ("y", "zl")

MESH = pl.DeviceIdType.MESH


def _greet(n, me, dp):
    barrier = pltpu.get_barrier_semaphore()
    for k in range(1, n):
        pl.semaphore_signal(barrier, 1, device_id=(*dp, (me + k) % n), device_id_type=MESH)
    pl.semaphore_wait(barrier, n - 1)


def _mp_sum_kernel(n, x_ref, o_ref, recv, send_sem, recv_sem):
    me = lax.axis_index("mp")
    dp = tuple(lax.axis_index(name) for name in DP)
    rows = o_ref.shape[0]
    _greet(n, me, dp)
    copies = []
    for k in range(1, n):
        peer = (me + k) % n
        copy = pltpu.make_async_remote_copy(
            src_ref=x_ref.at[pl.ds(pl.multiple_of(peer * rows, rows), rows)],
            dst_ref=recv.at[k],
            send_sem=send_sem.at[k],
            recv_sem=recv_sem.at[k],
            device_id=(*dp, peer),
            device_id_type=MESH,
        )
        copy.start()
        copies.append(copy)
    for copy in copies:
        copy.wait()
    total = x_ref[pl.ds(pl.multiple_of(me * rows, rows), rows), :].astype(jnp.float32)
    for k in range(1, n):
        total = total + recv[k].astype(jnp.float32)
    o_ref[...] = total


def mp_sum_scatter(x, collective_id):
    n = lax.axis_size("mp")
    rows = x.shape[0] // n
    cols = x.shape[1]
    return pl.pallas_call(
        functools.partial(_mp_sum_kernel, n),
        out_shape=jax.ShapeDtypeStruct((rows, cols), jnp.float32),
        in_specs=[pl.BlockSpec(memory_space=pltpu.VMEM)],
        out_specs=pl.BlockSpec(memory_space=pltpu.VMEM),
        scratch_shapes=[
            pltpu.VMEM((n, rows, cols), x.dtype),
            pltpu.SemaphoreType.DMA((n,)),
            pltpu.SemaphoreType.DMA((n,)),
        ],
        compiler_params=pltpu.CompilerParams(collective_id=collective_id, has_side_effects=True),
    )(x)


def _mp_gather_kernel(n, x_ref, o_ref, recv, send_sem, recv_sem):
    me = lax.axis_index("mp")
    dp = tuple(lax.axis_index(name) for name in DP)
    rows = x_ref.shape[0]
    _greet(n, me, dp)
    copies = []
    for k in range(1, n):
        peer = (me + k) % n
        copy = pltpu.make_async_remote_copy(
            src_ref=x_ref,
            dst_ref=recv.at[k],
            send_sem=send_sem.at[k],
            recv_sem=recv_sem.at[k],
            device_id=(*dp, peer),
            device_id_type=MESH,
        )
        copy.start()
        copies.append(copy)
    for copy in copies:
        copy.wait()
    o_ref[pl.ds(pl.multiple_of(me * rows, rows), rows), :] = x_ref[...]
    for k in range(1, n):
        source = (me + n - k) % n
        o_ref[pl.ds(pl.multiple_of(source * rows, rows), rows), :] = recv[k]


def mp_gather(x, collective_id):
    n = lax.axis_size("mp")
    rows, cols = x.shape
    return pl.pallas_call(
        functools.partial(_mp_gather_kernel, n),
        out_shape=jax.ShapeDtypeStruct((n * rows, cols), x.dtype),
        in_specs=[pl.BlockSpec(memory_space=pltpu.VMEM)],
        out_specs=pl.BlockSpec(memory_space=pltpu.VMEM),
        scratch_shapes=[
            pltpu.VMEM((n, rows, cols), x.dtype),
            pltpu.SemaphoreType.DMA((n,)),
            pltpu.SemaphoreType.DMA((n,)),
        ],
        compiler_params=pltpu.CompilerParams(collective_id=collective_id, has_side_effects=True),
    )(x)


HD = 64
TOP = 2


EPS = 1e-05
NEGATIVE = -1e30


def rms_scale(rows, gain):
    rows_wide = rows.astype(jnp.float32)
    mean_square = jnp.mean(rows_wide * rows_wide, axis=-1, keepdims=True)
    return rows_wide * lax.rsqrt(mean_square + EPS) * gain


def level_partial(queries, node_keys, node_values, limits, heads_here, batched):
    senders, row_count, width = queries.shape
    head_dim = width // heads_here
    scale = 1.0 / math.sqrt(head_dim)
    query_heads = queries.reshape(senders, row_count, heads_here, head_dim)
    if batched:
        key_heads = node_keys.reshape(senders, -1, heads_here, head_dim)
        value_heads = node_values.reshape(senders, -1, heads_here, head_dim)
        scores = jnp.einsum(
            "sqhd,skhd->sqhk", query_heads, key_heads, preferred_element_type=jnp.float32
        )
    else:
        key_heads = node_keys.reshape(-1, heads_here, head_dim)
        value_heads = node_values.reshape(-1, heads_here, head_dim)
        scores = jnp.einsum(
            "sqhd,khd->sqhk", query_heads, key_heads, preferred_element_type=jnp.float32
        )
    scores = scores * scale
    slots = jnp.arange(scores.shape[-1], dtype=jnp.int32)
    allowed = slots[None, :] < limits[:, None]
    scores = jnp.where(allowed[:, None, None, :], scores, NEGATIVE)
    peak = jnp.max(scores, axis=-1)
    weights = jnp.exp(scores - peak[..., None])
    total = jnp.sum(weights, axis=-1)
    probs = weights.astype(jnp.bfloat16)
    if batched:
        summed = jnp.einsum(
            "sqhk,skhd->sqhd", probs, value_heads, preferred_element_type=jnp.float32
        )
    else:
        summed = jnp.einsum(
            "sqhk,khd->sqhd", probs, value_heads, preferred_element_type=jnp.float32
        )
    result = (summed / total[..., None]).reshape(senders, row_count, width)
    return (result, peak + jnp.log(total))


def on_device(
    hidden_in,
    attn_gain,
    w_query,
    w_key,
    w_value,
    w_out,
    root_cache,
    mid_cache,
    leaf_cache,
    mid_len,
    leaf_len,
    leaf_of,
    parents,
    suffix_len,
    ffn_gain,
    w_router,
    routes,
    w_gate,
    w_up,
    w_down,
):
    tok_rows, width = hidden_in.shape
    seq_rows = suffix_len.shape[0]
    suffix = tok_rows // seq_rows
    head_dim = HD
    local_width = w_query.shape[1]
    heads_here = local_width // head_dim
    scale = 1.0 / math.sqrt(head_dim)
    owners = lax.axis_size(DP)
    normed = rms_scale(hidden_in, attn_gain).astype(jnp.bfloat16)
    query = jnp.dot(normed, w_query, preferred_element_type=jnp.float32).astype(jnp.bfloat16)
    key = jnp.dot(normed, w_key, preferred_element_type=jnp.float32).astype(jnp.bfloat16)
    value = jnp.dot(normed, w_value, preferred_element_type=jnp.float32).astype(jnp.bfloat16)
    query_heads = query.reshape(tok_rows, heads_here, head_dim)
    piece = lax.all_gather(root_cache, DP, axis=1, tiled=True)
    running_peak = jnp.full((tok_rows, heads_here), NEGATIVE, jnp.float32)
    piece_keys = piece[0].reshape(-1, heads_here, head_dim)
    piece_values = piece[1].reshape(-1, heads_here, head_dim)
    scores = (
        jnp.einsum("qhd,khd->qhk", query_heads, piece_keys, preferred_element_type=jnp.float32)
        * scale
    )
    new_peak = jnp.maximum(running_peak, jnp.max(scores, axis=-1))
    weights = jnp.exp(scores - new_peak[..., None])
    new_total = jnp.sum(weights, axis=-1)
    added = jnp.einsum(
        "qhk,khd->qhd",
        weights.astype(jnp.bfloat16),
        piece_values,
        preferred_element_type=jnp.float32,
    )
    root_out = added / new_total[..., None]
    root_lse = new_peak + jnp.log(new_total)
    query_seq = query.reshape(seq_rows, suffix, heads_here, head_dim)
    key_seq = key.reshape(seq_rows, suffix, heads_here, head_dim)
    value_seq = value.reshape(seq_rows, suffix, heads_here, head_dim)
    slots = jnp.arange(suffix, dtype=jnp.int32)
    self_ok = (slots[None, None, :] <= slots[None, :, None]) & (
        slots[None, None, :] < suffix_len[:, None, None]
    )
    self_scores = (
        jnp.einsum("sqhd,skhd->sqhk", query_seq, key_seq, preferred_element_type=jnp.float32)
        * scale
    )
    self_scores = jnp.where(self_ok[:, :, None, :], self_scores, NEGATIVE)
    self_peak = jnp.max(self_scores, axis=-1)
    self_weights = jnp.exp(self_scores - self_peak[..., None])
    self_total = jnp.sum(self_weights, axis=-1)
    self_sum = jnp.einsum(
        "sqhk,skhd->sqhd",
        self_weights.astype(jnp.bfloat16),
        value_seq,
        preferred_element_type=jnp.float32,
    )
    self_out = (self_sum / self_total[..., None]).reshape(tok_rows, heads_here, head_dim)
    self_lse = (self_peak + jnp.log(self_total)).reshape(tok_rows, heads_here)
    mid_of = parents[leaf_of]
    leaf_owner = leaf_of // 2
    targets = jnp.arange(owners, dtype=jnp.int32)
    pick_mid = (mid_of[None, :] == targets[:, None]).astype(jnp.bfloat16)
    pick_leaf = (leaf_owner[None, :] == targets[:, None]).astype(jnp.bfloat16)
    flat_query = query.reshape(seq_rows, suffix * local_width)
    sent_mid = jnp.dot(pick_mid, flat_query, preferred_element_type=jnp.float32).astype(
        jnp.bfloat16
    )
    sent_leaf = jnp.dot(pick_leaf, flat_query, preferred_element_type=jnp.float32).astype(
        jnp.bfloat16
    )
    sent = jnp.stack([sent_mid, sent_leaf], axis=1).reshape(owners, 2, suffix, local_width)
    leaf_side = (leaf_of % 2).astype(jnp.float32)
    side_of_target = jnp.dot(
        pick_leaf.astype(jnp.float32), leaf_side, precision=lax.Precision.HIGHEST
    )
    side_rows = jnp.broadcast_to(side_of_target[:, None, None], (owners, 8, local_width))
    sent_all = jnp.concatenate(
        [sent.reshape(owners, 2 * suffix, local_width), side_rows.astype(jnp.bfloat16)], axis=1
    )
    got_all = lax.all_to_all(sent_all, DP, split_axis=0, concat_axis=0, tiled=True)
    sent_queries = got_all[:, : 2 * suffix].reshape(owners, 2, suffix, local_width)
    second = got_all[:, 2 * suffix, 0] > 0.5
    senders = sent_queries.shape[0]
    mid_limit = jnp.broadcast_to(mid_len[0], (senders,))
    mid_result, mid_logsum = level_partial(
        sent_queries[:, 0], mid_cache[0, 0], mid_cache[1, 0], mid_limit, heads_here, False
    )
    leaf_keys = jnp.where(second[:, None, None], leaf_cache[0, 1][None], leaf_cache[0, 0][None])
    leaf_values = jnp.where(second[:, None, None], leaf_cache[1, 1][None], leaf_cache[1, 0][None])
    leaf_limit = jnp.where(second, leaf_len[1], leaf_len[0])
    leaf_result, leaf_logsum = level_partial(
        sent_queries[:, 1], leaf_keys, leaf_values, leaf_limit, heads_here, True
    )
    owner_out = jnp.stack([mid_result, leaf_result], axis=1)
    owner_lse = jnp.stack([mid_logsum, leaf_logsum], axis=1)
    owner_all = jnp.concatenate([owner_out, owner_lse], axis=-1)
    back_all = lax.all_to_all(owner_all, DP, split_axis=0, concat_axis=0, tiled=True)
    back_out = back_all[..., :local_width]
    back_lse = back_all[..., local_width:]
    mid_out = back_out[mid_of, 0].reshape(tok_rows, heads_here, head_dim)
    mid_lse = back_lse[mid_of, 0].reshape(tok_rows, heads_here)
    leaf_out = back_out[leaf_owner, 1].reshape(tok_rows, heads_here, head_dim)
    leaf_lse = back_lse[leaf_owner, 1].reshape(tok_rows, heads_here)
    stacked_lse = jnp.stack([root_lse, mid_lse, leaf_lse, self_lse])
    stacked_out = jnp.stack([root_out, mid_out, leaf_out, self_out])
    overall = jnp.max(stacked_lse, axis=0)
    shares = jnp.exp(stacked_lse - overall)
    combined = jnp.sum(shares[..., None] * stacked_out, axis=0) / jnp.sum(shares, axis=0)[..., None]
    attended = combined.reshape(tok_rows, local_width).astype(jnp.bfloat16)
    unit_weights = lax.all_gather(
        jnp.stack([w_gate[0], w_up[0], w_down[0].T]), "zh", axis=0, tiled=False
    )
    projected = jnp.dot(attended, w_out, preferred_element_type=jnp.float32)
    rows_here = tok_rows // lax.axis_size("mp")
    first = lax.axis_index("mp") * rows_here
    attn_rows = mp_sum_scatter(projected.astype(jnp.bfloat16), 0)
    resid = lax.dynamic_slice_in_dim(hidden_in, first, rows_here, 0).astype(jnp.float32) + attn_rows
    ffn_rows = rms_scale(resid, ffn_gain).astype(jnp.bfloat16)
    ffn_in = mp_gather(ffn_rows, 1)
    unit_weights, ffn_in = lax.optimization_barrier((unit_weights, ffn_in))
    logits = jnp.dot(ffn_in.astype(jnp.float32), w_router, precision=lax.Precision.HIGHEST)
    chosen = jnp.take_along_axis(logits, routes, axis=1)
    squashed = jax.nn.sigmoid(chosen)
    gates = squashed / jnp.sum(squashed, axis=1, keepdims=True)
    expert = lax.axis_index("mp")
    hit_each = routes == expert
    hit = jnp.any(hit_each, axis=1)
    gate_here = jnp.sum(jnp.where(hit_each, gates, 0.0), axis=1)
    order = jnp.cumsum(hit.astype(jnp.int32)) - 1
    capacity = 3 * TOP * tok_rows // (2 * lax.axis_size("mp"))
    slot_ids = jnp.arange(capacity, dtype=jnp.int32)
    pick_slot = (order[None, :] == slot_ids[:, None]) & hit[None, :]
    dispatch = jnp.dot(
        pick_slot.astype(jnp.bfloat16), ffn_in, preferred_element_type=jnp.float32
    ).astype(jnp.bfloat16)
    slot_gate = jnp.dot(pick_slot.astype(jnp.float32), gate_here, precision=lax.Precision.HIGHEST)
    piece = lax.all_gather(dispatch, TOKEN_GROUP, axis=0, tiled=True)
    gate_part = jnp.einsum(
        "td,zdu->tzu", piece, unit_weights[:, 0], preferred_element_type=jnp.float32
    )
    up_part = jnp.einsum(
        "td,zdu->tzu", piece, unit_weights[:, 1], preferred_element_type=jnp.float32
    )
    partial_out = jnp.einsum(
        "tzu,zdu->td",
        (jax.nn.silu(gate_part) * up_part).astype(jnp.bfloat16),
        unit_weights[:, 2],
        preferred_element_type=jnp.float32,
    )
    expert_out = lax.psum_scatter(
        partial_out.astype(jnp.bfloat16), TOKEN_GROUP, scatter_dimension=0, tiled=True
    )
    weighted = expert_out.astype(jnp.float32) * slot_gate[:, None]
    spread = jnp.dot(pick_slot.astype(jnp.float32).T, weighted, precision=lax.Precision.HIGHEST)
    mixed = mp_sum_scatter(spread.astype(jnp.bfloat16), 2)
    row_ids = first + jnp.arange(rows_here, dtype=jnp.int32)
    valid = row_ids % suffix < suffix_len[row_ids // suffix]
    return jnp.where(valid[:, None], resid + mixed, 0.0).astype(jnp.bfloat16)


def solution(mesh):
    return jax.shard_map(
        on_device,
        mesh=Mesh(mesh.devices.reshape(4, 2, 2, -1), (*DP, "mp")),
        in_specs=(
            P(DP, None),
            P(),
            P(None, "mp"),
            P(None, "mp"),
            P(None, "mp"),
            P("mp", None),
            P(None, DP, "mp"),
            P(None, DP, None, "mp"),
            P(None, DP, None, "mp"),
            P(DP),
            P(DP),
            P(DP),
            P(),
            P(DP),
            P(),
            P(),
            P(DP, None),
            P("mp", None, DP),
            P("mp", None, DP),
            P("mp", DP, None),
        ),
        out_specs=P((*DP, "mp"), None),
        check_vma=False,
    )
```

```python
import math

import jax
import jax.numpy as jnp
from jax import lax
import functools

from jax.experimental import pallas as pl
from jax.experimental.pallas import tpu as pltpu
from jax.sharding import Mesh, PartitionSpec as P

DP = ("y", "zh", "zl")

MESH = pl.DeviceIdType.MESH


def _greet(n, me, dp):
    barrier = pltpu.get_barrier_semaphore()
    for k in range(1, n):
        pl.semaphore_signal(barrier, 1, device_id=(*dp, (me + k) % n), device_id_type=MESH)
    pl.semaphore_wait(barrier, n - 1)


def _mp_sum_kernel(n, x_ref, o_ref, recv, send_sem, recv_sem):
    me = lax.axis_index("mp")
    dp = tuple(lax.axis_index(name) for name in DP)
    rows = o_ref.shape[0]
    _greet(n, me, dp)
    copies = []
    for k in range(1, n):
        peer = (me + k) % n
        copy = pltpu.make_async_remote_copy(
            src_ref=x_ref.at[pl.ds(pl.multiple_of(peer * rows, rows), rows)],
            dst_ref=recv.at[k],
            send_sem=send_sem.at[k],
            recv_sem=recv_sem.at[k],
            device_id=(*dp, peer),
            device_id_type=MESH,
        )
        copy.start()
        copies.append(copy)
    for copy in copies:
        copy.wait()
    total = x_ref[pl.ds(pl.multiple_of(me * rows, rows), rows), :].astype(jnp.float32)
    for k in range(1, n):
        total = total + recv[k].astype(jnp.float32)
    o_ref[...] = total


def mp_sum_scatter(x, collective_id):
    n = lax.axis_size("mp")
    rows = x.shape[0] // n
    cols = x.shape[1]
    return pl.pallas_call(
        functools.partial(_mp_sum_kernel, n),
        out_shape=jax.ShapeDtypeStruct((rows, cols), jnp.float32),
        in_specs=[pl.BlockSpec(memory_space=pltpu.VMEM)],
        out_specs=pl.BlockSpec(memory_space=pltpu.VMEM),
        scratch_shapes=[
            pltpu.VMEM((n, rows, cols), x.dtype),
            pltpu.SemaphoreType.DMA((n,)),
            pltpu.SemaphoreType.DMA((n,)),
        ],
        compiler_params=pltpu.CompilerParams(collective_id=collective_id, has_side_effects=True),
    )(x)


def _mp_gather_kernel(n, x_ref, o_ref, recv, send_sem, recv_sem):
    me = lax.axis_index("mp")
    dp = tuple(lax.axis_index(name) for name in DP)
    rows = x_ref.shape[0]
    _greet(n, me, dp)
    copies = []
    for k in range(1, n):
        peer = (me + k) % n
        copy = pltpu.make_async_remote_copy(
            src_ref=x_ref,
            dst_ref=recv.at[k],
            send_sem=send_sem.at[k],
            recv_sem=recv_sem.at[k],
            device_id=(*dp, peer),
            device_id_type=MESH,
        )
        copy.start()
        copies.append(copy)
    for copy in copies:
        copy.wait()
    o_ref[pl.ds(pl.multiple_of(me * rows, rows), rows), :] = x_ref[...]
    for k in range(1, n):
        source = (me + n - k) % n
        o_ref[pl.ds(pl.multiple_of(source * rows, rows), rows), :] = recv[k]


def mp_gather(x, collective_id):
    n = lax.axis_size("mp")
    rows, cols = x.shape
    return pl.pallas_call(
        functools.partial(_mp_gather_kernel, n),
        out_shape=jax.ShapeDtypeStruct((n * rows, cols), x.dtype),
        in_specs=[pl.BlockSpec(memory_space=pltpu.VMEM)],
        out_specs=pl.BlockSpec(memory_space=pltpu.VMEM),
        scratch_shapes=[
            pltpu.VMEM((n, rows, cols), x.dtype),
            pltpu.SemaphoreType.DMA((n,)),
            pltpu.SemaphoreType.DMA((n,)),
        ],
        compiler_params=pltpu.CompilerParams(collective_id=collective_id, has_side_effects=True),
    )(x)


HD = 64
TOP = 2


EPS = 1e-05
NEGATIVE = -1e30


def rms_scale(rows, gain):
    rows_wide = rows.astype(jnp.float32)
    mean_square = jnp.mean(rows_wide * rows_wide, axis=-1, keepdims=True)
    return rows_wide * lax.rsqrt(mean_square + EPS) * gain


def level_partial(queries, node_keys, node_values, limits, heads_here, batched):
    senders, row_count, width = queries.shape
    head_dim = width // heads_here
    scale = 1.0 / math.sqrt(head_dim)
    query_heads = queries.reshape(senders, row_count, heads_here, head_dim)
    if batched:
        key_heads = node_keys.reshape(senders, -1, heads_here, head_dim)
        value_heads = node_values.reshape(senders, -1, heads_here, head_dim)
        scores = jnp.einsum(
            "sqhd,skhd->sqhk", query_heads, key_heads, preferred_element_type=jnp.float32
        )
    else:
        key_heads = node_keys.reshape(-1, heads_here, head_dim)
        value_heads = node_values.reshape(-1, heads_here, head_dim)
        scores = jnp.einsum(
            "sqhd,khd->sqhk", query_heads, key_heads, preferred_element_type=jnp.float32
        )
    scores = scores * scale
    slots = jnp.arange(scores.shape[-1], dtype=jnp.int32)
    allowed = slots[None, :] < limits[:, None]
    scores = jnp.where(allowed[:, None, None, :], scores, NEGATIVE)
    peak = jnp.max(scores, axis=-1)
    weights = jnp.exp(scores - peak[..., None])
    total = jnp.sum(weights, axis=-1)
    probs = weights.astype(jnp.bfloat16)
    if batched:
        summed = jnp.einsum(
            "sqhk,skhd->sqhd", probs, value_heads, preferred_element_type=jnp.float32
        )
    else:
        summed = jnp.einsum(
            "sqhk,khd->sqhd", probs, value_heads, preferred_element_type=jnp.float32
        )
    result = (summed / total[..., None]).reshape(senders, row_count, width)
    return (result, peak + jnp.log(total))


def on_device(
    hidden_in,
    attn_gain,
    w_query,
    w_key,
    w_value,
    w_out,
    root_cache,
    mid_cache,
    leaf_cache,
    mid_len,
    leaf_len,
    leaf_of,
    parents,
    suffix_len,
    ffn_gain,
    w_router,
    routes,
    w_gate,
    w_up,
    w_down,
):
    tok_rows, width = hidden_in.shape
    seq_rows = suffix_len.shape[0]
    suffix = tok_rows // seq_rows
    head_dim = HD
    local_width = w_query.shape[1]
    heads_here = local_width // head_dim
    scale = 1.0 / math.sqrt(head_dim)
    owners = lax.axis_size(DP)
    normed = rms_scale(hidden_in, attn_gain).astype(jnp.bfloat16)
    query = jnp.dot(normed, w_query, preferred_element_type=jnp.float32).astype(jnp.bfloat16)
    key = jnp.dot(normed, w_key, preferred_element_type=jnp.float32).astype(jnp.bfloat16)
    value = jnp.dot(normed, w_value, preferred_element_type=jnp.float32).astype(jnp.bfloat16)
    query_heads = query.reshape(tok_rows, heads_here, head_dim)
    piece = lax.all_gather(root_cache, DP, axis=1, tiled=True)
    running_peak = jnp.full((tok_rows, heads_here), NEGATIVE, jnp.float32)
    piece_keys = piece[0].reshape(-1, heads_here, head_dim)
    piece_values = piece[1].reshape(-1, heads_here, head_dim)
    scores = (
        jnp.einsum("qhd,khd->qhk", query_heads, piece_keys, preferred_element_type=jnp.float32)
        * scale
    )
    new_peak = jnp.maximum(running_peak, jnp.max(scores, axis=-1))
    weights = jnp.exp(scores - new_peak[..., None])
    new_total = jnp.sum(weights, axis=-1)
    added = jnp.einsum(
        "qhk,khd->qhd",
        weights.astype(jnp.bfloat16),
        piece_values,
        preferred_element_type=jnp.float32,
    )
    root_out = added / new_total[..., None]
    root_lse = new_peak + jnp.log(new_total)
    query_seq = query.reshape(seq_rows, suffix, heads_here, head_dim)
    key_seq = key.reshape(seq_rows, suffix, heads_here, head_dim)
    value_seq = value.reshape(seq_rows, suffix, heads_here, head_dim)
    slots = jnp.arange(suffix, dtype=jnp.int32)
    self_ok = (slots[None, None, :] <= slots[None, :, None]) & (
        slots[None, None, :] < suffix_len[:, None, None]
    )
    self_scores = (
        jnp.einsum("sqhd,skhd->sqhk", query_seq, key_seq, preferred_element_type=jnp.float32)
        * scale
    )
    self_scores = jnp.where(self_ok[:, :, None, :], self_scores, NEGATIVE)
    self_peak = jnp.max(self_scores, axis=-1)
    self_weights = jnp.exp(self_scores - self_peak[..., None])
    self_total = jnp.sum(self_weights, axis=-1)
    self_sum = jnp.einsum(
        "sqhk,skhd->sqhd",
        self_weights.astype(jnp.bfloat16),
        value_seq,
        preferred_element_type=jnp.float32,
    )
    self_out = (self_sum / self_total[..., None]).reshape(tok_rows, heads_here, head_dim)
    self_lse = (self_peak + jnp.log(self_total)).reshape(tok_rows, heads_here)
    mid_of = parents[leaf_of]
    leaf_owner = leaf_of // 2
    targets = jnp.arange(owners, dtype=jnp.int32)
    pick_mid = (mid_of[None, :] == targets[:, None]).astype(jnp.bfloat16)
    pick_leaf = (leaf_owner[None, :] == targets[:, None]).astype(jnp.bfloat16)
    flat_query = query.reshape(seq_rows, suffix * local_width)
    sent_mid = jnp.dot(pick_mid, flat_query, preferred_element_type=jnp.float32).astype(
        jnp.bfloat16
    )
    sent_leaf = jnp.dot(pick_leaf, flat_query, preferred_element_type=jnp.float32).astype(
        jnp.bfloat16
    )
    sent = jnp.stack([sent_mid, sent_leaf], axis=1).reshape(owners, 2, suffix, local_width)
    leaf_side = (leaf_of % 2).astype(jnp.float32)
    side_of_target = jnp.dot(
        pick_leaf.astype(jnp.float32), leaf_side, precision=lax.Precision.HIGHEST
    )
    side_rows = jnp.broadcast_to(side_of_target[:, None, None], (owners, 8, local_width))
    sent_all = jnp.concatenate(
        [sent.reshape(owners, 2 * suffix, local_width), side_rows.astype(jnp.bfloat16)], axis=1
    )
    got_all = lax.all_to_all(sent_all, DP, split_axis=0, concat_axis=0, tiled=True)
    sent_queries = got_all[:, : 2 * suffix].reshape(owners, 2, suffix, local_width)
    second = got_all[:, 2 * suffix, 0] > 0.5
    senders = sent_queries.shape[0]
    mid_limit = jnp.broadcast_to(mid_len[0], (senders,))
    mid_result, mid_logsum = level_partial(
        sent_queries[:, 0], mid_cache[0, 0], mid_cache[1, 0], mid_limit, heads_here, False
    )
    leaf_keys = jnp.where(second[:, None, None], leaf_cache[0, 1][None], leaf_cache[0, 0][None])
    leaf_values = jnp.where(second[:, None, None], leaf_cache[1, 1][None], leaf_cache[1, 0][None])
    leaf_limit = jnp.where(second, leaf_len[1], leaf_len[0])
    leaf_result, leaf_logsum = level_partial(
        sent_queries[:, 1], leaf_keys, leaf_values, leaf_limit, heads_here, True
    )
    owner_out = jnp.stack([mid_result, leaf_result], axis=1)
    owner_lse = jnp.stack([mid_logsum, leaf_logsum], axis=1)
    owner_all = jnp.concatenate([owner_out, owner_lse], axis=-1)
    back_all = lax.all_to_all(owner_all, DP, split_axis=0, concat_axis=0, tiled=True)
    back_out = back_all[..., :local_width]
    back_lse = back_all[..., local_width:]
    mid_out = back_out[mid_of, 0].reshape(tok_rows, heads_here, head_dim)
    mid_lse = back_lse[mid_of, 0].reshape(tok_rows, heads_here)
    leaf_out = back_out[leaf_owner, 1].reshape(tok_rows, heads_here, head_dim)
    leaf_lse = back_lse[leaf_owner, 1].reshape(tok_rows, heads_here)
    stacked_lse = jnp.stack([root_lse, mid_lse, leaf_lse, self_lse])
    stacked_out = jnp.stack([root_out, mid_out, leaf_out, self_out])
    overall = jnp.max(stacked_lse, axis=0)
    shares = jnp.exp(stacked_lse - overall)
    combined = jnp.sum(shares[..., None] * stacked_out, axis=0) / jnp.sum(shares, axis=0)[..., None]
    attended = combined.reshape(tok_rows, local_width).astype(jnp.bfloat16)
    unit_weights = lax.all_gather(
        jnp.stack([w_gate[0], w_up[0], w_down[0].T]), "zl", axis=0, tiled=False
    )
    projected = jnp.dot(attended, w_out, preferred_element_type=jnp.float32)
    rows_here = tok_rows // lax.axis_size("mp")
    first = lax.axis_index("mp") * rows_here
    attn_rows = mp_sum_scatter(projected.astype(jnp.bfloat16), 0)
    resid = lax.dynamic_slice_in_dim(hidden_in, first, rows_here, 0).astype(jnp.float32) + attn_rows
    ffn_rows = rms_scale(resid, ffn_gain).astype(jnp.bfloat16)
    ffn_in = mp_gather(ffn_rows, 1)
    unit_weights, ffn_in = lax.optimization_barrier((unit_weights, ffn_in))
    logits = jnp.dot(ffn_in.astype(jnp.float32), w_router, precision=lax.Precision.HIGHEST)
    chosen = jnp.take_along_axis(logits, routes, axis=1)
    squashed = jax.nn.sigmoid(chosen)
    gates = squashed / jnp.sum(squashed, axis=1, keepdims=True)
    expert = lax.axis_index("mp")
    hit_each = routes == expert
    hit = jnp.any(hit_each, axis=1)
    gate_here = jnp.sum(jnp.where(hit_each, gates, 0.0), axis=1)
    order = jnp.cumsum(hit.astype(jnp.int32)) - 1
    capacity = 3 * TOP * tok_rows // (2 * lax.axis_size("mp"))
    slot_ids = jnp.arange(capacity, dtype=jnp.int32)
    pick_slot = (order[None, :] == slot_ids[:, None]) & hit[None, :]
    dispatch = jnp.dot(
        pick_slot.astype(jnp.bfloat16), ffn_in, preferred_element_type=jnp.float32
    ).astype(jnp.bfloat16)
    slot_gate = jnp.dot(pick_slot.astype(jnp.float32), gate_here, precision=lax.Precision.HIGHEST)
    piece = lax.all_gather(
        lax.all_gather(dispatch, "zh", axis=0, tiled=True), "y", axis=0, tiled=True
    )
    gate_part = jnp.einsum(
        "td,zdu->tzu", piece, unit_weights[:, 0], preferred_element_type=jnp.float32
    )
    up_part = jnp.einsum(
        "td,zdu->tzu", piece, unit_weights[:, 1], preferred_element_type=jnp.float32
    )
    partial_out = jnp.einsum(
        "tzu,zdu->td",
        (jax.nn.silu(gate_part) * up_part).astype(jnp.bfloat16),
        unit_weights[:, 2],
        preferred_element_type=jnp.float32,
    )
    expert_out = lax.psum_scatter(
        lax.psum_scatter(partial_out.astype(jnp.bfloat16), "y", scatter_dimension=0, tiled=True),
        "zh",
        scatter_dimension=0,
        tiled=True,
    )
    weighted = expert_out.astype(jnp.float32) * slot_gate[:, None]
    spread = jnp.dot(pick_slot.astype(jnp.float32).T, weighted, precision=lax.Precision.HIGHEST)
    mixed = mp_sum_scatter(spread.astype(jnp.bfloat16), 2)
    row_ids = first + jnp.arange(rows_here, dtype=jnp.int32)
    valid = row_ids % suffix < suffix_len[row_ids // suffix]
    return jnp.where(valid[:, None], resid + mixed, 0.0).astype(jnp.bfloat16)


def solution(mesh):
    return jax.shard_map(
        on_device,
        mesh=Mesh(mesh.devices.reshape(4, 2, 2, -1), (*DP, "mp")),
        in_specs=(
            P(DP, None),
            P(),
            P(None, "mp"),
            P(None, "mp"),
            P(None, "mp"),
            P("mp", None),
            P(None, DP, "mp"),
            P(None, DP, None, "mp"),
            P(None, DP, None, "mp"),
            P(DP),
            P(DP),
            P(DP),
            P(),
            P(DP),
            P(),
            P(),
            P(DP, None),
            P("mp", None, DP),
            P("mp", None, DP),
            P("mp", DP, None),
        ),
        out_specs=P((*DP, "mp"), None),
        check_vma=False,
    )
```

```python
import math

import jax
import jax.numpy as jnp
from jax import lax
import functools

from jax.experimental import pallas as pl
from jax.experimental.pallas import tpu as pltpu
from jax.sharding import Mesh, PartitionSpec as P

DP = ("y", "z")

MESH = pl.DeviceIdType.MESH


def _greet(n, me, dp):
    barrier = pltpu.get_barrier_semaphore()
    for k in range(1, n):
        pl.semaphore_signal(barrier, 1, device_id=(*dp, (me + k) % n), device_id_type=MESH)
    pl.semaphore_wait(barrier, n - 1)


def _mp_sum_kernel(n, x_ref, o_ref, recv, send_sem, recv_sem):
    me = lax.axis_index("mp")
    dp = (lax.axis_index("y"), lax.axis_index("z"))
    rows = o_ref.shape[0]
    _greet(n, me, dp)
    copies = []
    for k in range(1, n):
        peer = (me + k) % n
        copy = pltpu.make_async_remote_copy(
            src_ref=x_ref.at[pl.ds(pl.multiple_of(peer * rows, rows), rows)],
            dst_ref=recv.at[k],
            send_sem=send_sem.at[k],
            recv_sem=recv_sem.at[k],
            device_id=(*dp, peer),
            device_id_type=MESH,
        )
        copy.start()
        copies.append(copy)
    for copy in copies:
        copy.wait()
    total = x_ref[pl.ds(pl.multiple_of(me * rows, rows), rows), :].astype(jnp.float32)
    for k in range(1, n):
        total = total + recv[k].astype(jnp.float32)
    o_ref[...] = total


def mp_sum_scatter(x, collective_id):
    n = lax.axis_size("mp")
    rows = x.shape[0] // n
    cols = x.shape[1]
    return pl.pallas_call(
        functools.partial(_mp_sum_kernel, n),
        out_shape=jax.ShapeDtypeStruct((rows, cols), jnp.float32),
        in_specs=[pl.BlockSpec(memory_space=pltpu.VMEM)],
        out_specs=pl.BlockSpec(memory_space=pltpu.VMEM),
        scratch_shapes=[
            pltpu.VMEM((n, rows, cols), x.dtype),
            pltpu.SemaphoreType.DMA((n,)),
            pltpu.SemaphoreType.DMA((n,)),
        ],
        compiler_params=pltpu.CompilerParams(collective_id=collective_id, has_side_effects=True),
    )(x)


def _mp_gather_kernel(n, x_ref, o_ref, recv, send_sem, recv_sem):
    me = lax.axis_index("mp")
    dp = (lax.axis_index("y"), lax.axis_index("z"))
    rows = x_ref.shape[0]
    _greet(n, me, dp)
    copies = []
    for k in range(1, n):
        peer = (me + k) % n
        copy = pltpu.make_async_remote_copy(
            src_ref=x_ref,
            dst_ref=recv.at[k],
            send_sem=send_sem.at[k],
            recv_sem=recv_sem.at[k],
            device_id=(*dp, peer),
            device_id_type=MESH,
        )
        copy.start()
        copies.append(copy)
    for copy in copies:
        copy.wait()
    o_ref[pl.ds(pl.multiple_of(me * rows, rows), rows), :] = x_ref[...]
    for k in range(1, n):
        source = (me + n - k) % n
        o_ref[pl.ds(pl.multiple_of(source * rows, rows), rows), :] = recv[k]


def mp_gather(x, collective_id):
    n = lax.axis_size("mp")
    rows, cols = x.shape
    return pl.pallas_call(
        functools.partial(_mp_gather_kernel, n),
        out_shape=jax.ShapeDtypeStruct((n * rows, cols), x.dtype),
        in_specs=[pl.BlockSpec(memory_space=pltpu.VMEM)],
        out_specs=pl.BlockSpec(memory_space=pltpu.VMEM),
        scratch_shapes=[
            pltpu.VMEM((n, rows, cols), x.dtype),
            pltpu.SemaphoreType.DMA((n,)),
            pltpu.SemaphoreType.DMA((n,)),
        ],
        compiler_params=pltpu.CompilerParams(collective_id=collective_id, has_side_effects=True),
    )(x)


HD = 64
TOP = 2


EPS = 1e-05
NEGATIVE = -1e30


def rms_scale(rows, gain):
    rows_wide = rows.astype(jnp.float32)
    mean_square = jnp.mean(rows_wide * rows_wide, axis=-1, keepdims=True)
    return rows_wide * lax.rsqrt(mean_square + EPS) * gain


def level_partial(queries, node_keys, node_values, limits, heads_here, batched):
    senders, row_count, width = queries.shape
    head_dim = width // heads_here
    scale = 1.0 / math.sqrt(head_dim)
    query_heads = queries.reshape(senders, row_count, heads_here, head_dim)
    if batched:
        key_heads = node_keys.reshape(senders, -1, heads_here, head_dim)
        value_heads = node_values.reshape(senders, -1, heads_here, head_dim)
        scores = jnp.einsum(
            "sqhd,skhd->sqhk", query_heads, key_heads, preferred_element_type=jnp.float32
        )
    else:
        key_heads = node_keys.reshape(-1, heads_here, head_dim)
        value_heads = node_values.reshape(-1, heads_here, head_dim)
        scores = jnp.einsum(
            "sqhd,khd->sqhk", query_heads, key_heads, preferred_element_type=jnp.float32
        )
    scores = scores * scale
    slots = jnp.arange(scores.shape[-1], dtype=jnp.int32)
    allowed = slots[None, :] < limits[:, None]
    scores = jnp.where(allowed[:, None, None, :], scores, NEGATIVE)
    peak = jnp.max(scores, axis=-1)
    weights = jnp.exp(scores - peak[..., None])
    total = jnp.sum(weights, axis=-1)
    probs = weights.astype(jnp.bfloat16)
    if batched:
        summed = jnp.einsum(
            "sqhk,skhd->sqhd", probs, value_heads, preferred_element_type=jnp.float32
        )
    else:
        summed = jnp.einsum(
            "sqhk,khd->sqhd", probs, value_heads, preferred_element_type=jnp.float32
        )
    result = (summed / total[..., None]).reshape(senders, row_count, width)
    return (result, peak + jnp.log(total))


def on_device(
    hidden_in,
    attn_gain,
    w_query,
    w_key,
    w_value,
    w_out,
    root_cache,
    mid_cache,
    leaf_cache,
    mid_len,
    leaf_len,
    leaf_of,
    parents,
    suffix_len,
    ffn_gain,
    w_router,
    routes,
    w_gate,
    w_up,
    w_down,
):
    tok_rows, width = hidden_in.shape
    seq_rows = suffix_len.shape[0]
    suffix = tok_rows // seq_rows
    head_dim = HD
    local_width = w_query.shape[1]
    heads_here = local_width // head_dim
    scale = 1.0 / math.sqrt(head_dim)
    owners = lax.axis_size(DP)
    normed = rms_scale(hidden_in, attn_gain).astype(jnp.bfloat16)
    query = jnp.dot(normed, w_query, preferred_element_type=jnp.float32).astype(jnp.bfloat16)
    key = jnp.dot(normed, w_key, preferred_element_type=jnp.float32).astype(jnp.bfloat16)
    value = jnp.dot(normed, w_value, preferred_element_type=jnp.float32).astype(jnp.bfloat16)
    query_heads = query.reshape(tok_rows, heads_here, head_dim)
    piece = lax.all_gather(root_cache, DP, axis=1, tiled=True)
    running_peak = jnp.full((tok_rows, heads_here), NEGATIVE, jnp.float32)
    piece_keys = piece[0].reshape(-1, heads_here, head_dim)
    piece_values = piece[1].reshape(-1, heads_here, head_dim)
    scores = (
        jnp.einsum("qhd,khd->qhk", query_heads, piece_keys, preferred_element_type=jnp.float32)
        * scale
    )
    new_peak = jnp.maximum(running_peak, jnp.max(scores, axis=-1))
    weights = jnp.exp(scores - new_peak[..., None])
    new_total = jnp.sum(weights, axis=-1)
    added = jnp.einsum(
        "qhk,khd->qhd",
        weights.astype(jnp.bfloat16),
        piece_values,
        preferred_element_type=jnp.float32,
    )
    root_out = added / new_total[..., None]
    root_lse = new_peak + jnp.log(new_total)
    query_seq = query.reshape(seq_rows, suffix, heads_here, head_dim)
    key_seq = key.reshape(seq_rows, suffix, heads_here, head_dim)
    value_seq = value.reshape(seq_rows, suffix, heads_here, head_dim)
    slots = jnp.arange(suffix, dtype=jnp.int32)
    self_ok = (slots[None, None, :] <= slots[None, :, None]) & (
        slots[None, None, :] < suffix_len[:, None, None]
    )
    self_scores = (
        jnp.einsum("sqhd,skhd->sqhk", query_seq, key_seq, preferred_element_type=jnp.float32)
        * scale
    )
    self_scores = jnp.where(self_ok[:, :, None, :], self_scores, NEGATIVE)
    self_peak = jnp.max(self_scores, axis=-1)
    self_weights = jnp.exp(self_scores - self_peak[..., None])
    self_total = jnp.sum(self_weights, axis=-1)
    self_sum = jnp.einsum(
        "sqhk,skhd->sqhd",
        self_weights.astype(jnp.bfloat16),
        value_seq,
        preferred_element_type=jnp.float32,
    )
    self_out = (self_sum / self_total[..., None]).reshape(tok_rows, heads_here, head_dim)
    self_lse = (self_peak + jnp.log(self_total)).reshape(tok_rows, heads_here)
    mid_of = parents[leaf_of]
    leaf_owner = leaf_of // 2
    targets = jnp.arange(owners, dtype=jnp.int32)
    pick_mid = (mid_of[None, :] == targets[:, None]).astype(jnp.bfloat16)
    pick_leaf = (leaf_owner[None, :] == targets[:, None]).astype(jnp.bfloat16)
    flat_query = query.reshape(seq_rows, suffix * local_width)
    sent_mid = jnp.dot(pick_mid, flat_query, preferred_element_type=jnp.float32).astype(
        jnp.bfloat16
    )
    sent_leaf = jnp.dot(pick_leaf, flat_query, preferred_element_type=jnp.float32).astype(
        jnp.bfloat16
    )
    sent = jnp.stack([sent_mid, sent_leaf], axis=1).reshape(owners, 2, suffix, local_width)
    leaf_side = (leaf_of % 2).astype(jnp.float32)
    side_of_target = jnp.dot(
        pick_leaf.astype(jnp.float32), leaf_side, precision=lax.Precision.HIGHEST
    )
    side_rows = jnp.broadcast_to(side_of_target[:, None, None], (owners, 8, local_width))
    sent_all = jnp.concatenate(
        [sent.reshape(owners, 2 * suffix, local_width), side_rows.astype(jnp.bfloat16)], axis=1
    )
    got_all = lax.all_to_all(sent_all, DP, split_axis=0, concat_axis=0, tiled=True)
    sent_queries = got_all[:, : 2 * suffix].reshape(owners, 2, suffix, local_width)
    second = got_all[:, 2 * suffix, 0] > 0.5
    senders = sent_queries.shape[0]
    mid_limit = jnp.broadcast_to(mid_len[0], (senders,))
    mid_result, mid_logsum = level_partial(
        sent_queries[:, 0], mid_cache[0, 0], mid_cache[1, 0], mid_limit, heads_here, False
    )
    leaf_keys = jnp.where(second[:, None, None], leaf_cache[0, 1][None], leaf_cache[0, 0][None])
    leaf_values = jnp.where(second[:, None, None], leaf_cache[1, 1][None], leaf_cache[1, 0][None])
    leaf_limit = jnp.where(second, leaf_len[1], leaf_len[0])
    leaf_result, leaf_logsum = level_partial(
        sent_queries[:, 1], leaf_keys, leaf_values, leaf_limit, heads_here, True
    )
    owner_out = jnp.stack([mid_result, leaf_result], axis=1)
    owner_lse = jnp.stack([mid_logsum, leaf_logsum], axis=1)
    owner_all = jnp.concatenate([owner_out, owner_lse], axis=-1)
    back_all = lax.all_to_all(owner_all, DP, split_axis=0, concat_axis=0, tiled=True)
    back_out = back_all[..., :local_width]
    back_lse = back_all[..., local_width:]
    mid_out = back_out[mid_of, 0].reshape(tok_rows, heads_here, head_dim)
    mid_lse = back_lse[mid_of, 0].reshape(tok_rows, heads_here)
    leaf_out = back_out[leaf_owner, 1].reshape(tok_rows, heads_here, head_dim)
    leaf_lse = back_lse[leaf_owner, 1].reshape(tok_rows, heads_here)
    stacked_lse = jnp.stack([root_lse, mid_lse, leaf_lse, self_lse])
    stacked_out = jnp.stack([root_out, mid_out, leaf_out, self_out])
    overall = jnp.max(stacked_lse, axis=0)
    shares = jnp.exp(stacked_lse - overall)
    combined = jnp.sum(shares[..., None] * stacked_out, axis=0) / jnp.sum(shares, axis=0)[..., None]
    attended = combined.reshape(tok_rows, local_width).astype(jnp.bfloat16)
    unit_weights = lax.all_gather(
        jnp.stack([w_gate[0], w_up[0], w_down[0].T]), "z", axis=0, tiled=False
    )
    projected = jnp.dot(attended, w_out, preferred_element_type=jnp.float32)
    rows_here = tok_rows // lax.axis_size("mp")
    first = lax.axis_index("mp") * rows_here
    attn_rows = mp_sum_scatter(projected.astype(jnp.bfloat16), 0)
    resid = lax.dynamic_slice_in_dim(hidden_in, first, rows_here, 0).astype(jnp.float32) + attn_rows
    ffn_rows = rms_scale(resid, ffn_gain).astype(jnp.bfloat16)
    ffn_in = mp_gather(ffn_rows, 1)
    unit_weights, ffn_in = lax.optimization_barrier((unit_weights, ffn_in))
    logits = jnp.dot(ffn_in.astype(jnp.float32), w_router, precision=lax.Precision.HIGHEST)
    chosen = jnp.take_along_axis(logits, routes, axis=1)
    squashed = jax.nn.sigmoid(chosen)
    gates = squashed / jnp.sum(squashed, axis=1, keepdims=True)
    expert = lax.axis_index("mp")
    hit_each = routes == expert
    hit = jnp.any(hit_each, axis=1)
    gate_here = jnp.sum(jnp.where(hit_each, gates, 0.0), axis=1)
    order = jnp.cumsum(hit.astype(jnp.int32)) - 1
    capacity = 3 * TOP * tok_rows // (2 * lax.axis_size("mp"))
    slot_ids = jnp.arange(capacity, dtype=jnp.int32)
    pick_slot = (order[None, :] == slot_ids[:, None]) & hit[None, :]
    dispatch = jnp.dot(
        pick_slot.astype(jnp.bfloat16), ffn_in, preferred_element_type=jnp.float32
    ).astype(jnp.bfloat16)
    slot_gate = jnp.dot(pick_slot.astype(jnp.float32), gate_here, precision=lax.Precision.HIGHEST)
    piece = lax.all_gather(dispatch, "y", axis=0, tiled=True)
    gate_part = jnp.einsum(
        "td,zdu->tzu", piece, unit_weights[:, 0], preferred_element_type=jnp.float32
    )
    up_part = jnp.einsum(
        "td,zdu->tzu", piece, unit_weights[:, 1], preferred_element_type=jnp.float32
    )
    partial_out = jnp.einsum(
        "tzu,zdu->td",
        (jax.nn.silu(gate_part) * up_part).astype(jnp.bfloat16),
        unit_weights[:, 2],
        preferred_element_type=jnp.float32,
    )
    expert_out = lax.psum_scatter(
        partial_out.astype(jnp.bfloat16), "y", scatter_dimension=0, tiled=True
    )
    weighted = expert_out.astype(jnp.float32) * slot_gate[:, None]
    spread = jnp.dot(pick_slot.astype(jnp.float32).T, weighted, precision=lax.Precision.HIGHEST)
    mixed = mp_sum_scatter(spread.astype(jnp.bfloat16), 2)
    row_ids = first + jnp.arange(rows_here, dtype=jnp.int32)
    valid = row_ids % suffix < suffix_len[row_ids // suffix]
    return jnp.where(valid[:, None], resid + mixed, 0.0).astype(jnp.bfloat16)


def solution(mesh):
    return jax.shard_map(
        on_device,
        mesh=Mesh(mesh.devices.reshape(4, 4, -1), ("y", "z", "mp")),
        in_specs=(
            P(DP, None),
            P(),
            P(None, "mp"),
            P(None, "mp"),
            P(None, "mp"),
            P("mp", None),
            P(None, DP, "mp"),
            P(None, DP, None, "mp"),
            P(None, DP, None, "mp"),
            P(DP),
            P(DP),
            P(DP),
            P(),
            P(DP),
            P(),
            P(),
            P(DP, None),
            P("mp", None, DP),
            P("mp", None, DP),
            P("mp", DP, None),
        ),
        out_specs=P(("y", "z", "mp"), None),
        check_vma=False,
    )
```

```python
import math

import jax
import jax.numpy as jnp
from jax import lax
import functools

from jax.experimental import pallas as pl
from jax.experimental.pallas import tpu as pltpu
from jax.sharding import Mesh, PartitionSpec as P

DP = ("y", "z")

MESH = pl.DeviceIdType.MESH


def _greet(n, me, dp):
    barrier = pltpu.get_barrier_semaphore()
    for k in range(1, n):
        pl.semaphore_signal(barrier, 1, device_id=(*dp, (me + k) % n), device_id_type=MESH)
    pl.semaphore_wait(barrier, n - 1)


def _mp_sum_kernel(n, x_ref, o_ref, recv, send_sem, recv_sem):
    me = lax.axis_index("mp")
    dp = (lax.axis_index("y"), lax.axis_index("z"))
    rows = o_ref.shape[0]
    _greet(n, me, dp)
    copies = []
    for k in range(1, n):
        peer = (me + k) % n
        copy = pltpu.make_async_remote_copy(
            src_ref=x_ref.at[pl.ds(pl.multiple_of(peer * rows, rows), rows)],
            dst_ref=recv.at[k],
            send_sem=send_sem.at[k],
            recv_sem=recv_sem.at[k],
            device_id=(*dp, peer),
            device_id_type=MESH,
        )
        copy.start()
        copies.append(copy)
    for copy in copies:
        copy.wait()
    total = x_ref[pl.ds(pl.multiple_of(me * rows, rows), rows), :].astype(jnp.float32)
    for k in range(1, n):
        total = total + recv[k].astype(jnp.float32)
    o_ref[...] = total


def mp_sum_scatter(x, collective_id):
    n = lax.axis_size("mp")
    rows = x.shape[0] // n
    cols = x.shape[1]
    return pl.pallas_call(
        functools.partial(_mp_sum_kernel, n),
        out_shape=jax.ShapeDtypeStruct((rows, cols), jnp.float32),
        in_specs=[pl.BlockSpec(memory_space=pltpu.VMEM)],
        out_specs=pl.BlockSpec(memory_space=pltpu.VMEM),
        scratch_shapes=[
            pltpu.VMEM((n, rows, cols), x.dtype),
            pltpu.SemaphoreType.DMA((n,)),
            pltpu.SemaphoreType.DMA((n,)),
        ],
        compiler_params=pltpu.CompilerParams(collective_id=collective_id, has_side_effects=True),
    )(x)


def _mp_gather_kernel(n, x_ref, o_ref, recv, send_sem, recv_sem):
    me = lax.axis_index("mp")
    dp = (lax.axis_index("y"), lax.axis_index("z"))
    rows = x_ref.shape[0]
    _greet(n, me, dp)
    copies = []
    for k in range(1, n):
        peer = (me + k) % n
        copy = pltpu.make_async_remote_copy(
            src_ref=x_ref,
            dst_ref=recv.at[k],
            send_sem=send_sem.at[k],
            recv_sem=recv_sem.at[k],
            device_id=(*dp, peer),
            device_id_type=MESH,
        )
        copy.start()
        copies.append(copy)
    for copy in copies:
        copy.wait()
    o_ref[pl.ds(pl.multiple_of(me * rows, rows), rows), :] = x_ref[...]
    for k in range(1, n):
        source = (me + n - k) % n
        o_ref[pl.ds(pl.multiple_of(source * rows, rows), rows), :] = recv[k]


def mp_gather(x, collective_id):
    n = lax.axis_size("mp")
    rows, cols = x.shape
    return pl.pallas_call(
        functools.partial(_mp_gather_kernel, n),
        out_shape=jax.ShapeDtypeStruct((n * rows, cols), x.dtype),
        in_specs=[pl.BlockSpec(memory_space=pltpu.VMEM)],
        out_specs=pl.BlockSpec(memory_space=pltpu.VMEM),
        scratch_shapes=[
            pltpu.VMEM((n, rows, cols), x.dtype),
            pltpu.SemaphoreType.DMA((n,)),
            pltpu.SemaphoreType.DMA((n,)),
        ],
        compiler_params=pltpu.CompilerParams(collective_id=collective_id, has_side_effects=True),
    )(x)


HD = 64
TOP = 2


EPS = 1e-05
NEGATIVE = -1e30


def rms_scale(rows, gain):
    rows_wide = rows.astype(jnp.float32)
    mean_square = jnp.mean(rows_wide * rows_wide, axis=-1, keepdims=True)
    return rows_wide * lax.rsqrt(mean_square + EPS) * gain


def level_partial(queries, node_keys, node_values, limits, heads_here, batched):
    senders, row_count, width = queries.shape
    head_dim = width // heads_here
    scale = 1.0 / math.sqrt(head_dim)
    query_heads = queries.reshape(senders, row_count, heads_here, head_dim)
    if batched:
        key_heads = node_keys.reshape(senders, -1, heads_here, head_dim)
        value_heads = node_values.reshape(senders, -1, heads_here, head_dim)
        scores = jnp.einsum(
            "sqhd,skhd->sqhk", query_heads, key_heads, preferred_element_type=jnp.float32
        )
    else:
        key_heads = node_keys.reshape(-1, heads_here, head_dim)
        value_heads = node_values.reshape(-1, heads_here, head_dim)
        scores = jnp.einsum(
            "sqhd,khd->sqhk", query_heads, key_heads, preferred_element_type=jnp.float32
        )
    scores = scores * scale
    slots = jnp.arange(scores.shape[-1], dtype=jnp.int32)
    allowed = slots[None, :] < limits[:, None]
    scores = jnp.where(allowed[:, None, None, :], scores, NEGATIVE)
    peak = jnp.max(scores, axis=-1)
    weights = jnp.exp(scores - peak[..., None])
    total = jnp.sum(weights, axis=-1)
    probs = weights.astype(jnp.bfloat16)
    if batched:
        summed = jnp.einsum(
            "sqhk,skhd->sqhd", probs, value_heads, preferred_element_type=jnp.float32
        )
    else:
        summed = jnp.einsum(
            "sqhk,khd->sqhd", probs, value_heads, preferred_element_type=jnp.float32
        )
    result = (summed / total[..., None]).reshape(senders, row_count, width)
    return (result, peak + jnp.log(total))


def on_device(
    hidden_in,
    attn_gain,
    w_query,
    w_key,
    w_value,
    w_out,
    root_cache,
    mid_cache,
    leaf_cache,
    mid_len,
    leaf_len,
    leaf_of,
    parents,
    suffix_len,
    ffn_gain,
    w_router,
    routes,
    w_gate,
    w_up,
    w_down,
):
    tok_rows, width = hidden_in.shape
    seq_rows = suffix_len.shape[0]
    suffix = tok_rows // seq_rows
    head_dim = HD
    local_width = w_query.shape[1]
    heads_here = local_width // head_dim
    scale = 1.0 / math.sqrt(head_dim)
    owners = lax.axis_size(DP)
    normed = rms_scale(hidden_in, attn_gain).astype(jnp.bfloat16)
    query = jnp.dot(normed, w_query, preferred_element_type=jnp.float32).astype(jnp.bfloat16)
    key = jnp.dot(normed, w_key, preferred_element_type=jnp.float32).astype(jnp.bfloat16)
    value = jnp.dot(normed, w_value, preferred_element_type=jnp.float32).astype(jnp.bfloat16)
    query_heads = query.reshape(tok_rows, heads_here, head_dim)
    root_copies = jnp.broadcast_to(root_cache[None], (owners,) + root_cache.shape)
    root_got = lax.all_to_all(root_copies, DP, split_axis=0, concat_axis=0, tiled=True)
    piece = root_got.transpose(1, 0, 2, 3).reshape(
        root_cache.shape[0], owners * root_cache.shape[1], root_cache.shape[2]
    )
    running_peak = jnp.full((tok_rows, heads_here), NEGATIVE, jnp.float32)
    piece_keys = piece[0].reshape(-1, heads_here, head_dim)
    piece_values = piece[1].reshape(-1, heads_here, head_dim)
    scores = (
        jnp.einsum("qhd,khd->qhk", query_heads, piece_keys, preferred_element_type=jnp.float32)
        * scale
    )
    new_peak = jnp.maximum(running_peak, jnp.max(scores, axis=-1))
    weights = jnp.exp(scores - new_peak[..., None])
    new_total = jnp.sum(weights, axis=-1)
    added = jnp.einsum(
        "qhk,khd->qhd",
        weights.astype(jnp.bfloat16),
        piece_values,
        preferred_element_type=jnp.float32,
    )
    root_out = added / new_total[..., None]
    root_lse = new_peak + jnp.log(new_total)
    query_seq = query.reshape(seq_rows, suffix, heads_here, head_dim)
    key_seq = key.reshape(seq_rows, suffix, heads_here, head_dim)
    value_seq = value.reshape(seq_rows, suffix, heads_here, head_dim)
    slots = jnp.arange(suffix, dtype=jnp.int32)
    self_ok = (slots[None, None, :] <= slots[None, :, None]) & (
        slots[None, None, :] < suffix_len[:, None, None]
    )
    self_scores = (
        jnp.einsum("sqhd,skhd->sqhk", query_seq, key_seq, preferred_element_type=jnp.float32)
        * scale
    )
    self_scores = jnp.where(self_ok[:, :, None, :], self_scores, NEGATIVE)
    self_peak = jnp.max(self_scores, axis=-1)
    self_weights = jnp.exp(self_scores - self_peak[..., None])
    self_total = jnp.sum(self_weights, axis=-1)
    self_sum = jnp.einsum(
        "sqhk,skhd->sqhd",
        self_weights.astype(jnp.bfloat16),
        value_seq,
        preferred_element_type=jnp.float32,
    )
    self_out = (self_sum / self_total[..., None]).reshape(tok_rows, heads_here, head_dim)
    self_lse = (self_peak + jnp.log(self_total)).reshape(tok_rows, heads_here)
    mid_of = parents[leaf_of]
    leaf_owner = leaf_of // 2
    targets = jnp.arange(owners, dtype=jnp.int32)
    pick_mid = (mid_of[None, :] == targets[:, None]).astype(jnp.bfloat16)
    pick_leaf = (leaf_owner[None, :] == targets[:, None]).astype(jnp.bfloat16)
    flat_query = query.reshape(seq_rows, suffix * local_width)
    sent_mid = jnp.dot(pick_mid, flat_query, preferred_element_type=jnp.float32).astype(
        jnp.bfloat16
    )
    sent_leaf = jnp.dot(pick_leaf, flat_query, preferred_element_type=jnp.float32).astype(
        jnp.bfloat16
    )
    sent = jnp.stack([sent_mid, sent_leaf], axis=1).reshape(owners, 2, suffix, local_width)
    leaf_side = (leaf_of % 2).astype(jnp.float32)
    side_of_target = jnp.dot(
        pick_leaf.astype(jnp.float32), leaf_side, precision=lax.Precision.HIGHEST
    )
    side_rows = jnp.broadcast_to(side_of_target[:, None, None], (owners, 8, local_width))
    sent_all = jnp.concatenate(
        [sent.reshape(owners, 2 * suffix, local_width), side_rows.astype(jnp.bfloat16)], axis=1
    )
    got_all = lax.all_to_all(sent_all, DP, split_axis=0, concat_axis=0, tiled=True)
    sent_queries = got_all[:, : 2 * suffix].reshape(owners, 2, suffix, local_width)
    second = got_all[:, 2 * suffix, 0] > 0.5
    senders = sent_queries.shape[0]
    mid_limit = jnp.broadcast_to(mid_len[0], (senders,))
    mid_result, mid_logsum = level_partial(
        sent_queries[:, 0], mid_cache[0, 0], mid_cache[1, 0], mid_limit, heads_here, False
    )
    leaf_keys = jnp.where(second[:, None, None], leaf_cache[0, 1][None], leaf_cache[0, 0][None])
    leaf_values = jnp.where(second[:, None, None], leaf_cache[1, 1][None], leaf_cache[1, 0][None])
    leaf_limit = jnp.where(second, leaf_len[1], leaf_len[0])
    leaf_result, leaf_logsum = level_partial(
        sent_queries[:, 1], leaf_keys, leaf_values, leaf_limit, heads_here, True
    )
    owner_out = jnp.stack([mid_result, leaf_result], axis=1)
    owner_lse = jnp.stack([mid_logsum, leaf_logsum], axis=1)
    owner_all = jnp.concatenate([owner_out, owner_lse], axis=-1)
    back_all = lax.all_to_all(owner_all, DP, split_axis=0, concat_axis=0, tiled=True)
    back_out = back_all[..., :local_width]
    back_lse = back_all[..., local_width:]
    mid_out = back_out[mid_of, 0].reshape(tok_rows, heads_here, head_dim)
    mid_lse = back_lse[mid_of, 0].reshape(tok_rows, heads_here)
    leaf_out = back_out[leaf_owner, 1].reshape(tok_rows, heads_here, head_dim)
    leaf_lse = back_lse[leaf_owner, 1].reshape(tok_rows, heads_here)
    stacked_lse = jnp.stack([root_lse, mid_lse, leaf_lse, self_lse])
    stacked_out = jnp.stack([root_out, mid_out, leaf_out, self_out])
    overall = jnp.max(stacked_lse, axis=0)
    shares = jnp.exp(stacked_lse - overall)
    combined = jnp.sum(shares[..., None] * stacked_out, axis=0) / jnp.sum(shares, axis=0)[..., None]
    attended = combined.reshape(tok_rows, local_width).astype(jnp.bfloat16)
    unit_weights = lax.all_gather(
        jnp.stack([w_gate[0], w_up[0], w_down[0].T]), "z", axis=0, tiled=False
    )
    projected = jnp.dot(attended, w_out, preferred_element_type=jnp.float32)
    rows_here = tok_rows // lax.axis_size("mp")
    first = lax.axis_index("mp") * rows_here
    attn_rows = mp_sum_scatter(projected.astype(jnp.bfloat16), 0)
    resid = lax.dynamic_slice_in_dim(hidden_in, first, rows_here, 0).astype(jnp.float32) + attn_rows
    ffn_rows = rms_scale(resid, ffn_gain).astype(jnp.bfloat16)
    ffn_in = mp_gather(ffn_rows, 1)
    unit_weights, ffn_in = lax.optimization_barrier((unit_weights, ffn_in))
    logits = jnp.dot(ffn_in.astype(jnp.float32), w_router, precision=lax.Precision.HIGHEST)
    chosen = jnp.take_along_axis(logits, routes, axis=1)
    squashed = jax.nn.sigmoid(chosen)
    gates = squashed / jnp.sum(squashed, axis=1, keepdims=True)
    expert = lax.axis_index("mp")
    hit_each = routes == expert
    hit = jnp.any(hit_each, axis=1)
    gate_here = jnp.sum(jnp.where(hit_each, gates, 0.0), axis=1)
    order = jnp.cumsum(hit.astype(jnp.int32)) - 1
    capacity = 3 * TOP * tok_rows // (2 * lax.axis_size("mp"))
    slot_ids = jnp.arange(capacity, dtype=jnp.int32)
    pick_slot = (order[None, :] == slot_ids[:, None]) & hit[None, :]
    dispatch = jnp.dot(
        pick_slot.astype(jnp.bfloat16), ffn_in, preferred_element_type=jnp.float32
    ).astype(jnp.bfloat16)
    slot_gate = jnp.dot(pick_slot.astype(jnp.float32), gate_here, precision=lax.Precision.HIGHEST)
    piece = lax.all_gather(dispatch, "y", axis=0, tiled=True)
    gate_part = jnp.einsum(
        "td,zdu->tzu", piece, unit_weights[:, 0], preferred_element_type=jnp.float32
    )
    up_part = jnp.einsum(
        "td,zdu->tzu", piece, unit_weights[:, 1], preferred_element_type=jnp.float32
    )
    partial_out = jnp.einsum(
        "tzu,zdu->td",
        (jax.nn.silu(gate_part) * up_part).astype(jnp.bfloat16),
        unit_weights[:, 2],
        preferred_element_type=jnp.float32,
    )
    expert_out = lax.psum_scatter(
        partial_out.astype(jnp.bfloat16), "y", scatter_dimension=0, tiled=True
    )
    weighted = expert_out.astype(jnp.float32) * slot_gate[:, None]
    spread = jnp.dot(pick_slot.astype(jnp.float32).T, weighted, precision=lax.Precision.HIGHEST)
    mixed = mp_sum_scatter(spread.astype(jnp.bfloat16), 2)
    row_ids = first + jnp.arange(rows_here, dtype=jnp.int32)
    valid = row_ids % suffix < suffix_len[row_ids // suffix]
    return jnp.where(valid[:, None], resid + mixed, 0.0).astype(jnp.bfloat16)


def solution(mesh):
    return jax.shard_map(
        on_device,
        mesh=Mesh(mesh.devices.reshape(4, 4, -1), ("y", "z", "mp")),
        in_specs=(
            P(DP, None),
            P(),
            P(None, "mp"),
            P(None, "mp"),
            P(None, "mp"),
            P("mp", None),
            P(None, DP, "mp"),
            P(None, DP, None, "mp"),
            P(None, DP, None, "mp"),
            P(DP),
            P(DP),
            P(DP),
            P(),
            P(DP),
            P(),
            P(),
            P(DP, None),
            P("mp", None, DP),
            P("mp", None, DP),
            P("mp", DP, None),
        ),
        out_specs=P(("y", "z", "mp"), None),
        check_vma=False,
    )
```

```python
import math

import jax
import jax.numpy as jnp
from jax import lax
import functools

from jax.experimental import pallas as pl
from jax.experimental.pallas import tpu as pltpu
from jax.sharding import Mesh, PartitionSpec as P

DP = ("y", "z")

MESH = pl.DeviceIdType.MESH


def _greet(n, me, dp):
    barrier = pltpu.get_barrier_semaphore()
    for k in range(1, n):
        pl.semaphore_signal(barrier, 1, device_id=(*dp, (me + k) % n), device_id_type=MESH)
    pl.semaphore_wait(barrier, n - 1)


def _mp_sum_kernel(n, x_ref, o_ref, recv, send_sem, recv_sem):
    me = lax.axis_index("mp")
    dp = (lax.axis_index("y"), lax.axis_index("z"))
    rows = o_ref.shape[0]
    _greet(n, me, dp)
    copies = []
    for k in range(1, n):
        peer = (me + k) % n
        copy = pltpu.make_async_remote_copy(
            src_ref=x_ref.at[pl.ds(pl.multiple_of(peer * rows, rows), rows)],
            dst_ref=recv.at[k],
            send_sem=send_sem.at[k],
            recv_sem=recv_sem.at[k],
            device_id=(*dp, peer),
            device_id_type=MESH,
        )
        copy.start()
        copies.append(copy)
    for copy in copies:
        copy.wait()
    total = x_ref[pl.ds(pl.multiple_of(me * rows, rows), rows), :].astype(jnp.float32)
    for k in range(1, n):
        total = total + recv[k].astype(jnp.float32)
    o_ref[...] = total


def mp_sum_scatter(x, collective_id):
    n = lax.axis_size("mp")
    rows = x.shape[0] // n
    cols = x.shape[1]
    return pl.pallas_call(
        functools.partial(_mp_sum_kernel, n),
        out_shape=jax.ShapeDtypeStruct((rows, cols), jnp.float32),
        in_specs=[pl.BlockSpec(memory_space=pltpu.VMEM)],
        out_specs=pl.BlockSpec(memory_space=pltpu.VMEM),
        scratch_shapes=[
            pltpu.VMEM((n, rows, cols), x.dtype),
            pltpu.SemaphoreType.DMA((n,)),
            pltpu.SemaphoreType.DMA((n,)),
        ],
        compiler_params=pltpu.CompilerParams(collective_id=collective_id, has_side_effects=True),
    )(x)


def _mp_gather_kernel(n, x_ref, o_ref, recv, send_sem, recv_sem):
    me = lax.axis_index("mp")
    dp = (lax.axis_index("y"), lax.axis_index("z"))
    rows = x_ref.shape[0]
    _greet(n, me, dp)
    copies = []
    for k in range(1, n):
        peer = (me + k) % n
        copy = pltpu.make_async_remote_copy(
            src_ref=x_ref,
            dst_ref=recv.at[k],
            send_sem=send_sem.at[k],
            recv_sem=recv_sem.at[k],
            device_id=(*dp, peer),
            device_id_type=MESH,
        )
        copy.start()
        copies.append(copy)
    for copy in copies:
        copy.wait()
    o_ref[pl.ds(pl.multiple_of(me * rows, rows), rows), :] = x_ref[...]
    for k in range(1, n):
        source = (me + n - k) % n
        o_ref[pl.ds(pl.multiple_of(source * rows, rows), rows), :] = recv[k]


def mp_gather(x, collective_id):
    n = lax.axis_size("mp")
    rows, cols = x.shape
    return pl.pallas_call(
        functools.partial(_mp_gather_kernel, n),
        out_shape=jax.ShapeDtypeStruct((n * rows, cols), x.dtype),
        in_specs=[pl.BlockSpec(memory_space=pltpu.VMEM)],
        out_specs=pl.BlockSpec(memory_space=pltpu.VMEM),
        scratch_shapes=[
            pltpu.VMEM((n, rows, cols), x.dtype),
            pltpu.SemaphoreType.DMA((n,)),
            pltpu.SemaphoreType.DMA((n,)),
        ],
        compiler_params=pltpu.CompilerParams(collective_id=collective_id, has_side_effects=True),
    )(x)


HD = 64
TOP = 2


EPS = 1e-05
NEGATIVE = -1e30


def rms_scale(rows, gain):
    rows_wide = rows.astype(jnp.float32)
    mean_square = jnp.mean(rows_wide * rows_wide, axis=-1, keepdims=True)
    return rows_wide * lax.rsqrt(mean_square + EPS) * gain


def level_partial(queries, node_keys, node_values, limits, heads_here, batched):
    senders, row_count, width = queries.shape
    head_dim = width // heads_here
    scale = 1.0 / math.sqrt(head_dim)
    query_heads = queries.reshape(senders, row_count, heads_here, head_dim)
    if batched:
        key_heads = node_keys.reshape(senders, -1, heads_here, head_dim)
        value_heads = node_values.reshape(senders, -1, heads_here, head_dim)
        scores = jnp.einsum(
            "sqhd,skhd->sqhk", query_heads, key_heads, preferred_element_type=jnp.float32
        )
    else:
        key_heads = node_keys.reshape(-1, heads_here, head_dim)
        value_heads = node_values.reshape(-1, heads_here, head_dim)
        scores = jnp.einsum(
            "sqhd,khd->sqhk", query_heads, key_heads, preferred_element_type=jnp.float32
        )
    scores = scores * scale
    slots = jnp.arange(scores.shape[-1], dtype=jnp.int32)
    allowed = slots[None, :] < limits[:, None]
    scores = jnp.where(allowed[:, None, None, :], scores, NEGATIVE)
    peak = jnp.max(scores, axis=-1)
    weights = jnp.exp(scores - peak[..., None])
    total = jnp.sum(weights, axis=-1)
    probs = weights.astype(jnp.bfloat16)
    if batched:
        summed = jnp.einsum(
            "sqhk,skhd->sqhd", probs, value_heads, preferred_element_type=jnp.float32
        )
    else:
        summed = jnp.einsum(
            "sqhk,khd->sqhd", probs, value_heads, preferred_element_type=jnp.float32
        )
    result = (summed / total[..., None]).reshape(senders, row_count, width)
    return (result, peak + jnp.log(total))


def on_device(
    hidden_in,
    attn_gain,
    w_query,
    w_key,
    w_value,
    w_out,
    root_cache,
    mid_cache,
    leaf_cache,
    mid_len,
    leaf_len,
    leaf_of,
    parents,
    suffix_len,
    ffn_gain,
    w_router,
    routes,
    w_gate,
    w_up,
    w_down,
):
    tok_rows, width = hidden_in.shape
    seq_rows = suffix_len.shape[0]
    suffix = tok_rows // seq_rows
    head_dim = HD
    local_width = w_query.shape[1]
    heads_here = local_width // head_dim
    scale = 1.0 / math.sqrt(head_dim)
    owners = lax.axis_size(DP)
    normed = rms_scale(hidden_in, attn_gain).astype(jnp.bfloat16)
    query = jnp.dot(normed, w_query, preferred_element_type=jnp.float32).astype(jnp.bfloat16)
    key = jnp.dot(normed, w_key, preferred_element_type=jnp.float32).astype(jnp.bfloat16)
    value = jnp.dot(normed, w_value, preferred_element_type=jnp.float32).astype(jnp.bfloat16)
    query_heads = query.reshape(tok_rows, heads_here, head_dim)
    piece = lax.all_gather(
        lax.all_gather(root_cache, "z", axis=1, tiled=True), "y", axis=1, tiled=True
    )
    running_peak = jnp.full((tok_rows, heads_here), NEGATIVE, jnp.float32)
    piece_keys = piece[0].reshape(-1, heads_here, head_dim)
    piece_values = piece[1].reshape(-1, heads_here, head_dim)
    scores = (
        jnp.einsum("qhd,khd->qhk", query_heads, piece_keys, preferred_element_type=jnp.float32)
        * scale
    )
    new_peak = jnp.maximum(running_peak, jnp.max(scores, axis=-1))
    weights = jnp.exp(scores - new_peak[..., None])
    new_total = jnp.sum(weights, axis=-1)
    added = jnp.einsum(
        "qhk,khd->qhd",
        weights.astype(jnp.bfloat16),
        piece_values,
        preferred_element_type=jnp.float32,
    )
    root_out = added / new_total[..., None]
    root_lse = new_peak + jnp.log(new_total)
    query_seq = query.reshape(seq_rows, suffix, heads_here, head_dim)
    key_seq = key.reshape(seq_rows, suffix, heads_here, head_dim)
    value_seq = value.reshape(seq_rows, suffix, heads_here, head_dim)
    slots = jnp.arange(suffix, dtype=jnp.int32)
    self_ok = (slots[None, None, :] <= slots[None, :, None]) & (
        slots[None, None, :] < suffix_len[:, None, None]
    )
    self_scores = (
        jnp.einsum("sqhd,skhd->sqhk", query_seq, key_seq, preferred_element_type=jnp.float32)
        * scale
    )
    self_scores = jnp.where(self_ok[:, :, None, :], self_scores, NEGATIVE)
    self_peak = jnp.max(self_scores, axis=-1)
    self_weights = jnp.exp(self_scores - self_peak[..., None])
    self_total = jnp.sum(self_weights, axis=-1)
    self_sum = jnp.einsum(
        "sqhk,skhd->sqhd",
        self_weights.astype(jnp.bfloat16),
        value_seq,
        preferred_element_type=jnp.float32,
    )
    self_out = (self_sum / self_total[..., None]).reshape(tok_rows, heads_here, head_dim)
    self_lse = (self_peak + jnp.log(self_total)).reshape(tok_rows, heads_here)
    mid_of = parents[leaf_of]
    leaf_owner = leaf_of // 2
    targets = jnp.arange(owners, dtype=jnp.int32)
    pick_mid = (mid_of[None, :] == targets[:, None]).astype(jnp.bfloat16)
    pick_leaf = (leaf_owner[None, :] == targets[:, None]).astype(jnp.bfloat16)
    flat_query = query.reshape(seq_rows, suffix * local_width)
    sent_mid = jnp.dot(pick_mid, flat_query, preferred_element_type=jnp.float32).astype(
        jnp.bfloat16
    )
    sent_leaf = jnp.dot(pick_leaf, flat_query, preferred_element_type=jnp.float32).astype(
        jnp.bfloat16
    )
    sent = jnp.stack([sent_mid, sent_leaf], axis=1).reshape(owners, 2, suffix, local_width)
    leaf_side = (leaf_of % 2).astype(jnp.float32)
    side_of_target = jnp.dot(
        pick_leaf.astype(jnp.float32), leaf_side, precision=lax.Precision.HIGHEST
    )
    side_rows = jnp.broadcast_to(side_of_target[:, None, None], (owners, 8, local_width))
    sent_all = jnp.concatenate(
        [sent.reshape(owners, 2 * suffix, local_width), side_rows.astype(jnp.bfloat16)], axis=1
    )
    got_all = lax.all_to_all(sent_all, DP, split_axis=0, concat_axis=0, tiled=True)
    sent_queries = got_all[:, : 2 * suffix].reshape(owners, 2, suffix, local_width)
    second = got_all[:, 2 * suffix, 0] > 0.5
    senders = sent_queries.shape[0]
    mid_limit = jnp.broadcast_to(mid_len[0], (senders,))
    mid_result, mid_logsum = level_partial(
        sent_queries[:, 0], mid_cache[0, 0], mid_cache[1, 0], mid_limit, heads_here, False
    )
    leaf_keys = jnp.where(second[:, None, None], leaf_cache[0, 1][None], leaf_cache[0, 0][None])
    leaf_values = jnp.where(second[:, None, None], leaf_cache[1, 1][None], leaf_cache[1, 0][None])
    leaf_limit = jnp.where(second, leaf_len[1], leaf_len[0])
    leaf_result, leaf_logsum = level_partial(
        sent_queries[:, 1], leaf_keys, leaf_values, leaf_limit, heads_here, True
    )
    owner_out = jnp.stack([mid_result, leaf_result], axis=1)
    owner_lse = jnp.stack([mid_logsum, leaf_logsum], axis=1)
    owner_all = jnp.concatenate([owner_out, owner_lse], axis=-1)
    back_all = lax.all_to_all(owner_all, DP, split_axis=0, concat_axis=0, tiled=True)
    back_out = back_all[..., :local_width]
    back_lse = back_all[..., local_width:]
    mid_out = back_out[mid_of, 0].reshape(tok_rows, heads_here, head_dim)
    mid_lse = back_lse[mid_of, 0].reshape(tok_rows, heads_here)
    leaf_out = back_out[leaf_owner, 1].reshape(tok_rows, heads_here, head_dim)
    leaf_lse = back_lse[leaf_owner, 1].reshape(tok_rows, heads_here)
    stacked_lse = jnp.stack([root_lse, mid_lse, leaf_lse, self_lse])
    stacked_out = jnp.stack([root_out, mid_out, leaf_out, self_out])
    overall = jnp.max(stacked_lse, axis=0)
    shares = jnp.exp(stacked_lse - overall)
    combined = jnp.sum(shares[..., None] * stacked_out, axis=0) / jnp.sum(shares, axis=0)[..., None]
    attended = combined.reshape(tok_rows, local_width).astype(jnp.bfloat16)
    unit_weights = lax.all_gather(
        jnp.stack([w_gate[0], w_up[0], w_down[0].T]), "z", axis=0, tiled=False
    )
    projected = jnp.dot(attended, w_out, preferred_element_type=jnp.float32)
    rows_here = tok_rows // lax.axis_size("mp")
    first = lax.axis_index("mp") * rows_here
    attn_rows = mp_sum_scatter(projected.astype(jnp.bfloat16), 0)
    resid = lax.dynamic_slice_in_dim(hidden_in, first, rows_here, 0).astype(jnp.float32) + attn_rows
    ffn_rows = rms_scale(resid, ffn_gain).astype(jnp.bfloat16)
    ffn_in = mp_gather(ffn_rows, 1)
    unit_weights, ffn_in = lax.optimization_barrier((unit_weights, ffn_in))
    logits = jnp.dot(ffn_in.astype(jnp.float32), w_router, precision=lax.Precision.HIGHEST)
    chosen = jnp.take_along_axis(logits, routes, axis=1)
    squashed = jax.nn.sigmoid(chosen)
    gates = squashed / jnp.sum(squashed, axis=1, keepdims=True)
    expert = lax.axis_index("mp")
    hit_each = routes == expert
    hit = jnp.any(hit_each, axis=1)
    gate_here = jnp.sum(jnp.where(hit_each, gates, 0.0), axis=1)
    order = jnp.cumsum(hit.astype(jnp.int32)) - 1
    capacity = 3 * TOP * tok_rows // (2 * lax.axis_size("mp"))
    slot_ids = jnp.arange(capacity, dtype=jnp.int32)
    pick_slot = (order[None, :] == slot_ids[:, None]) & hit[None, :]
    dispatch = jnp.dot(
        pick_slot.astype(jnp.bfloat16), ffn_in, preferred_element_type=jnp.float32
    ).astype(jnp.bfloat16)
    slot_gate = jnp.dot(pick_slot.astype(jnp.float32), gate_here, precision=lax.Precision.HIGHEST)
    piece = lax.all_gather(dispatch, "y", axis=0, tiled=True)
    gate_part = jnp.einsum(
        "td,zdu->tzu", piece, unit_weights[:, 0], preferred_element_type=jnp.float32
    )
    up_part = jnp.einsum(
        "td,zdu->tzu", piece, unit_weights[:, 1], preferred_element_type=jnp.float32
    )
    partial_out = jnp.einsum(
        "tzu,zdu->td",
        (jax.nn.silu(gate_part) * up_part).astype(jnp.bfloat16),
        unit_weights[:, 2],
        preferred_element_type=jnp.float32,
    )
    expert_out = lax.psum_scatter(
        partial_out.astype(jnp.bfloat16), "y", scatter_dimension=0, tiled=True
    )
    weighted = expert_out.astype(jnp.float32) * slot_gate[:, None]
    spread = jnp.dot(pick_slot.astype(jnp.float32).T, weighted, precision=lax.Precision.HIGHEST)
    mixed = mp_sum_scatter(spread.astype(jnp.bfloat16), 2)
    row_ids = first + jnp.arange(rows_here, dtype=jnp.int32)
    valid = row_ids % suffix < suffix_len[row_ids // suffix]
    return jnp.where(valid[:, None], resid + mixed, 0.0).astype(jnp.bfloat16)


def solution(mesh):
    return jax.shard_map(
        on_device,
        mesh=Mesh(mesh.devices.reshape(4, 4, -1), ("y", "z", "mp")),
        in_specs=(
            P(DP, None),
            P(),
            P(None, "mp"),
            P(None, "mp"),
            P(None, "mp"),
            P("mp", None),
            P(None, DP, "mp"),
            P(None, DP, None, "mp"),
            P(None, DP, None, "mp"),
            P(DP),
            P(DP),
            P(DP),
            P(),
            P(DP),
            P(),
            P(),
            P(DP, None),
            P("mp", None, DP),
            P("mp", None, DP),
            P("mp", DP, None),
        ),
        out_specs=P(("y", "z", "mp"), None),
        check_vma=False,
    )
```

```python
import math

import jax
import jax.numpy as jnp
from jax import lax
import functools

from jax.experimental import pallas as pl
from jax.experimental.pallas import tpu as pltpu
from jax.sharding import Mesh, PartitionSpec as P

DP = ("y", "z")

MESH = pl.DeviceIdType.MESH


def _greet(n, me, dp):
    barrier = pltpu.get_barrier_semaphore()
    for k in range(1, n):
        pl.semaphore_signal(barrier, 1, device_id=(*dp, (me + k) % n), device_id_type=MESH)
    pl.semaphore_wait(barrier, n - 1)


def _mp_sum_kernel(n, x_ref, o_ref, recv, send_sem, recv_sem):
    me = lax.axis_index("mp")
    dp = (lax.axis_index("y"), lax.axis_index("z"))
    rows = o_ref.shape[0]
    _greet(n, me, dp)
    copies = []
    for k in range(1, n):
        peer = (me + k) % n
        copy = pltpu.make_async_remote_copy(
            src_ref=x_ref.at[pl.ds(pl.multiple_of(peer * rows, rows), rows)],
            dst_ref=recv.at[k],
            send_sem=send_sem.at[k],
            recv_sem=recv_sem.at[k],
            device_id=(*dp, peer),
            device_id_type=MESH,
        )
        copy.start()
        copies.append(copy)
    for copy in copies:
        copy.wait()
    total = x_ref[pl.ds(pl.multiple_of(me * rows, rows), rows), :].astype(jnp.float32)
    for k in range(1, n):
        total = total + recv[k].astype(jnp.float32)
    o_ref[...] = total


def mp_sum_scatter(x, collective_id):
    n = lax.axis_size("mp")
    rows = x.shape[0] // n
    cols = x.shape[1]
    return pl.pallas_call(
        functools.partial(_mp_sum_kernel, n),
        out_shape=jax.ShapeDtypeStruct((rows, cols), jnp.float32),
        in_specs=[pl.BlockSpec(memory_space=pltpu.VMEM)],
        out_specs=pl.BlockSpec(memory_space=pltpu.VMEM),
        scratch_shapes=[
            pltpu.VMEM((n, rows, cols), x.dtype),
            pltpu.SemaphoreType.DMA((n,)),
            pltpu.SemaphoreType.DMA((n,)),
        ],
        compiler_params=pltpu.CompilerParams(collective_id=collective_id, has_side_effects=True),
    )(x)


def _mp_gather_kernel(n, x_ref, o_ref, recv, send_sem, recv_sem):
    me = lax.axis_index("mp")
    dp = (lax.axis_index("y"), lax.axis_index("z"))
    rows = x_ref.shape[0]
    _greet(n, me, dp)
    copies = []
    for k in range(1, n):
        peer = (me + k) % n
        copy = pltpu.make_async_remote_copy(
            src_ref=x_ref,
            dst_ref=recv.at[k],
            send_sem=send_sem.at[k],
            recv_sem=recv_sem.at[k],
            device_id=(*dp, peer),
            device_id_type=MESH,
        )
        copy.start()
        copies.append(copy)
    for copy in copies:
        copy.wait()
    o_ref[pl.ds(pl.multiple_of(me * rows, rows), rows), :] = x_ref[...]
    for k in range(1, n):
        source = (me + n - k) % n
        o_ref[pl.ds(pl.multiple_of(source * rows, rows), rows), :] = recv[k]


def mp_gather(x, collective_id):
    n = lax.axis_size("mp")
    rows, cols = x.shape
    return pl.pallas_call(
        functools.partial(_mp_gather_kernel, n),
        out_shape=jax.ShapeDtypeStruct((n * rows, cols), x.dtype),
        in_specs=[pl.BlockSpec(memory_space=pltpu.VMEM)],
        out_specs=pl.BlockSpec(memory_space=pltpu.VMEM),
        scratch_shapes=[
            pltpu.VMEM((n, rows, cols), x.dtype),
            pltpu.SemaphoreType.DMA((n,)),
            pltpu.SemaphoreType.DMA((n,)),
        ],
        compiler_params=pltpu.CompilerParams(collective_id=collective_id, has_side_effects=True),
    )(x)


HD = 64
TOP = 2


EPS = 1e-05
NEGATIVE = -1e30


def rms_scale(rows, gain):
    rows_wide = rows.astype(jnp.float32)
    mean_square = jnp.mean(rows_wide * rows_wide, axis=-1, keepdims=True)
    return rows_wide * lax.rsqrt(mean_square + EPS) * gain


def level_partial(queries, node_keys, node_values, limits, heads_here, batched):
    senders, row_count, width = queries.shape
    head_dim = width // heads_here
    scale = 1.0 / math.sqrt(head_dim)
    query_heads = queries.reshape(senders, row_count, heads_here, head_dim)
    if batched:
        key_heads = node_keys.reshape(senders, -1, heads_here, head_dim)
        value_heads = node_values.reshape(senders, -1, heads_here, head_dim)
        scores = jnp.einsum(
            "sqhd,skhd->sqhk", query_heads, key_heads, preferred_element_type=jnp.float32
        )
    else:
        key_heads = node_keys.reshape(-1, heads_here, head_dim)
        value_heads = node_values.reshape(-1, heads_here, head_dim)
        scores = jnp.einsum(
            "sqhd,khd->sqhk", query_heads, key_heads, preferred_element_type=jnp.float32
        )
    scores = scores * scale
    slots = jnp.arange(scores.shape[-1], dtype=jnp.int32)
    allowed = slots[None, :] < limits[:, None]
    scores = jnp.where(allowed[:, None, None, :], scores, NEGATIVE)
    peak = jnp.max(scores, axis=-1)
    weights = jnp.exp(scores - peak[..., None])
    total = jnp.sum(weights, axis=-1)
    probs = weights.astype(jnp.bfloat16)
    if batched:
        summed = jnp.einsum(
            "sqhk,skhd->sqhd", probs, value_heads, preferred_element_type=jnp.float32
        )
    else:
        summed = jnp.einsum(
            "sqhk,khd->sqhd", probs, value_heads, preferred_element_type=jnp.float32
        )
    result = (summed / total[..., None]).reshape(senders, row_count, width)
    return (result, peak + jnp.log(total))


def on_device(
    hidden_in,
    attn_gain,
    w_query,
    w_key,
    w_value,
    w_out,
    root_cache,
    mid_cache,
    leaf_cache,
    mid_len,
    leaf_len,
    leaf_of,
    parents,
    suffix_len,
    ffn_gain,
    w_router,
    routes,
    w_gate,
    w_up,
    w_down,
):
    tok_rows, width = hidden_in.shape
    seq_rows = suffix_len.shape[0]
    suffix = tok_rows // seq_rows
    head_dim = HD
    local_width = w_query.shape[1]
    heads_here = local_width // head_dim
    scale = 1.0 / math.sqrt(head_dim)
    owners = lax.axis_size(DP)
    normed = rms_scale(hidden_in, attn_gain).astype(jnp.bfloat16)
    query = jnp.dot(normed, w_query, preferred_element_type=jnp.float32).astype(jnp.bfloat16)
    key = jnp.dot(normed, w_key, preferred_element_type=jnp.float32).astype(jnp.bfloat16)
    value = jnp.dot(normed, w_value, preferred_element_type=jnp.float32).astype(jnp.bfloat16)
    query_heads = query.reshape(tok_rows, heads_here, head_dim)
    root_copies = jnp.broadcast_to(root_cache[None], (owners,) + root_cache.shape)
    root_got = lax.all_to_all(root_copies, DP, split_axis=0, concat_axis=0, tiled=True)
    root_got, query = lax.optimization_barrier((root_got, query))
    piece = root_got.transpose(1, 0, 2, 3).reshape(
        root_cache.shape[0], owners * root_cache.shape[1], root_cache.shape[2]
    )
    running_peak = jnp.full((tok_rows, heads_here), NEGATIVE, jnp.float32)
    piece_keys = piece[0].reshape(-1, heads_here, head_dim)
    piece_values = piece[1].reshape(-1, heads_here, head_dim)
    scores = (
        jnp.einsum("qhd,khd->qhk", query_heads, piece_keys, preferred_element_type=jnp.float32)
        * scale
    )
    new_peak = jnp.maximum(running_peak, jnp.max(scores, axis=-1))
    weights = jnp.exp(scores - new_peak[..., None])
    new_total = jnp.sum(weights, axis=-1)
    added = jnp.einsum(
        "qhk,khd->qhd",
        weights.astype(jnp.bfloat16),
        piece_values,
        preferred_element_type=jnp.float32,
    )
    root_out = added / new_total[..., None]
    root_lse = new_peak + jnp.log(new_total)
    query_seq = query.reshape(seq_rows, suffix, heads_here, head_dim)
    key_seq = key.reshape(seq_rows, suffix, heads_here, head_dim)
    value_seq = value.reshape(seq_rows, suffix, heads_here, head_dim)
    slots = jnp.arange(suffix, dtype=jnp.int32)
    self_ok = (slots[None, None, :] <= slots[None, :, None]) & (
        slots[None, None, :] < suffix_len[:, None, None]
    )
    self_scores = (
        jnp.einsum("sqhd,skhd->sqhk", query_seq, key_seq, preferred_element_type=jnp.float32)
        * scale
    )
    self_scores = jnp.where(self_ok[:, :, None, :], self_scores, NEGATIVE)
    self_peak = jnp.max(self_scores, axis=-1)
    self_weights = jnp.exp(self_scores - self_peak[..., None])
    self_total = jnp.sum(self_weights, axis=-1)
    self_sum = jnp.einsum(
        "sqhk,skhd->sqhd",
        self_weights.astype(jnp.bfloat16),
        value_seq,
        preferred_element_type=jnp.float32,
    )
    self_out = (self_sum / self_total[..., None]).reshape(tok_rows, heads_here, head_dim)
    self_lse = (self_peak + jnp.log(self_total)).reshape(tok_rows, heads_here)
    mid_of = parents[leaf_of]
    leaf_owner = leaf_of // 2
    targets = jnp.arange(owners, dtype=jnp.int32)
    pick_mid = (mid_of[None, :] == targets[:, None]).astype(jnp.bfloat16)
    pick_leaf = (leaf_owner[None, :] == targets[:, None]).astype(jnp.bfloat16)
    flat_query = query.reshape(seq_rows, suffix * local_width)
    sent_mid = jnp.dot(pick_mid, flat_query, preferred_element_type=jnp.float32).astype(
        jnp.bfloat16
    )
    sent_leaf = jnp.dot(pick_leaf, flat_query, preferred_element_type=jnp.float32).astype(
        jnp.bfloat16
    )
    sent = jnp.stack([sent_mid, sent_leaf], axis=1).reshape(owners, 2, suffix, local_width)
    leaf_side = (leaf_of % 2).astype(jnp.float32)
    side_of_target = jnp.dot(
        pick_leaf.astype(jnp.float32), leaf_side, precision=lax.Precision.HIGHEST
    )
    side_rows = jnp.broadcast_to(side_of_target[:, None, None], (owners, 8, local_width))
    sent_all = jnp.concatenate(
        [sent.reshape(owners, 2 * suffix, local_width), side_rows.astype(jnp.bfloat16)], axis=1
    )
    got_all = lax.all_to_all(sent_all, DP, split_axis=0, concat_axis=0, tiled=True)
    sent_queries = got_all[:, : 2 * suffix].reshape(owners, 2, suffix, local_width)
    second = got_all[:, 2 * suffix, 0] > 0.5
    senders = sent_queries.shape[0]
    mid_limit = jnp.broadcast_to(mid_len[0], (senders,))
    mid_result, mid_logsum = level_partial(
        sent_queries[:, 0], mid_cache[0, 0], mid_cache[1, 0], mid_limit, heads_here, False
    )
    leaf_keys = jnp.where(second[:, None, None], leaf_cache[0, 1][None], leaf_cache[0, 0][None])
    leaf_values = jnp.where(second[:, None, None], leaf_cache[1, 1][None], leaf_cache[1, 0][None])
    leaf_limit = jnp.where(second, leaf_len[1], leaf_len[0])
    leaf_result, leaf_logsum = level_partial(
        sent_queries[:, 1], leaf_keys, leaf_values, leaf_limit, heads_here, True
    )
    owner_out = jnp.stack([mid_result, leaf_result], axis=1)
    owner_lse = jnp.stack([mid_logsum, leaf_logsum], axis=1)
    owner_all = jnp.concatenate([owner_out, owner_lse], axis=-1)
    back_all = lax.all_to_all(owner_all, DP, split_axis=0, concat_axis=0, tiled=True)
    back_out = back_all[..., :local_width]
    back_lse = back_all[..., local_width:]
    mid_out = back_out[mid_of, 0].reshape(tok_rows, heads_here, head_dim)
    mid_lse = back_lse[mid_of, 0].reshape(tok_rows, heads_here)
    leaf_out = back_out[leaf_owner, 1].reshape(tok_rows, heads_here, head_dim)
    leaf_lse = back_lse[leaf_owner, 1].reshape(tok_rows, heads_here)
    stacked_lse = jnp.stack([root_lse, mid_lse, leaf_lse, self_lse])
    stacked_out = jnp.stack([root_out, mid_out, leaf_out, self_out])
    overall = jnp.max(stacked_lse, axis=0)
    shares = jnp.exp(stacked_lse - overall)
    combined = jnp.sum(shares[..., None] * stacked_out, axis=0) / jnp.sum(shares, axis=0)[..., None]
    attended = combined.reshape(tok_rows, local_width).astype(jnp.bfloat16)
    unit_weights = lax.all_gather(
        jnp.stack([w_gate[0], w_up[0], w_down[0].T]), "z", axis=0, tiled=False
    )
    projected = jnp.dot(attended, w_out, preferred_element_type=jnp.float32)
    rows_here = tok_rows // lax.axis_size("mp")
    first = lax.axis_index("mp") * rows_here
    attn_rows = mp_sum_scatter(projected.astype(jnp.bfloat16), 0)
    resid = lax.dynamic_slice_in_dim(hidden_in, first, rows_here, 0).astype(jnp.float32) + attn_rows
    ffn_rows = rms_scale(resid, ffn_gain).astype(jnp.bfloat16)
    ffn_in = mp_gather(ffn_rows, 1)
    unit_weights, ffn_in = lax.optimization_barrier((unit_weights, ffn_in))
    logits = jnp.dot(ffn_in.astype(jnp.float32), w_router, precision=lax.Precision.HIGHEST)
    chosen = jnp.take_along_axis(logits, routes, axis=1)
    squashed = jax.nn.sigmoid(chosen)
    gates = squashed / jnp.sum(squashed, axis=1, keepdims=True)
    expert = lax.axis_index("mp")
    hit_each = routes == expert
    hit = jnp.any(hit_each, axis=1)
    gate_here = jnp.sum(jnp.where(hit_each, gates, 0.0), axis=1)
    order = jnp.cumsum(hit.astype(jnp.int32)) - 1
    capacity = 3 * TOP * tok_rows // (2 * lax.axis_size("mp"))
    slot_ids = jnp.arange(capacity, dtype=jnp.int32)
    pick_slot = (order[None, :] == slot_ids[:, None]) & hit[None, :]
    dispatch = jnp.dot(
        pick_slot.astype(jnp.bfloat16), ffn_in, preferred_element_type=jnp.float32
    ).astype(jnp.bfloat16)
    slot_gate = jnp.dot(pick_slot.astype(jnp.float32), gate_here, precision=lax.Precision.HIGHEST)
    piece = lax.all_gather(dispatch, "y", axis=0, tiled=True)
    gate_part = jnp.einsum(
        "td,zdu->tzu", piece, unit_weights[:, 0], preferred_element_type=jnp.float32
    )
    up_part = jnp.einsum(
        "td,zdu->tzu", piece, unit_weights[:, 1], preferred_element_type=jnp.float32
    )
    partial_out = jnp.einsum(
        "tzu,zdu->td",
        (jax.nn.silu(gate_part) * up_part).astype(jnp.bfloat16),
        unit_weights[:, 2],
        preferred_element_type=jnp.float32,
    )
    expert_out = lax.psum_scatter(
        partial_out.astype(jnp.bfloat16), "y", scatter_dimension=0, tiled=True
    )
    weighted = expert_out.astype(jnp.float32) * slot_gate[:, None]
    spread = jnp.dot(pick_slot.astype(jnp.float32).T, weighted, precision=lax.Precision.HIGHEST)
    mixed = mp_sum_scatter(spread.astype(jnp.bfloat16), 2)
    row_ids = first + jnp.arange(rows_here, dtype=jnp.int32)
    valid = row_ids % suffix < suffix_len[row_ids // suffix]
    return jnp.where(valid[:, None], resid + mixed, 0.0).astype(jnp.bfloat16)


def solution(mesh):
    return jax.shard_map(
        on_device,
        mesh=Mesh(mesh.devices.reshape(4, 4, -1), ("y", "z", "mp")),
        in_specs=(
            P(DP, None),
            P(),
            P(None, "mp"),
            P(None, "mp"),
            P(None, "mp"),
            P("mp", None),
            P(None, DP, "mp"),
            P(None, DP, None, "mp"),
            P(None, DP, None, "mp"),
            P(DP),
            P(DP),
            P(DP),
            P(),
            P(DP),
            P(),
            P(),
            P(DP, None),
            P("mp", None, DP),
            P("mp", None, DP),
            P("mp", DP, None),
        ),
        out_specs=P(("y", "z", "mp"), None),
        check_vma=False,
    )
```

```python
import math

import jax
import jax.numpy as jnp
from jax import lax
import functools

from jax.experimental import pallas as pl
from jax.experimental.pallas import tpu as pltpu
from jax.sharding import Mesh, PartitionSpec as P

DP = ("y", "z")

MESH = pl.DeviceIdType.MESH


def _greet(n, me, dp):
    barrier = pltpu.get_barrier_semaphore()
    for k in range(1, n):
        pl.semaphore_signal(barrier, 1, device_id=(*dp, (me + k) % n), device_id_type=MESH)
    pl.semaphore_wait(barrier, n - 1)


def _mp_sum_kernel(n, x_ref, o_ref, recv, send_sem, recv_sem):
    me = lax.axis_index("mp")
    dp = (lax.axis_index("y"), lax.axis_index("z"))
    rows = o_ref.shape[0]
    _greet(n, me, dp)
    copies = []
    for k in range(1, n):
        peer = (me + k) % n
        copy = pltpu.make_async_remote_copy(
            src_ref=x_ref.at[pl.ds(pl.multiple_of(peer * rows, rows), rows)],
            dst_ref=recv.at[k],
            send_sem=send_sem.at[k],
            recv_sem=recv_sem.at[k],
            device_id=(*dp, peer),
            device_id_type=MESH,
        )
        copy.start()
        copies.append(copy)
    for copy in copies:
        copy.wait()
    total = x_ref[pl.ds(pl.multiple_of(me * rows, rows), rows), :].astype(jnp.float32)
    for k in range(1, n):
        total = total + recv[k].astype(jnp.float32)
    o_ref[...] = total


def mp_sum_scatter(x, collective_id):
    n = lax.axis_size("mp")
    rows = x.shape[0] // n
    cols = x.shape[1]
    return pl.pallas_call(
        functools.partial(_mp_sum_kernel, n),
        out_shape=jax.ShapeDtypeStruct((rows, cols), jnp.float32),
        in_specs=[pl.BlockSpec(memory_space=pltpu.VMEM)],
        out_specs=pl.BlockSpec(memory_space=pltpu.VMEM),
        scratch_shapes=[
            pltpu.VMEM((n, rows, cols), x.dtype),
            pltpu.SemaphoreType.DMA((n,)),
            pltpu.SemaphoreType.DMA((n,)),
        ],
        compiler_params=pltpu.CompilerParams(collective_id=collective_id, has_side_effects=True),
    )(x)


def _mp_gather_kernel(n, x_ref, o_ref, recv, send_sem, recv_sem):
    me = lax.axis_index("mp")
    dp = (lax.axis_index("y"), lax.axis_index("z"))
    rows = x_ref.shape[0]
    _greet(n, me, dp)
    copies = []
    for k in range(1, n):
        peer = (me + k) % n
        copy = pltpu.make_async_remote_copy(
            src_ref=x_ref,
            dst_ref=recv.at[k],
            send_sem=send_sem.at[k],
            recv_sem=recv_sem.at[k],
            device_id=(*dp, peer),
            device_id_type=MESH,
        )
        copy.start()
        copies.append(copy)
    for copy in copies:
        copy.wait()
    o_ref[pl.ds(pl.multiple_of(me * rows, rows), rows), :] = x_ref[...]
    for k in range(1, n):
        source = (me + n - k) % n
        o_ref[pl.ds(pl.multiple_of(source * rows, rows), rows), :] = recv[k]


def mp_gather(x, collective_id):
    n = lax.axis_size("mp")
    rows, cols = x.shape
    return pl.pallas_call(
        functools.partial(_mp_gather_kernel, n),
        out_shape=jax.ShapeDtypeStruct((n * rows, cols), x.dtype),
        in_specs=[pl.BlockSpec(memory_space=pltpu.VMEM)],
        out_specs=pl.BlockSpec(memory_space=pltpu.VMEM),
        scratch_shapes=[
            pltpu.VMEM((n, rows, cols), x.dtype),
            pltpu.SemaphoreType.DMA((n,)),
            pltpu.SemaphoreType.DMA((n,)),
        ],
        compiler_params=pltpu.CompilerParams(collective_id=collective_id, has_side_effects=True),
    )(x)


HD = 64
TOP = 2


EPS = 1e-05
NEGATIVE = -1e30


def rms_scale(rows, gain):
    rows_wide = rows.astype(jnp.float32)
    mean_square = jnp.mean(rows_wide * rows_wide, axis=-1, keepdims=True)
    return rows_wide * lax.rsqrt(mean_square + EPS) * gain


def level_partial(queries, node_keys, node_values, limits, heads_here, batched):
    senders, row_count, width = queries.shape
    head_dim = width // heads_here
    scale = 1.0 / math.sqrt(head_dim)
    query_heads = queries.reshape(senders, row_count, heads_here, head_dim)
    if batched:
        key_heads = node_keys.reshape(senders, -1, heads_here, head_dim)
        value_heads = node_values.reshape(senders, -1, heads_here, head_dim)
        scores = jnp.einsum(
            "sqhd,skhd->sqhk", query_heads, key_heads, preferred_element_type=jnp.float32
        )
    else:
        key_heads = node_keys.reshape(-1, heads_here, head_dim)
        value_heads = node_values.reshape(-1, heads_here, head_dim)
        scores = jnp.einsum(
            "sqhd,khd->sqhk", query_heads, key_heads, preferred_element_type=jnp.float32
        )
    scores = scores * scale
    slots = jnp.arange(scores.shape[-1], dtype=jnp.int32)
    allowed = slots[None, :] < limits[:, None]
    scores = jnp.where(allowed[:, None, None, :], scores, NEGATIVE)
    peak = jnp.max(scores, axis=-1)
    weights = jnp.exp(scores - peak[..., None])
    total = jnp.sum(weights, axis=-1)
    probs = weights.astype(jnp.bfloat16)
    if batched:
        summed = jnp.einsum(
            "sqhk,skhd->sqhd", probs, value_heads, preferred_element_type=jnp.float32
        )
    else:
        summed = jnp.einsum(
            "sqhk,khd->sqhd", probs, value_heads, preferred_element_type=jnp.float32
        )
    result = (summed / total[..., None]).reshape(senders, row_count, width)
    return (result, peak + jnp.log(total))


def on_device(
    hidden_in,
    attn_gain,
    w_query,
    w_key,
    w_value,
    w_out,
    root_cache,
    mid_cache,
    leaf_cache,
    mid_len,
    leaf_len,
    leaf_of,
    parents,
    suffix_len,
    ffn_gain,
    w_router,
    routes,
    w_gate,
    w_up,
    w_down,
):
    tok_rows, width = hidden_in.shape
    seq_rows = suffix_len.shape[0]
    suffix = tok_rows // seq_rows
    head_dim = HD
    local_width = w_query.shape[1]
    heads_here = local_width // head_dim
    scale = 1.0 / math.sqrt(head_dim)
    owners = lax.axis_size(DP)
    normed = rms_scale(hidden_in, attn_gain).astype(jnp.bfloat16)
    query = jnp.dot(normed, w_query, preferred_element_type=jnp.float32).astype(jnp.bfloat16)
    key = jnp.dot(normed, w_key, preferred_element_type=jnp.float32).astype(jnp.bfloat16)
    value = jnp.dot(normed, w_value, preferred_element_type=jnp.float32).astype(jnp.bfloat16)
    query_heads = query.reshape(tok_rows, heads_here, head_dim)
    z_size, y_size = lax.axis_size("z"), lax.axis_size("y")
    root_z = lax.all_to_all(
        jnp.broadcast_to(root_cache[None], (z_size,) + root_cache.shape),
        "z", split_axis=0, concat_axis=0, tiled=True,
    )
    root_got = lax.all_to_all(
        jnp.broadcast_to(root_z[None], (y_size,) + root_z.shape),
        "y", split_axis=0, concat_axis=0, tiled=True,
    )
    piece = root_got.transpose(2, 0, 1, 3, 4).reshape(
        root_cache.shape[0], owners * root_cache.shape[1], root_cache.shape[2]
    )
    running_peak = jnp.full((tok_rows, heads_here), NEGATIVE, jnp.float32)
    piece_keys = piece[0].reshape(-1, heads_here, head_dim)
    piece_values = piece[1].reshape(-1, heads_here, head_dim)
    scores = (
        jnp.einsum("qhd,khd->qhk", query_heads, piece_keys, preferred_element_type=jnp.float32)
        * scale
    )
    new_peak = jnp.maximum(running_peak, jnp.max(scores, axis=-1))
    weights = jnp.exp(scores - new_peak[..., None])
    new_total = jnp.sum(weights, axis=-1)
    added = jnp.einsum(
        "qhk,khd->qhd",
        weights.astype(jnp.bfloat16),
        piece_values,
        preferred_element_type=jnp.float32,
    )
    root_out = added / new_total[..., None]
    root_lse = new_peak + jnp.log(new_total)
    query_seq = query.reshape(seq_rows, suffix, heads_here, head_dim)
    key_seq = key.reshape(seq_rows, suffix, heads_here, head_dim)
    value_seq = value.reshape(seq_rows, suffix, heads_here, head_dim)
    slots = jnp.arange(suffix, dtype=jnp.int32)
    self_ok = (slots[None, None, :] <= slots[None, :, None]) & (
        slots[None, None, :] < suffix_len[:, None, None]
    )
    self_scores = (
        jnp.einsum("sqhd,skhd->sqhk", query_seq, key_seq, preferred_element_type=jnp.float32)
        * scale
    )
    self_scores = jnp.where(self_ok[:, :, None, :], self_scores, NEGATIVE)
    self_peak = jnp.max(self_scores, axis=-1)
    self_weights = jnp.exp(self_scores - self_peak[..., None])
    self_total = jnp.sum(self_weights, axis=-1)
    self_sum = jnp.einsum(
        "sqhk,skhd->sqhd",
        self_weights.astype(jnp.bfloat16),
        value_seq,
        preferred_element_type=jnp.float32,
    )
    self_out = (self_sum / self_total[..., None]).reshape(tok_rows, heads_here, head_dim)
    self_lse = (self_peak + jnp.log(self_total)).reshape(tok_rows, heads_here)
    mid_of = parents[leaf_of]
    leaf_owner = leaf_of // 2
    targets = jnp.arange(owners, dtype=jnp.int32)
    pick_mid = (mid_of[None, :] == targets[:, None]).astype(jnp.bfloat16)
    pick_leaf = (leaf_owner[None, :] == targets[:, None]).astype(jnp.bfloat16)
    flat_query = query.reshape(seq_rows, suffix * local_width)
    sent_mid = jnp.dot(pick_mid, flat_query, preferred_element_type=jnp.float32).astype(
        jnp.bfloat16
    )
    sent_leaf = jnp.dot(pick_leaf, flat_query, preferred_element_type=jnp.float32).astype(
        jnp.bfloat16
    )
    sent = jnp.stack([sent_mid, sent_leaf], axis=1).reshape(owners, 2, suffix, local_width)
    leaf_side = (leaf_of % 2).astype(jnp.float32)
    side_of_target = jnp.dot(
        pick_leaf.astype(jnp.float32), leaf_side, precision=lax.Precision.HIGHEST
    )
    side_rows = jnp.broadcast_to(side_of_target[:, None, None], (owners, 8, local_width))
    sent_all = jnp.concatenate(
        [sent.reshape(owners, 2 * suffix, local_width), side_rows.astype(jnp.bfloat16)], axis=1
    )
    got_all = lax.all_to_all(sent_all, DP, split_axis=0, concat_axis=0, tiled=True)
    sent_queries = got_all[:, : 2 * suffix].reshape(owners, 2, suffix, local_width)
    second = got_all[:, 2 * suffix, 0] > 0.5
    senders = sent_queries.shape[0]
    mid_limit = jnp.broadcast_to(mid_len[0], (senders,))
    mid_result, mid_logsum = level_partial(
        sent_queries[:, 0], mid_cache[0, 0], mid_cache[1, 0], mid_limit, heads_here, False
    )
    leaf_keys = jnp.where(second[:, None, None], leaf_cache[0, 1][None], leaf_cache[0, 0][None])
    leaf_values = jnp.where(second[:, None, None], leaf_cache[1, 1][None], leaf_cache[1, 0][None])
    leaf_limit = jnp.where(second, leaf_len[1], leaf_len[0])
    leaf_result, leaf_logsum = level_partial(
        sent_queries[:, 1], leaf_keys, leaf_values, leaf_limit, heads_here, True
    )
    owner_out = jnp.stack([mid_result, leaf_result], axis=1)
    owner_lse = jnp.stack([mid_logsum, leaf_logsum], axis=1)
    owner_all = jnp.concatenate([owner_out, owner_lse], axis=-1)
    back_all = lax.all_to_all(owner_all, DP, split_axis=0, concat_axis=0, tiled=True)
    back_out = back_all[..., :local_width]
    back_lse = back_all[..., local_width:]
    mid_out = back_out[mid_of, 0].reshape(tok_rows, heads_here, head_dim)
    mid_lse = back_lse[mid_of, 0].reshape(tok_rows, heads_here)
    leaf_out = back_out[leaf_owner, 1].reshape(tok_rows, heads_here, head_dim)
    leaf_lse = back_lse[leaf_owner, 1].reshape(tok_rows, heads_here)
    stacked_lse = jnp.stack([root_lse, mid_lse, leaf_lse, self_lse])
    stacked_out = jnp.stack([root_out, mid_out, leaf_out, self_out])
    overall = jnp.max(stacked_lse, axis=0)
    shares = jnp.exp(stacked_lse - overall)
    combined = jnp.sum(shares[..., None] * stacked_out, axis=0) / jnp.sum(shares, axis=0)[..., None]
    attended = combined.reshape(tok_rows, local_width).astype(jnp.bfloat16)
    unit_weights = lax.all_gather(
        jnp.stack([w_gate[0], w_up[0], w_down[0].T]), "z", axis=0, tiled=False
    )
    projected = jnp.dot(attended, w_out, preferred_element_type=jnp.float32)
    rows_here = tok_rows // lax.axis_size("mp")
    first = lax.axis_index("mp") * rows_here
    attn_rows = mp_sum_scatter(projected.astype(jnp.bfloat16), 0)
    resid = lax.dynamic_slice_in_dim(hidden_in, first, rows_here, 0).astype(jnp.float32) + attn_rows
    ffn_rows = rms_scale(resid, ffn_gain).astype(jnp.bfloat16)
    ffn_in = mp_gather(ffn_rows, 1)
    unit_weights, ffn_in = lax.optimization_barrier((unit_weights, ffn_in))
    logits = jnp.dot(ffn_in.astype(jnp.float32), w_router, precision=lax.Precision.HIGHEST)
    chosen = jnp.take_along_axis(logits, routes, axis=1)
    squashed = jax.nn.sigmoid(chosen)
    gates = squashed / jnp.sum(squashed, axis=1, keepdims=True)
    expert = lax.axis_index("mp")
    hit_each = routes == expert
    hit = jnp.any(hit_each, axis=1)
    gate_here = jnp.sum(jnp.where(hit_each, gates, 0.0), axis=1)
    order = jnp.cumsum(hit.astype(jnp.int32)) - 1
    capacity = 3 * TOP * tok_rows // (2 * lax.axis_size("mp"))
    slot_ids = jnp.arange(capacity, dtype=jnp.int32)
    pick_slot = (order[None, :] == slot_ids[:, None]) & hit[None, :]
    dispatch = jnp.dot(
        pick_slot.astype(jnp.bfloat16), ffn_in, preferred_element_type=jnp.float32
    ).astype(jnp.bfloat16)
    slot_gate = jnp.dot(pick_slot.astype(jnp.float32), gate_here, precision=lax.Precision.HIGHEST)
    piece = lax.all_gather(dispatch, "y", axis=0, tiled=True)
    gate_part = jnp.einsum(
        "td,zdu->tzu", piece, unit_weights[:, 0], preferred_element_type=jnp.float32
    )
    up_part = jnp.einsum(
        "td,zdu->tzu", piece, unit_weights[:, 1], preferred_element_type=jnp.float32
    )
    partial_out = jnp.einsum(
        "tzu,zdu->td",
        (jax.nn.silu(gate_part) * up_part).astype(jnp.bfloat16),
        unit_weights[:, 2],
        preferred_element_type=jnp.float32,
    )
    expert_out = lax.psum_scatter(
        partial_out.astype(jnp.bfloat16), "y", scatter_dimension=0, tiled=True
    )
    weighted = expert_out.astype(jnp.float32) * slot_gate[:, None]
    spread = jnp.dot(pick_slot.astype(jnp.float32).T, weighted, precision=lax.Precision.HIGHEST)
    mixed = mp_sum_scatter(spread.astype(jnp.bfloat16), 2)
    row_ids = first + jnp.arange(rows_here, dtype=jnp.int32)
    valid = row_ids % suffix < suffix_len[row_ids // suffix]
    return jnp.where(valid[:, None], resid + mixed, 0.0).astype(jnp.bfloat16)


def solution(mesh):
    return jax.shard_map(
        on_device,
        mesh=Mesh(mesh.devices.reshape(4, 4, -1), ("y", "z", "mp")),
        in_specs=(
            P(DP, None),
            P(),
            P(None, "mp"),
            P(None, "mp"),
            P(None, "mp"),
            P("mp", None),
            P(None, DP, "mp"),
            P(None, DP, None, "mp"),
            P(None, DP, None, "mp"),
            P(DP),
            P(DP),
            P(DP),
            P(),
            P(DP),
            P(),
            P(),
            P(DP, None),
            P("mp", None, DP),
            P("mp", None, DP),
            P("mp", DP, None),
        ),
        out_specs=P(("y", "z", "mp"), None),
        check_vma=False,
    )
```
